32 devices in a mesh: groups: 2 (over y), seq: 4 (over z), blk: 2 (over x), tp: 2 (over core).
Axes of the slice: x: 2, y: 2, z: 4, core: 2. Of those that a mesh axis runs over, the one named last changes fastest.
Arguments:
- queries: bfloat16 [2048, 8192], P(('groups', 'seq', 'blk'), 'tp'), parts along dimension 0, may hold values from -160 to 160
- rotated_keys: bfloat16 [2048, 1024], P(('groups', 'seq', 'blk'), 'tp'), parts along dimension 0, may hold values from -5 to 5
- head_value_rows: bfloat16 [2048, 1024], P(('groups', 'seq', 'blk'), 'tp'), parts along dimension 0, may hold values from -6 to 6
- doc_lengths: int32 [16], P('groups'), parts along dimension 0, may hold values from 1 to 256, 1024 in all
- owner_plan: int32 [8, 2], P('groups'), parts along dimension 0, may hold values from 0 to 3, as said below
Outputs:
- attended: bfloat16 [4096, 8192], P(('groups', 'seq', 'blk'), 'tp'), parts along dimension 0
The draws below stay inside these ranges and needn't reach their ends.
There are 2 independent parts, one for each index of `groups`. The reference program is written for one: setup_inputs(seed, part) draws one part's arguments, and reference() takes and returns one part's arrays. A program takes and returns all parts, laid end to end along the dimension named above; each array names one. Nothing has to cross between parts.
Inputs may be any that keep to these rules, and one draw needn't show every extreme that they name: `doc_lengths`: the lengths sum to 1024. `owner_plan`: group g consists of tokens g * 256 to g * 256 + 255, its block j of tokens j * 128 to j * 128 + 127 within the group. The entries of one row are distinct, so one group sends at most 1 block to one owner; in every draw some owner receives 1 block from every group.
All inputs are finite; a program needn't handle non-finite values.
Results may differ from the reference program's by a relative error of at most 0.0037.
Values may be sent and summed in bfloat16 or wider, within the bound.
A program may use at most 64 MiB of HBM per device.

```python
import math
import jax
import jax.numpy as jnp
import numpy as np
from jax import lax

QUERY_HEADS = 64
KEY_HEADS = 8
HEAD_WIDTH = 128
BLOCK = 128
GROUP_BLOCKS = 2
PAIR = 1
PACKED_LENGTH = 1024
SLOTS = 512
DOC_MAX = 256
NDOCS = 8
N_SEQ = 4


def draw_both(base_key):
    key_random, query_draw = jax.random.split(base_key, 2)
    key_entries = jnp.clip(jax.random.normal(key_random, (PACKED_LENGTH, KEY_HEADS, HEAD_WIDTH), jnp.float32), -5.0, 5.0)
    query_entries = jnp.clip(jax.random.normal(query_draw, (PACKED_LENGTH, QUERY_HEADS, HEAD_WIDTH), jnp.float32), -5.0, 5.0)
    return (query_entries.reshape(PACKED_LENGTH, QUERY_HEADS * HEAD_WIDTH), key_entries.reshape(PACKED_LENGTH, KEY_HEADS * HEAD_WIDTH))


def draw_queries(key, part):
    return draw_both(jax.random.fold_in(key, 11))[0].astype(jnp.bfloat16)


def draw_rotated_keys(key, part):
    return draw_both(jax.random.fold_in(key, 11))[1].astype(jnp.bfloat16)


def draw_owner_plan(key, part):
    full_draw, pick_draw, order_draw = jax.random.split(jax.random.fold_in(key, 5), 3)
    slot_total = N_SEQ * PAIR
    full_owner = jax.random.randint(full_draw, (), 0, N_SEQ)
    slot_ids = jnp.arange(slot_total, dtype=jnp.int32)
    noise_score = jax.random.randint(pick_draw, (N_SEQ, slot_total), 0, 1 << 16) * slot_total + slot_ids[None, :]
    ranking = jnp.where((slot_ids // PAIR == full_owner)[None, :], slot_ids[None, :] - slot_total, noise_score)
    picked = jnp.argsort(ranking, axis=1)[:, :GROUP_BLOCKS]
    order_score = jax.random.randint(order_draw, (N_SEQ, GROUP_BLOCKS), 0, 1 << 16) * GROUP_BLOCKS + jnp.arange(GROUP_BLOCKS, dtype=jnp.int32)[None, :]
    order_index = jnp.argsort(order_score, axis=1)
    return jnp.take_along_axis(picked, order_index, axis=1).astype(jnp.int32)


def steps_of(rng, shape, shards, low, largest):
    loudness, own = 1.0, jax.random.fold_in(rng, 6)
    for axis_at, parts in shards:
        steps = jnp.exp(jax.random.uniform(jax.random.fold_in(own, axis_at), (parts,), jnp.float32, low / len(shards), largest / len(shards)))
        loudness = loudness * jnp.repeat(steps, shape[axis_at] // parts).reshape([-1 if axis == axis_at else 1 for axis in range(len(shape))])
    return loudness


def length_profile(number_of, total, limit, lean):
    weights = [(1 << 20) // math.isqrt(standing ** lean) + 1 for standing in range(2, number_of + 1)]
    rest, holding = total - limit - (number_of - 1), [1] * (number_of - 1)
    while rest > 0:
        movable = [i for i in range(number_of - 1) if holding[i] < limit]
        pool, left = sum([weights[i] for i in movable]), rest
        for i in movable:
            extra = min(limit - holding[i], max(1, left * weights[i] // pool), rest)
            holding[i] = holding[i] + extra
            rest = rest - extra
    return np.array([limit] + holding)


def uneven_parts(stream_key, amount, total, limit, skew):
    if amount == 2:
        one = jax.random.randint(stream_key, (), max(1, total - limit), min(limit, total - 1) + 1)
        return jnp.stack([one, total - one])
    tallies = jnp.asarray(length_profile(amount, total, limit, skew), jnp.int32)
    twos = (amount - 1) // 2
    donor, receiver = tallies[1:1 + 2 * twos:2], tallies[2:2 + 2 * twos:2]
    slack = jnp.minimum(donor - 1, limit - receiver)
    passed = jax.random.randint(jax.random.fold_in(stream_key, 1), (twos,), 0, 1 << 20) % (slack + 1)
    tallies = tallies.at[1:1 + 2 * twos:2].set(donor - passed).at[2:2 + 2 * twos:2].set(receiver + passed)
    return tallies[jax.random.permutation(jax.random.fold_in(stream_key, 2), amount)]


def gaussian(rng, extent, scale, bound, pieces=(), held_as=jnp.bfloat16):
    drawn = scale * jax.random.normal(rng, extent, jnp.float32)
    if pieces:
        drawn = drawn * steps_of(rng, extent, pieces, -0.22, 0.18)
    return jnp.clip(drawn, -bound, bound).astype(held_as)


def setup_inputs(seed: int = 0, part: int = 0) -> dict:
    arg_keys = jax.random.split(jax.random.key(seed), 6)
    own_keys = jax.random.split(jax.random.fold_in(arg_keys[5], part), 6)
    return {
        "queries": draw_queries(jax.random.fold_in(jax.random.fold_in(arg_keys[5], part), 71), part),
        "rotated_keys": draw_rotated_keys(jax.random.fold_in(jax.random.fold_in(arg_keys[5], part), 71), part),
        "head_value_rows": gaussian(own_keys[2], (PACKED_LENGTH, KEY_HEADS * HEAD_WIDTH), 1.0, 6.0, ((0, 8), (1, 2))),
        "doc_lengths": uneven_parts(own_keys[3], NDOCS, PACKED_LENGTH, DOC_MAX, 1).astype(jnp.int32),
        "owner_plan": draw_owner_plan(jax.random.fold_in(jax.random.fold_in(arg_keys[5], part), 71), part),
    }


masked_score = -1e+30

def document_of(positions, doc_ends):
    return lax.optimization_barrier(jnp.sum((positions[:, None] >= doc_ends[None, :]).astype(jnp.int32), axis=1))

def reference(queries, rotated_keys, head_value_rows, doc_lengths, owner_plan):
    total_length = queries.shape[0]
    heads_per_group = QUERY_HEADS // KEY_HEADS
    doc_ends = jnp.cumsum(doc_lengths).astype(jnp.int32)
    row_block = math.gcd(total_length, 256)
    backward_reach = DOC_MAX
    window = backward_reach + row_block
    score_scale = 1.0 / math.sqrt(HEAD_WIDTH)
    query_head_rows = queries.reshape(total_length, KEY_HEADS, heads_per_group, HEAD_WIDTH)
    key_padded_rows = jnp.concatenate([jnp.zeros((backward_reach, KEY_HEADS * HEAD_WIDTH), rotated_keys.dtype), rotated_keys], axis=0).reshape(total_length + backward_reach, KEY_HEADS, HEAD_WIDTH)
    value_padded_rows = jnp.concatenate([jnp.zeros((backward_reach, KEY_HEADS * HEAD_WIDTH), head_value_rows.dtype), head_value_rows], axis=0).reshape(total_length + backward_reach, KEY_HEADS, HEAD_WIDTH)

    def one_block(block_index):
        first_row = (block_index * row_block).astype(jnp.int32)
        query_tile = lax.dynamic_slice_in_dim(query_head_rows, first_row, row_block, 0).astype(jnp.float32)
        key_tile = lax.dynamic_slice_in_dim(key_padded_rows, first_row, window, 0).astype(jnp.float32)
        value_tile = lax.dynamic_slice_in_dim(value_padded_rows, first_row, window, 0).astype(jnp.float32)
        query_pos = first_row + jnp.arange(row_block, dtype=jnp.int32)
        key_pos = first_row - backward_reach + jnp.arange(window, dtype=jnp.int32)
        same_doc = document_of(query_pos, doc_ends)[:, None] == document_of(key_pos, doc_ends)[None, :]
        allowed = same_doc & (key_pos[None, :] <= query_pos[:, None]) & (key_pos[None, :] >= 0)
        allowed = allowed[:, None, None, :]
        scores = jnp.einsum('qghd,kgd->qghk', query_tile, key_tile, precision=lax.Precision.HIGHEST) * score_scale
        scores = jnp.where(allowed, scores, masked_score)
        highest = lax.optimization_barrier(jnp.max(scores, axis=3, keepdims=True))
        exponent = jnp.where(allowed, jnp.exp(scores - highest), 0.0)
        totals = lax.optimization_barrier(jnp.sum(exponent, axis=3))
        weights = lax.optimization_barrier(exponent.astype(jnp.bfloat16)).astype(jnp.float32)
        mixed = jnp.einsum('qghk,kgd->qghd', weights, value_tile, precision=lax.Precision.HIGHEST)
        return (mixed / totals[..., None]).astype(jnp.bfloat16).reshape(row_block, QUERY_HEADS * HEAD_WIDTH)
    token_out = lax.map(one_block, jnp.arange(total_length // row_block, dtype=jnp.int32)).reshape(total_length, QUERY_HEADS * HEAD_WIDTH)
    blocks_out = token_out.reshape(N_SEQ, GROUP_BLOCKS, BLOCK, QUERY_HEADS * HEAD_WIDTH)
    owner_ids = jnp.arange(N_SEQ, dtype=jnp.int32)
    pair_ids = jnp.arange(PAIR, dtype=jnp.int32)
    wanted = owner_ids[:, None] * PAIR + pair_ids[None, :]
    matches = owner_plan[None, :, None, :] == wanted[:, None, :, None]
    slot_live = jnp.any(matches, axis=3)
    block_pick = lax.optimization_barrier(jnp.sum(jnp.where(matches, jnp.arange(GROUP_BLOCKS, dtype=jnp.int32), 0), axis=3)).astype(jnp.int32)
    group_ids = jnp.broadcast_to(owner_ids[None, :, None], block_pick.shape)
    picked = blocks_out[group_ids, block_pick]
    picked = jnp.where(slot_live[:, :, :, None, None], picked, jnp.zeros_like(picked))
    return picked.reshape(N_SEQ * SLOTS, QUERY_HEADS * HEAD_WIDTH)
```

```python
import functools
import math

import jax
import jax.numpy as jnp
from jax import lax
from jax.experimental import pallas as pl
from jax.experimental.pallas import tpu as pltpu
from jax.sharding import PartitionSpec as P

QUERY_HEADS = 64
KEY_HEADS = 8
HEAD_WIDTH = 128
BLOCK = 128
CHUNK_HEADS = 2
PIECES = 8

MESH = pl.DeviceIdType.MESH
masked_score = -1e30
JOIN_LAG = 1
SPREAD_LAG = 2
COLLECT_LAG = 3
VMEM_MAIN = 20 * 2**20
VMEM_REST = 4 * 2**20


def kernel(
    dims,
    lengths_ref,
    plan_ref,
    q_ref,
    k_ref,
    v_ref,
    out_ref,
    q_group,
    k_near,
    v_near,
    bias,
    block_out,
    message,
    landed,
    local_sem,
    q_send,
    q_recv,
    kv_send,
    kv_recv,
    near_send,
    near_recv,
    z_send,
    z_recv,
    x_send,
    x_recv,
):
    seq, blk, heads_dev, groups_kv, heads_per_group, chunk_heads, slots = dims
    g = lax.axis_index("seq")
    b = lax.axis_index("blk")
    chunks = heads_dev // chunk_heads
    width = chunk_heads * HEAD_WIDTH
    columns_dev = heads_dev * HEAD_WIDTH
    window = (blk + 1) * BLOCK
    group_len = blk * BLOCK
    scale = 1.0 / math.sqrt(HEAD_WIDTH)

    def kv_columns(owner, h):
        first = owner * heads_dev // heads_per_group + h
        return pl.ds(pl.multiple_of(first * HEAD_WIDTH, HEAD_WIDTH), HEAD_WIDTH)

    def q_columns(owner, c):
        return pl.ds(pl.multiple_of(owner * columns_dev + c * width, HEAD_WIDTH), width)

    barrier = pltpu.get_barrier_semaphore()
    for e in range(1, blk):
        pl.semaphore_signal(
            barrier, inc=1, device_id={"blk": lax.rem(b + e, blk)}, device_id_type=MESH
        )
    for d in range(1, seq):
        pl.semaphore_signal(
            barrier, inc=1, device_id={"seq": lax.rem(g + d, seq)}, device_id_type=MESH
        )

    pairs = ((k_ref, k_near), (v_ref, v_near))
    own_kv = [
        pltpu.make_async_copy(
            src.at[:, kv_columns(b, h)], dst.at[h, blk + b], local_sem.at[2 * h + i]
        )
        for h in range(groups_kv)
        for i, (src, dst) in enumerate(pairs)
    ]
    own_q = [
        pltpu.make_async_copy(
            q_ref.at[:, q_columns(b, c)], q_group.at[c, b], local_sem.at[2 * groups_kv + c]
        )
        for c in range(chunks)
    ]
    for copy in own_kv + own_q:
        copy.start()

    def kv_copy(h, i, e):
        src, dst = pairs[i]
        peer = lax.rem(b + e, blk)
        return pltpu.make_async_remote_copy(
            src_ref=src.at[:, kv_columns(peer, h)],
            dst_ref=dst.at[h, blk + b],
            send_sem=kv_send.at[h, i, e - 1],
            recv_sem=kv_recv.at[h, i, e - 1],
            device_id={"blk": peer},
            device_id_type=MESH,
        )

    def near_copy(h, i, e):
        src, dst = pairs[i]
        origin = lax.rem(b - e + blk, blk)
        if e == 0:
            source = src.at[:, kv_columns(b, h)]
        else:
            source = dst.at[h, blk + origin]
        return pltpu.make_async_remote_copy(
            src_ref=source,
            dst_ref=dst.at[h, origin],
            send_sem=near_send.at[h, i, e],
            recv_sem=near_recv.at[h, i, e],
            device_id={"seq": lax.rem(g + 1, seq)},
            device_id_type=MESH,
        )

    def q_copy(c, e):
        peer = lax.rem(b + e, blk)
        return pltpu.make_async_remote_copy(
            src_ref=q_ref.at[:, q_columns(peer, c)],
            dst_ref=q_group.at[c, b],
            send_sem=q_send.at[c, e - 1],
            recv_sem=q_recv.at[c, e - 1],
            device_id={"blk": peer},
            device_id_type=MESH,
        )

    for j in range(blk):
        first_row = g * group_len + j * BLOCK
        row_pos = first_row + lax.broadcasted_iota(jnp.int32, (BLOCK, 1), 0)
        end = jnp.int32(0)
        start = jnp.zeros((BLOCK, 1), jnp.int32)
        for n in range(lengths_ref.shape[0]):
            end = end + lengths_ref[n]
            start = jnp.where(row_pos >= end, end, start)
        key_pos = first_row - group_len + lax.broadcasted_iota(jnp.int32, (BLOCK, window), 1)
        allowed = (key_pos >= start) & (key_pos <= row_pos)
        bias[j] = jnp.where(allowed, 0.0, masked_score)
    block_out[blk] = jnp.zeros(block_out.shape[1:], block_out.dtype)

    @pl.when(g == 0)
    def _():
        for h in range(groups_kv):
            for j in range(blk):
                k_near[h, j] = jnp.zeros(k_near.shape[2:], k_near.dtype)
                v_near[h, j] = jnp.zeros(v_near.shape[2:], v_near.dtype)

    pl.semaphore_wait(barrier, blk - 1 + seq - 1)

    def send_kv(h):
        for e in range(1, blk):
            for i in range(2):
                kv_copy(h, i, e).start()

    def send_q(c):
        for e in range(1, blk):
            q_copy(c, e).start()

    def forward_kv(h):
        for e in range(1, blk):
            for i in range(2):
                kv_copy(h, i, e).wait_recv()

        @pl.when(g < seq - 1)
        def _():
            for e in range(1, blk):
                for i in range(2):
                    near_copy(h, i, e).start()

    def wait_near(h):
        @pl.when(g > 0)
        def _():
            for e in range(blk):
                for i in range(2):
                    near_copy(h, i, e).wait_recv()

    send_kv(0)

    @pl.when(g < seq - 1)
    def _():
        for h in range(groups_kv):
            for i in range(2):
                near_copy(h, i, 0).start()

    send_q(0)
    for h in range(1, groups_kv):
        send_kv(h)
    for c in range(1, chunks):
        send_q(c)

    forward_kv(0)
    for copy in own_kv:
        copy.wait()

    half = seq // 2
    side, place_in = g // half, lax.rem(g, half)

    def target(k):
        if k < half:
            return side * half + lax.rem(place_in + k, half)
        return (1 - side) * half + lax.rem(place_in + k - half, half)

    def origin_of(k):
        if k < half:
            return side * half + lax.rem(place_in - k + half, half)
        return (1 - side) * half + lax.rem(place_in - (k - half) + half, half)

    picked = []
    for d in range(seq):
        owner = target(d)
        index = jnp.int32(blk)
        for j in range(blk):
            index = jnp.where(plan_ref[j, g] == owner, jnp.int32(j), index)
        picked.append(index)

    def z_copy(c, d):
        return pltpu.make_async_remote_copy(
            src_ref=message.at[c, d],
            dst_ref=landed.at[c, d - 1],
            send_sem=z_send.at[c, d - 1],
            recv_sem=z_recv.at[c, d - 1],
            device_id={"seq": target(d)},
            device_id_type=MESH,
        )

    near, far = list(range(1, half)), list(range(half, seq))
    sends = [[] for _ in range(chunks)]
    for c in range(chunks):
        if c > 0:
            sends[c] += [(c, k) for k in near]
        if c in (0, chunks - 1):
            sends[c] += [(m, k) for m in range(max(c - 1, min(c, 1)), c + 1) for k in far]
        elif c > 1:
            sends[c] += [(c - 1, k) for k in far]
        if c == 0:
            sends[c] += [(c, k) for k in near]
    arrivals = [message for row in sends for message in row]
    for c in range(chunks):
        own_q[c].wait()
        for e in range(1, blk):
            q_copy(c, e).wait_recv()
        kv_head = c * chunk_heads // heads_per_group
        if c * chunk_heads % heads_per_group == 0 or c == 0:
            wait_near(kv_head)
        for j in range(blk):
            query = q_group[c, j]
            rows = jnp.concatenate(
                [query[:, h * HEAD_WIDTH : (h + 1) * HEAD_WIDTH] for h in range(chunk_heads)], axis=0
            )
            keys = k_near[kv_head, j : j + blk + 1].reshape(window, HEAD_WIDTH)
            values = v_near[kv_head, j : j + blk + 1].reshape(window, HEAD_WIDTH)
            scores = lax.dot_general(
                rows, keys, (((1,), (1,)), ((), ())), preferred_element_type=jnp.float32
            )
            scores = scores.reshape(chunk_heads, BLOCK, window) * scale + bias[j][None]
            top = jnp.max(scores, axis=2, keepdims=True)
            weights = jnp.exp(scores - top)
            total = jnp.sum(weights, axis=2, keepdims=True)
            mixed = jnp.dot(
                weights.astype(jnp.bfloat16).reshape(chunk_heads * BLOCK, window),
                values,
                preferred_element_type=jnp.float32,
            ).reshape(chunk_heads, BLOCK, HEAD_WIDTH)
            result = (mixed / total).astype(jnp.bfloat16)
            for h in range(chunk_heads):
                block_out[j, :, h * HEAD_WIDTH : (h + 1) * HEAD_WIDTH] = result[h]
        for d in range(seq):
            message[c, d] = block_out[picked[d]]
        for m, k in sends[c]:
            z_copy(m, k).start()
        if c == 0:
            for h in range(1, groups_kv):
                forward_kv(h)

    def place(c, d, waiting):
        origin = origin_of(d)
        source = message.at[c, 0] if d == 0 else landed.at[c, d - 1]
        holder = origin // slots
        slot = lax.rem(origin, slots)
        target = out_ref.at[
            pl.ds(pl.multiple_of(slot * BLOCK, BLOCK), BLOCK), q_columns(b, c)
        ]
        hop = lax.rem(holder - b + blk, blk)

        @pl.when(holder == b)
        def _():
            copy = pltpu.make_async_copy(source, target, x_send.at[c, d])
            if waiting:
                copy.wait()
            else:
                copy.start()

        @pl.when(holder != b)
        def _():
            copy = pltpu.make_async_remote_copy(
                src_ref=source,
                dst_ref=target,
                send_sem=x_send.at[c, d],
                recv_sem=x_recv.at[c, slot, lax.rem(hop - 1 + blk, blk)],
                device_id={"blk": holder},
                device_id_type=MESH,
            )
            if waiting:
                copy.wait_send()
            else:
                copy.start()

    for c in range(chunks):
        place(c, 0, False)
    for c, d in arrivals:
        z_copy(c, d).wait_recv()
        place(c, d, False)

    for c in range(chunks):
        for s in range(slots):
            for e in range(1, blk):
                sender = lax.rem(b - e + blk, blk)
                pltpu.make_async_remote_copy(
                    src_ref=message.at[c, 0],
                    dst_ref=out_ref.at[s * BLOCK : (s + 1) * BLOCK, q_columns(sender, c)],
                    send_sem=x_send.at[c, 0],
                    recv_sem=x_recv.at[c, s, e - 1],
                    device_id={"blk": sender},
                    device_id_type=MESH,
                ).wait_recv()
        for d in range(seq):
            place(c, d, True)
            if d > 0:
                z_copy(c, d).wait_send()
        for e in range(1, blk):
            q_copy(c, e).wait_send()
    for h in range(groups_kv):
        for i in range(2):
            for e in range(1, blk):
                kv_copy(h, i, e).wait_send()

    @pl.when(g < seq - 1)
    def _():
        for h in range(groups_kv):
            for e in range(blk):
                for i in range(2):
                    near_copy(h, i, e).wait_send()


def settle(pieces, src_ref, dst_ref, held, in_sem, out_sem):
    rows = src_ref.shape[0] // pieces
    taken = [
        pltpu.make_async_copy(src_ref.at[pl.ds(n * rows, rows)], held.at[n], in_sem.at[n])
        for n in range(pieces)
    ]
    put = [
        pltpu.make_async_copy(held.at[n], dst_ref.at[pl.ds(n * rows, rows)], out_sem.at[n])
        for n in range(pieces)
    ]
    for copy in taken:
        copy.start()
    for n in range(pieces):
        taken[n].wait()
        put[n].start()
    for copy in put:
        copy.wait()


def quad_kernel(
    dims,
    lengths_hbm,
    plan_hbm,
    q_ref,
    k_ref,
    v_ref,
    out_ref,
    extra_ref,
    flag_ref,
    q_group,
    k_near,
    v_near,
    bias,
    block_out,
    first,
    second,
    homeward,
    relay,
    spare,
    land_first,
    land_near,
    land_second,
    mine,
    word,
    word_in,
    lengths_ref,
    plan_ref,
    table_sem,
    local_sem,
    q_send,
    q_recv,
    kv_send,
    kv_recv,
    near_send,
    near_recv,
    first_send,
    first_recv,
    second_send,
    near_x_recv,
    second_recv,
    home_send,
    home_recv,
    x_send,
    x_recv,
    extra_sem,
    word_send,
    word_recv,
):
    seq, blk, heads_dev, groups_kv, heads_per_group, chunk_heads, slots, parts = dims
    g = lax.axis_index("seq")
    b = lax.axis_index("blk")
    part = lax.axis_index("groups")
    chunks = heads_dev // chunk_heads
    width = chunk_heads * HEAD_WIDTH
    columns_dev = heads_dev * HEAD_WIDTH
    window = (blk + 1) * BLOCK
    group_len = blk * BLOCK
    scale = math.log2(math.e) / math.sqrt(HEAD_WIDTH)

    left = g < 2
    inner = (g == 1) | (g == 2)
    outer = jnp.logical_not(inner)
    far_inner = jnp.where(left, 2, 1)
    far_outer = jnp.where(left, 3, 0)
    near_inner = jnp.where(left, 1, 2)
    near_outer = jnp.where(left, 0, 3)
    peer = 1 - b

    def kv_columns(owner, h):
        start = owner * heads_dev // heads_per_group + h
        return pl.ds(pl.multiple_of(start * HEAD_WIDTH, HEAD_WIDTH), HEAD_WIDTH)

    def q_columns(owner, c):
        return pl.ds(pl.multiple_of(owner * columns_dev + c * width, HEAD_WIDTH), width)

    def remote(src, dst, send, recv, **where):
        return pltpu.make_async_remote_copy(
            src_ref=src,
            dst_ref=dst,
            send_sem=send,
            recv_sem=recv,
            device_id=where,
            device_id_type=MESH,
        )

    barrier = pltpu.get_barrier_semaphore()
    greeted = [{"blk": peer}, {"groups": lax.rem(part + 1, parts)}]
    greeted += [{"seq": lax.rem(g + d, seq)} for d in range(1, seq)]
    greeted += [{"seq": lax.rem(g + d, seq), "blk": peer} for d in (1, seq - 1)]
    for device in greeted:
        pl.semaphore_signal(barrier, inc=1, device_id=device, device_id_type=MESH)

    tables = [
        pltpu.make_async_copy(lengths_hbm, lengths_ref, table_sem.at[0]),
        pltpu.make_async_copy(plan_hbm, plan_ref, table_sem.at[1]),
    ]
    for copy in tables:
        copy.start()
    pairs = ((k_ref, k_near), (v_ref, v_near))
    own_kv = [
        pltpu.make_async_copy(
            src.at[:, kv_columns(b, h)], dst.at[h, blk + b], local_sem.at[2 * h + i]
        )
        for h in range(groups_kv)
        for i, (src, dst) in enumerate(pairs)
    ]
    own_q = [
        pltpu.make_async_copy(
            q_ref.at[:, q_columns(b, c)], q_group.at[c, b], local_sem.at[2 * groups_kv + c]
        )
        for c in range(chunks)
    ]
    for copy in own_kv + own_q:
        copy.start()

    def kv_copy(h, i):
        src, dst = pairs[i]
        return remote(
            src.at[:, kv_columns(peer, h)],
            dst.at[h, blk + b],
            kv_send.at[h, i],
            kv_recv.at[h, i],
            blk=peer,
        )

    def near_copy(h, i, e):
        src, dst = pairs[i]
        to = b if e == 0 else peer
        return remote(
            src.at[:, kv_columns(to, h)],
            dst.at[h, b],
            near_send.at[h, i, e],
            near_recv.at[h, i, e],
            seq=lax.rem(g + 1, seq),
            blk=to,
        )

    def q_copy(c):
        return remote(
            q_ref.at[:, q_columns(peer, c)],
            q_group.at[c, b],
            q_send.at[c],
            q_recv.at[c],
            blk=peer,
        )

    @pl.when(g == 0)
    def _():
        for h in range(groups_kv):
            for j in range(blk):
                k_near[h, j] = jnp.zeros(k_near.shape[2:], k_near.dtype)
                v_near[h, j] = jnp.zeros(v_near.shape[2:], v_near.dtype)

    pl.semaphore_wait(barrier, len(greeted))

    def word_copy():
        return remote(word, word_in, word_send, word_recv, groups=lax.rem(part + 1, parts))

    def send_kv(h):
        for i in range(2):
            kv_copy(h, i).start()

        @pl.when(g < seq - 1)
        def _():
            for e in (1, 0):
                for i in range(2):
                    near_copy(h, i, e).start()

    send_kv(0)
    q_copy(0).start()
    q_copy(1).start()
    for h in range(1, groups_kv):
        send_kv(h)
    for c in range(2, chunks):
        q_copy(c).start()

    for copy in tables:
        copy.wait()

    def has(group, owner):
        return (plan_ref[0, group] == owner) | (plan_ref[1, group] == owner)

    def pick(owner):
        return jnp.where(
            plan_ref[0, g] == owner,
            jnp.int32(0),
            jnp.where(plan_ref[1, g] == owner, jnp.int32(1), jnp.int32(blk)),
        )

    full_right = has(0, 2) & has(0, 3) & has(1, 2) & has(1, 3)
    full_left = has(3, 1) & has(3, 0) & has(2, 1) & has(2, 0)
    spilled = jnp.where(full_right | full_left, jnp.int32(1), jnp.int32(0))
    word[...] = jnp.full(word.shape, spilled, jnp.int32)

    for j in range(blk):
        first_row = g * group_len + j * BLOCK
        row_pos = first_row + lax.broadcasted_iota(jnp.int32, (BLOCK, 1), 0)
        end = jnp.int32(0)
        start = jnp.zeros((BLOCK, 1), jnp.int32)
        for n in range(lengths_ref.shape[0]):
            end = end + lengths_ref[n]
            start = jnp.where(row_pos >= end, end, start)
        key_pos = first_row - group_len + lax.broadcasted_iota(jnp.int32, (BLOCK, window), 1)
        allowed = (key_pos >= start) & (key_pos <= row_pos)
        bias[j] = jnp.where(allowed, 0.0, masked_score)
    block_out[blk] = jnp.zeros(block_out.shape[1:], block_out.dtype)

    word_copy().start()
    for copy in own_kv:
        copy.wait()

    sender = jnp.where(inner, 1, 0)

    def first_copy(c, which):
        return remote(
            first.at[c],
            land_first.at[c, which],
            first_send.at[c],
            first_recv.at[c, which],
            seq=far_inner,
        )

    def to_near(c):
        return remote(
            second.at[c], land_near.at[c], second_send.at[c], near_x_recv.at[c], seq=near_inner
        )

    def to_far(c):
        return remote(
            second.at[c], land_second.at[c], second_send.at[c], second_recv.at[c], seq=far_inner
        )

    def home_copy(c, k):
        source = homeward.at[c] if k == 0 else relay.at[c, k - 1]
        group = (near_inner, far_inner, far_outer)[k]
        return remote(
            source, mine.at[c, group], home_send.at[c, k], home_recv.at[c, k], seq=near_outer
        )

    def extra_copy(c):
        return pltpu.make_async_copy(spare.at[c], extra_ref.at[c], extra_sem.at[c])

    def place(c, group, waiting):
        source = mine.at[c, group]
        holder = group // slots
        slot = lax.rem(group, slots)
        target = out_ref.at[
            pl.ds(pl.multiple_of(slot * BLOCK, BLOCK), BLOCK), q_columns(b, c)
        ]

        @pl.when(holder == b)
        def _():
            copy = pltpu.make_async_copy(source, target, x_send.at[c, group])
            if waiting:
                copy.wait()
            else:
                copy.start()

        @pl.when(holder != b)
        def _():
            copy = remote(
                source, target, x_send.at[c, group], x_recv.at[c, slot], blk=holder
            )
            if waiting:
                copy.wait_send()
            else:
                copy.start()

    to_inner, to_outer = pick(far_inner), pick(far_outer)
    both = (to_inner < blk) & (to_outer < blk)
    first_index = jnp.where(to_inner < blk, to_inner, to_outer)
    second_index = jnp.where(both, to_outer, jnp.int32(blk))
    near_index = jnp.where(both, to_outer, pick(near_inner))
    home_index, own_index = pick(near_outer), pick(g)

    near_both = has(near_outer, far_inner) & has(near_outer, far_outer)
    near_here = has(near_outer, g)
    a_here, a_on = has(far_outer, g), has(far_outer, near_outer)
    b_here, b_on = has(far_inner, g), has(far_inner, near_outer)
    nothing = jnp.zeros(block_out.shape[1:], block_out.dtype)

    def attend(c):
        own_q[c].wait()
        q_copy(c).wait_recv()
        kv_head = c * chunk_heads // heads_per_group
        if c * chunk_heads % heads_per_group == 0:
            for i in range(2):
                kv_copy(kv_head, i).wait_recv()

            @pl.when(g > 0)
            def _():
                for e in range(2):
                    for i in range(2):
                        near_copy(kv_head, i, e).wait_recv()

        for j in range(blk):
            query = q_group[c, j]
            rows = jnp.concatenate(
                [query[:, h * HEAD_WIDTH : (h + 1) * HEAD_WIDTH] for h in range(chunk_heads)], axis=0
            )
            keys = k_near[kv_head, j : j + blk + 1].reshape(window, HEAD_WIDTH)
            values = v_near[kv_head, j : j + blk + 1].reshape(window, HEAD_WIDTH)
            scores = lax.dot_general(
                rows, keys, (((1,), (1,)), ((), ())), preferred_element_type=jnp.float32
            )
            scores = scores.reshape(chunk_heads, BLOCK, window) * scale + bias[j][None]
            top = jnp.max(scores, axis=2, keepdims=True)
            weights = jnp.exp2(scores - top)
            total = jnp.sum(weights, axis=2, keepdims=True)
            mixed = jnp.dot(
                weights.astype(jnp.bfloat16).reshape(chunk_heads * BLOCK, window),
                values,
                preferred_element_type=jnp.float32,
            ).reshape(chunk_heads, BLOCK, HEAD_WIDTH)
            result = (mixed / total).astype(jnp.bfloat16)
            for h in range(chunk_heads):
                block_out[j, :, h * HEAD_WIDTH : (h + 1) * HEAD_WIDTH] = result[h]

    def dispatch(c):
        first[c] = block_out[first_index]
        first_copy(c, sender).start()

        @pl.when(outer)
        def _():
            second[c] = block_out[near_index]
            to_near(c).start()

        @pl.when(inner)
        def _():
            homeward[c] = block_out[home_index]
            home_copy(c, 0).start()
            spare[c] = block_out[second_index]
            extra_copy(c).start()

        mine[c, g] = block_out[own_index]
        place(c, g, False)

    def join(c):
        to_near(c).wait_recv()
        arrived = land_near[c]
        second[c] = jnp.where(near_both, arrived, spare[c])
        to_far(c).start()
        mine[c, near_outer] = jnp.where(near_here, arrived, nothing)
        place(c, near_outer, False)

    def spread(c):
        first_copy(c, 0).wait_recv()
        first_copy(c, 1).wait_recv()
        to_far(c).wait_recv()
        from_outer, from_inner, last = land_first[c, 0], land_first[c, 1], land_second[c]
        relay[c, 1] = jnp.where(a_on, jnp.where(a_here, last, from_outer), nothing)
        home_copy(c, 2).start()
        rest = jnp.where(a_here & a_on, nothing, last)
        relay[c, 0] = jnp.where(b_on, jnp.where(b_here, rest, from_inner), nothing)
        home_copy(c, 1).start()
        mine[c, far_outer] = jnp.where(a_here, from_outer, nothing)
        place(c, far_outer, False)
        mine[c, far_inner] = jnp.where(b_here, from_inner, nothing)
        place(c, far_inner, False)

    def collect(c):
        for k, group in enumerate((near_inner, far_inner, far_outer)):
            home_copy(c, k).wait_recv()
            place(c, group, False)

    for t in range(chunks + 3):
        if t < chunks:
            attend(t)
            dispatch(t)

        @pl.when(inner)
        def _():
            if 0 <= t - JOIN_LAG < chunks:
                join(t - JOIN_LAG)
            if 0 <= t - SPREAD_LAG < chunks:
                spread(t - SPREAD_LAG)

        @pl.when(outer)
        def _():
            if 0 <= t - COLLECT_LAG < chunks:
                collect(t - COLLECT_LAG)

    word_copy().wait()
    flag_ref[0, 0] = jnp.maximum(spilled, jnp.max(word_in[...]))

    for c in range(chunks):
        for s in range(slots):
            remote(
                mine.at[c, 0],
                out_ref.at[s * BLOCK : (s + 1) * BLOCK, q_columns(peer, c)],
                x_send.at[c, 0],
                x_recv.at[c, s],
                blk=peer,
            ).wait_recv()
        for s in range(seq):
            place(c, s, True)
        q_copy(c).wait_send()
        first_copy(c, sender).wait_send()

    @pl.when(outer)
    def _():
        for c in range(chunks):
            to_near(c).wait_send()

    @pl.when(inner)
    def _():
        for c in range(chunks):
            to_far(c).wait_send()
            extra_copy(c).wait()
            for k in range(3):
                home_copy(c, k).wait_send()

    for h in range(groups_kv):
        for i in range(2):
            kv_copy(h, i).wait_send()

    @pl.when(g < seq - 1)
    def _():
        for h in range(groups_kv):
            for e in range(2):
                for i in range(2):
                    near_copy(h, i, e).wait_send()


def spill_kernel(dims, extra_ref, got_ref, send, recv):
    seq, blk, chunks, width, slots = dims
    g = lax.axis_index("seq")
    b = lax.axis_index("blk")
    inner = (g == 1) | (g == 2)
    mate = lax.rem(g + 2, seq)
    barrier = pltpu.get_barrier_semaphore()
    for e in range(blk):
        pl.semaphore_signal(
            barrier, inc=1, device_id={"seq": mate, "blk": e}, device_id_type=MESH
        )
    pl.semaphore_wait(barrier, blk)

    def spill(c, half, holder):
        return pltpu.make_async_remote_copy(
            src_ref=extra_ref.at[c],
            dst_ref=got_ref.at[
                :, pl.ds(pl.multiple_of((half * chunks + c) * width, width), width)
            ],
            send_sem=send.at[c],
            recv_sem=recv.at[c, half],
            device_id={"seq": mate, "blk": holder},
            device_id_type=MESH,
        )

    @pl.when(inner)
    def _():
        for c in range(chunks):
            spill(c, b, g // slots).start()
        for c in range(chunks):
            spill(c, b, g // slots).wait_send()

    @pl.when(jnp.logical_not(inner) & (b == mate // slots))
    def _():
        for c in range(chunks):
            for half in range(blk):
                spill(c, half, b).wait_recv()


def finish(pieces, src_ref, dst_ref, sem):
    rows = src_ref.shape[0] // pieces
    copies = [
        pltpu.make_async_copy(
            src_ref.at[pl.ds(n * rows, rows)], dst_ref.at[pl.ds(n * rows, rows)], sem.at[n]
        )
        for n in range(pieces)
    ]
    for copy in copies:
        copy.start()
    for copy in copies:
        copy.wait()


def finish_spilled(slots, plan_ref, src_ref, got_ref, dst_ref, sem):
    owner = lax.axis_index("seq")
    b = lax.axis_index("blk")

    def has(group, wanted):
        return (plan_ref[0, group] == wanted) | (plan_ref[1, group] == wanted)

    full_right = has(0, 2) & has(0, 3) & has(1, 2) & has(1, 3)
    full_left = has(3, 1) & has(3, 0) & has(2, 1) & has(2, 0)
    for s in range(slots):
        group = b * slots + s
        rows = pl.ds(s * BLOCK, BLOCK)
        spilled = ((group == 1) & (owner == 3) & full_right) | (
            (group == 2) & (owner == 0) & full_left
        )

        @pl.when(spilled)
        def _():
            copy = pltpu.make_async_copy(got_ref, dst_ref.at[rows], sem.at[s])
            copy.start()
            copy.wait()

        @pl.when(jnp.logical_not(spilled))
        def _():
            copy = pltpu.make_async_copy(src_ref.at[rows], dst_ref.at[rows], sem.at[s])
            copy.start()
            copy.wait()


def quad(queries, rotated_keys, head_value_rows, doc_lengths, owner_plan):
    blk = lax.axis_size("blk")
    seq = lax.axis_size("seq")
    parts = lax.axis_size("groups")
    heads_dev = queries.shape[1] // HEAD_WIDTH // blk
    heads_per_group = QUERY_HEADS // KEY_HEADS
    groups_kv = heads_dev // heads_per_group
    chunk_heads = CHUNK_HEADS
    chunks = heads_dev // chunk_heads
    slots = seq // blk
    width = chunk_heads * HEAD_WIDTH
    dims = (seq, blk, heads_dev, groups_kv, heads_per_group, chunk_heads, slots, parts)
    bf16 = jnp.bfloat16
    dma = pltpu.SemaphoreType.DMA
    hbm = pl.BlockSpec(memory_space=pltpu.HBM)
    plan = owner_plan.T
    out_shape = jax.ShapeDtypeStruct((slots * BLOCK, queries.shape[1]), bf16)

    def unit(*lead):
        return pltpu.VMEM(lead + (BLOCK, width), bf16)

    placed, extra, flag = pl.pallas_call(
        functools.partial(quad_kernel, dims),
        out_shape=(
            out_shape,
            jax.ShapeDtypeStruct((chunks, BLOCK, width), bf16),
            jax.ShapeDtypeStruct((1, 1), jnp.int32),
        ),
        in_specs=[hbm] * 5,
        out_specs=(
            pl.BlockSpec(memory_space=pl.ANY),
            pl.BlockSpec(memory_space=pl.ANY),
            pl.BlockSpec(memory_space=pltpu.SMEM),
        ),
        scratch_shapes=[
            unit(chunks, blk),
            pltpu.VMEM((groups_kv, 2 * blk, BLOCK, HEAD_WIDTH), bf16),
            pltpu.VMEM((groups_kv, 2 * blk, BLOCK, HEAD_WIDTH), bf16),
            pltpu.VMEM((blk, BLOCK, (blk + 1) * BLOCK), jnp.float32),
            unit(blk + 1),
            unit(chunks),
            unit(chunks),
            unit(chunks),
            unit(chunks, 2),
            unit(chunks),
            unit(chunks, 2),
            unit(chunks),
            unit(chunks),
            unit(chunks, seq),
            pltpu.VMEM((8, 128), jnp.int32),
            pltpu.VMEM((8, 128), jnp.int32),
            pltpu.SMEM(doc_lengths.shape, jnp.int32),
            pltpu.SMEM(plan.shape, jnp.int32),
            dma((2,)),
            dma((2 * groups_kv + chunks,)),
            dma((chunks,)),
            dma((chunks,)),
            dma((groups_kv, 2)),
            dma((groups_kv, 2)),
            dma((groups_kv, 2, 2)),
            dma((groups_kv, 2, 2)),
            dma((chunks,)),
            dma((chunks, 2)),
            dma((chunks,)),
            dma((chunks,)),
            dma((chunks,)),
            dma((chunks, 3)),
            dma((chunks, 3)),
            dma((chunks, seq)),
            dma((chunks, slots)),
            dma((chunks,)),
            dma,
            dma,
        ],
        compiler_params=pltpu.CompilerParams(
            collective_id=0, has_side_effects=True, vmem_limit_bytes=VMEM_MAIN
        ),
    )(doc_lengths, plan, queries, rotated_keys, head_value_rows)

    def plain(placed, extra):
        return pl.pallas_call(
            functools.partial(finish, PIECES),
            out_shape=out_shape,
            in_specs=[pl.BlockSpec(memory_space=pl.ANY)],
            out_specs=hbm,
            scratch_shapes=[dma((PIECES,))],
            compiler_params=pltpu.CompilerParams(vmem_limit_bytes=VMEM_REST),
        )(placed)

    def spilled(placed, extra):
        got = pl.pallas_call(
            functools.partial(spill_kernel, (seq, blk, chunks, width, slots)),
            out_shape=jax.ShapeDtypeStruct((BLOCK, queries.shape[1]), bf16),
            in_specs=[pl.BlockSpec(memory_space=pl.ANY)],
            out_specs=pl.BlockSpec(memory_space=pl.ANY),
            scratch_shapes=[dma((chunks,)), dma((chunks, blk))],
            compiler_params=pltpu.CompilerParams(
                collective_id=1, has_side_effects=True, vmem_limit_bytes=VMEM_REST
            ),
        )(extra)
        return pl.pallas_call(
            functools.partial(finish_spilled, slots),
            out_shape=out_shape,
            in_specs=[pl.BlockSpec(memory_space=pltpu.SMEM)]
            + [pl.BlockSpec(memory_space=pl.ANY)] * 2,
            out_specs=hbm,
            scratch_shapes=[dma((slots,))],
            compiler_params=pltpu.CompilerParams(vmem_limit_bytes=VMEM_REST),
        )(plan, placed, got)

    return lax.cond(flag[0, 0] > 0, spilled, plain, placed, extra)


def per_device(queries, rotated_keys, head_value_rows, doc_lengths, owner_plan):
    blk = lax.axis_size("blk")
    seq = lax.axis_size("seq")
    heads_dev = queries.shape[1] // HEAD_WIDTH // blk
    heads_per_group = QUERY_HEADS // KEY_HEADS
    groups_kv = max(1, heads_dev // heads_per_group)
    chunk_heads = min(CHUNK_HEADS, heads_dev, heads_per_group)
    chunks = heads_dev // chunk_heads
    slots = seq // blk
    if (seq, blk, lax.axis_size("groups")) == (4, 2, 2) and heads_dev % heads_per_group == 0:
        return quad(queries, rotated_keys, head_value_rows, doc_lengths, owner_plan)
    width = chunk_heads * HEAD_WIDTH
    dims = (seq, blk, heads_dev, groups_kv, heads_per_group, chunk_heads, slots)
    bf16 = jnp.bfloat16
    dma = pltpu.SemaphoreType.DMA
    placed = pl.pallas_call(
        functools.partial(kernel, dims),
        out_shape=jax.ShapeDtypeStruct((slots * BLOCK, queries.shape[1]), bf16),
        in_specs=[pl.BlockSpec(memory_space=pltpu.SMEM)] * 2
        + [pl.BlockSpec(memory_space=pl.ANY)] * 3,
        out_specs=pl.BlockSpec(memory_space=pl.ANY),
        scratch_shapes=[
            pltpu.VMEM((chunks, blk, BLOCK, width), bf16),
            pltpu.VMEM((groups_kv, 2 * blk, BLOCK, HEAD_WIDTH), bf16),
            pltpu.VMEM((groups_kv, 2 * blk, BLOCK, HEAD_WIDTH), bf16),
            pltpu.VMEM((blk, BLOCK, (blk + 1) * BLOCK), jnp.float32),
            pltpu.VMEM((blk + 1, BLOCK, width), bf16),
            pltpu.VMEM((chunks, seq, BLOCK, width), bf16),
            pltpu.VMEM((chunks, seq - 1, BLOCK, width), bf16),
            dma((2 * groups_kv + chunks,)),
            dma((chunks, blk - 1)),
            dma((chunks, blk - 1)),
            dma((groups_kv, 2, blk - 1)),
            dma((groups_kv, 2, blk - 1)),
            dma((groups_kv, 2, blk)),
            dma((groups_kv, 2, blk)),
            dma((chunks, seq - 1)),
            dma((chunks, seq - 1)),
            dma((chunks, seq)),
            dma((chunks, slots, blk)),
        ],
        compiler_params=pltpu.CompilerParams(collective_id=0, has_side_effects=True),
    )(doc_lengths, owner_plan.T, queries, rotated_keys, head_value_rows)
    pieces = PIECES
    return pl.pallas_call(
        functools.partial(settle, pieces),
        out_shape=jax.ShapeDtypeStruct(placed.shape, bf16),
        in_specs=[pl.BlockSpec(memory_space=pl.ANY)],
        out_specs=pl.BlockSpec(memory_space=pl.ANY),
        scratch_shapes=[
            pltpu.VMEM((pieces, placed.shape[0] // pieces, placed.shape[1]), bf16),
            dma((pieces,)),
            dma((pieces,)),
        ],
    )(placed)


def solution(mesh):
    in_specs = (
        P(("groups", "seq", "blk"), "tp"),
        P(("groups", "seq", "blk"), "tp"),
        P(("groups", "seq", "blk"), "tp"),
        P("groups"),
        P("groups", None),
    )
    out_specs = P(("groups", "seq", "blk"), "tp")
    return jax.shard_map(
        per_device, mesh=mesh, in_specs=in_specs, out_specs=out_specs, check_vma=False
    )
```

```python
import functools
import math

import jax
import jax.numpy as jnp
from jax import lax
from jax.experimental import pallas as pl
from jax.experimental.pallas import tpu as pltpu
from jax.sharding import PartitionSpec as P

QUERY_HEADS = 64
KEY_HEADS = 8
HEAD_WIDTH = 128
BLOCK = 128
CHUNK_HEADS = 2
PIECES = 8

MESH = pl.DeviceIdType.MESH
masked_score = -1e30
JOIN_LAG = 1
SPREAD_LAG = 3
DIRECT_HEADS = 1
VMEM_MAIN = 58 * 2**20
QUERY_LEAD = 2
KV_LEAD = 4
VMEM_REST = 4 * 2**20


def kernel(
    dims,
    lengths_ref,
    plan_ref,
    q_ref,
    k_ref,
    v_ref,
    out_ref,
    q_group,
    k_near,
    v_near,
    bias,
    block_out,
    message,
    landed,
    local_sem,
    q_send,
    q_recv,
    kv_send,
    kv_recv,
    near_send,
    near_recv,
    z_send,
    z_recv,
    x_send,
    x_recv,
):
    seq, blk, heads_dev, groups_kv, heads_per_group, chunk_heads, slots = dims
    g = lax.axis_index("seq")
    b = lax.axis_index("blk")
    chunks = heads_dev // chunk_heads
    width = chunk_heads * HEAD_WIDTH
    columns_dev = heads_dev * HEAD_WIDTH
    window = (blk + 1) * BLOCK
    group_len = blk * BLOCK
    scale = 1.0 / math.sqrt(HEAD_WIDTH)

    def kv_columns(owner, h):
        first = owner * heads_dev // heads_per_group + h
        return pl.ds(pl.multiple_of(first * HEAD_WIDTH, HEAD_WIDTH), HEAD_WIDTH)

    def q_columns(owner, c):
        return pl.ds(pl.multiple_of(owner * columns_dev + c * width, HEAD_WIDTH), width)

    barrier = pltpu.get_barrier_semaphore()
    for e in range(1, blk):
        pl.semaphore_signal(
            barrier, inc=1, device_id={"blk": lax.rem(b + e, blk)}, device_id_type=MESH
        )
    for d in range(1, seq):
        pl.semaphore_signal(
            barrier, inc=1, device_id={"seq": lax.rem(g + d, seq)}, device_id_type=MESH
        )

    pairs = ((k_ref, k_near), (v_ref, v_near))
    own_kv = [
        pltpu.make_async_copy(
            src.at[:, kv_columns(b, h)], dst.at[h, blk + b], local_sem.at[2 * h + i]
        )
        for h in range(groups_kv)
        for i, (src, dst) in enumerate(pairs)
    ]
    own_q = [
        pltpu.make_async_copy(
            q_ref.at[:, q_columns(b, c)], q_group.at[c, b], local_sem.at[2 * groups_kv + c]
        )
        for c in range(chunks)
    ]
    for copy in own_kv + own_q:
        copy.start()

    def kv_copy(h, i, e):
        src, dst = pairs[i]
        peer = lax.rem(b + e, blk)
        return pltpu.make_async_remote_copy(
            src_ref=src.at[:, kv_columns(peer, h)],
            dst_ref=dst.at[h, blk + b],
            send_sem=kv_send.at[h, i, e - 1],
            recv_sem=kv_recv.at[h, i, e - 1],
            device_id={"blk": peer},
            device_id_type=MESH,
        )

    def near_copy(h, i, e):
        src, dst = pairs[i]
        origin = lax.rem(b - e + blk, blk)
        if e == 0:
            source = src.at[:, kv_columns(b, h)]
        else:
            source = dst.at[h, blk + origin]
        return pltpu.make_async_remote_copy(
            src_ref=source,
            dst_ref=dst.at[h, origin],
            send_sem=near_send.at[h, i, e],
            recv_sem=near_recv.at[h, i, e],
            device_id={"seq": lax.rem(g + 1, seq)},
            device_id_type=MESH,
        )

    def q_copy(c, e):
        peer = lax.rem(b + e, blk)
        return pltpu.make_async_remote_copy(
            src_ref=q_ref.at[:, q_columns(peer, c)],
            dst_ref=q_group.at[c, b],
            send_sem=q_send.at[c, e - 1],
            recv_sem=q_recv.at[c, e - 1],
            device_id={"blk": peer},
            device_id_type=MESH,
        )

    for j in range(blk):
        first_row = g * group_len + j * BLOCK
        row_pos = first_row + lax.broadcasted_iota(jnp.int32, (BLOCK, 1), 0)
        end = jnp.int32(0)
        start = jnp.zeros((BLOCK, 1), jnp.int32)
        for n in range(lengths_ref.shape[0]):
            end = end + lengths_ref[n]
            start = jnp.where(row_pos >= end, end, start)
        key_pos = first_row - group_len + lax.broadcasted_iota(jnp.int32, (BLOCK, window), 1)
        allowed = (key_pos >= start) & (key_pos <= row_pos)
        bias[j] = jnp.where(allowed, 0.0, masked_score)
    block_out[blk] = jnp.zeros(block_out.shape[1:], block_out.dtype)

    @pl.when(g == 0)
    def _():
        for h in range(groups_kv):
            for j in range(blk):
                k_near[h, j] = jnp.zeros(k_near.shape[2:], k_near.dtype)
                v_near[h, j] = jnp.zeros(v_near.shape[2:], v_near.dtype)

    pl.semaphore_wait(barrier, blk - 1 + seq - 1)

    def send_kv(h):
        for e in range(1, blk):
            for i in range(2):
                kv_copy(h, i, e).start()

    def send_q(c):
        for e in range(1, blk):
            q_copy(c, e).start()

    def forward_kv(h):
        for e in range(1, blk):
            for i in range(2):
                kv_copy(h, i, e).wait_recv()

        @pl.when(g < seq - 1)
        def _():
            for e in range(1, blk):
                for i in range(2):
                    near_copy(h, i, e).start()

    def wait_near(h):
        @pl.when(g > 0)
        def _():
            for e in range(blk):
                for i in range(2):
                    near_copy(h, i, e).wait_recv()

    send_kv(0)

    @pl.when(g < seq - 1)
    def _():
        for h in range(groups_kv):
            for i in range(2):
                near_copy(h, i, 0).start()

    send_q(0)
    for h in range(1, groups_kv):
        send_kv(h)
    for c in range(1, chunks):
        send_q(c)

    forward_kv(0)
    for copy in own_kv:
        copy.wait()

    half = seq // 2
    side, place_in = g // half, lax.rem(g, half)

    def target(k):
        if k < half:
            return side * half + lax.rem(place_in + k, half)
        return (1 - side) * half + lax.rem(place_in + k - half, half)

    def origin_of(k):
        if k < half:
            return side * half + lax.rem(place_in - k + half, half)
        return (1 - side) * half + lax.rem(place_in - (k - half) + half, half)

    picked = []
    for d in range(seq):
        owner = target(d)
        index = jnp.int32(blk)
        for j in range(blk):
            index = jnp.where(plan_ref[j, g] == owner, jnp.int32(j), index)
        picked.append(index)

    def z_copy(c, d):
        return pltpu.make_async_remote_copy(
            src_ref=message.at[c, d],
            dst_ref=landed.at[c, d - 1],
            send_sem=z_send.at[c, d - 1],
            recv_sem=z_recv.at[c, d - 1],
            device_id={"seq": target(d)},
            device_id_type=MESH,
        )

    near, far = list(range(1, half)), list(range(half, seq))
    sends = [[] for _ in range(chunks)]
    for c in range(chunks):
        if c > 0:
            sends[c] += [(c, k) for k in near]
        if c in (0, chunks - 1):
            sends[c] += [(m, k) for m in range(max(c - 1, min(c, 1)), c + 1) for k in far]
        elif c > 1:
            sends[c] += [(c - 1, k) for k in far]
        if c == 0:
            sends[c] += [(c, k) for k in near]
    arrivals = [message for row in sends for message in row]
    for c in range(chunks):
        own_q[c].wait()
        for e in range(1, blk):
            q_copy(c, e).wait_recv()
        kv_head = c * chunk_heads // heads_per_group
        if c * chunk_heads % heads_per_group == 0 or c == 0:
            wait_near(kv_head)
        for j in range(blk):
            query = q_group[c, j]
            rows = jnp.concatenate(
                [query[:, h * HEAD_WIDTH : (h + 1) * HEAD_WIDTH] for h in range(chunk_heads)], axis=0
            )
            keys = k_near[kv_head, j : j + blk + 1].reshape(window, HEAD_WIDTH)
            values = v_near[kv_head, j : j + blk + 1].reshape(window, HEAD_WIDTH)
            scores = lax.dot_general(
                rows, keys, (((1,), (1,)), ((), ())), preferred_element_type=jnp.float32
            )
            scores = scores.reshape(chunk_heads, BLOCK, window) * scale + bias[j][None]
            top = jnp.max(scores, axis=2, keepdims=True)
            weights = jnp.exp(scores - top)
            total = jnp.sum(weights, axis=2, keepdims=True)
            mixed = jnp.dot(
                weights.astype(jnp.bfloat16).reshape(chunk_heads * BLOCK, window),
                values,
                preferred_element_type=jnp.float32,
            ).reshape(chunk_heads, BLOCK, HEAD_WIDTH)
            result = (mixed / total).astype(jnp.bfloat16)
            for h in range(chunk_heads):
                block_out[j, :, h * HEAD_WIDTH : (h + 1) * HEAD_WIDTH] = result[h]
        for d in range(seq):
            message[c, d] = block_out[picked[d]]
        for m, k in sends[c]:
            z_copy(m, k).start()
        if c == 0:
            for h in range(1, groups_kv):
                forward_kv(h)

    def place(c, d, waiting):
        origin = origin_of(d)
        source = message.at[c, 0] if d == 0 else landed.at[c, d - 1]
        holder = origin // slots
        slot = lax.rem(origin, slots)
        target = out_ref.at[
            pl.ds(pl.multiple_of(slot * BLOCK, BLOCK), BLOCK), q_columns(b, c)
        ]
        hop = lax.rem(holder - b + blk, blk)

        @pl.when(holder == b)
        def _():
            copy = pltpu.make_async_copy(source, target, x_send.at[c, d])
            if waiting:
                copy.wait()
            else:
                copy.start()

        @pl.when(holder != b)
        def _():
            copy = pltpu.make_async_remote_copy(
                src_ref=source,
                dst_ref=target,
                send_sem=x_send.at[c, d],
                recv_sem=x_recv.at[c, slot, lax.rem(hop - 1 + blk, blk)],
                device_id={"blk": holder},
                device_id_type=MESH,
            )
            if waiting:
                copy.wait_send()
            else:
                copy.start()

    for c in range(chunks):
        place(c, 0, False)
    for c, d in arrivals:
        z_copy(c, d).wait_recv()
        place(c, d, False)

    for c in range(chunks):
        for s in range(slots):
            for e in range(1, blk):
                sender = lax.rem(b - e + blk, blk)
                pltpu.make_async_remote_copy(
                    src_ref=message.at[c, 0],
                    dst_ref=out_ref.at[s * BLOCK : (s + 1) * BLOCK, q_columns(sender, c)],
                    send_sem=x_send.at[c, 0],
                    recv_sem=x_recv.at[c, s, e - 1],
                    device_id={"blk": sender},
                    device_id_type=MESH,
                ).wait_recv()
        for d in range(seq):
            place(c, d, True)
            if d > 0:
                z_copy(c, d).wait_send()
        for e in range(1, blk):
            q_copy(c, e).wait_send()
    for h in range(groups_kv):
        for i in range(2):
            for e in range(1, blk):
                kv_copy(h, i, e).wait_send()

    @pl.when(g < seq - 1)
    def _():
        for h in range(groups_kv):
            for e in range(blk):
                for i in range(2):
                    near_copy(h, i, e).wait_send()


def settle(pieces, src_ref, dst_ref, held, in_sem, out_sem):
    rows = src_ref.shape[0] // pieces
    taken = [
        pltpu.make_async_copy(src_ref.at[pl.ds(n * rows, rows)], held.at[n], in_sem.at[n])
        for n in range(pieces)
    ]
    put = [
        pltpu.make_async_copy(held.at[n], dst_ref.at[pl.ds(n * rows, rows)], out_sem.at[n])
        for n in range(pieces)
    ]
    for copy in taken:
        copy.start()
    for n in range(pieces):
        taken[n].wait()
        put[n].start()
    for copy in put:
        copy.wait()


def quad_kernel(
    dims,
    lengths_hbm,
    plan_hbm,
    q_ref,
    k_ref,
    v_ref,
    out_ref,
    extra_ref,
    flag_ref,
    q_group,
    k_near,
    v_near,
    bias,
    block_out,
    first,
    second,
    homeward,
    relay,
    spare,
    land_first,
    land_near,
    land_second,
    mine,
    word,
    word_in,
    lengths_ref,
    plan_ref,
    table_sem,
    local_sem,
    q_send,
    q_recv,
    kv_send,
    kv_recv,
    near_send,
    near_recv,
    first_send,
    first_recv,
    second_send,
    near_x_recv,
    second_recv,
    home_send,
    x_send,
    x_recv,
    extra_sem,
    word_send,
    word_recv,
):
    seq, blk, heads_dev, groups_kv, heads_per_group, chunk_heads, slots, parts = dims
    g = lax.axis_index("seq")
    b = lax.axis_index("blk")
    part = lax.axis_index("groups")
    chunks = heads_dev // chunk_heads
    width = chunk_heads * HEAD_WIDTH
    columns_dev = heads_dev * HEAD_WIDTH
    window = (blk + 1) * BLOCK
    group_len = blk * BLOCK
    scale = math.log2(math.e) / math.sqrt(HEAD_WIDTH)

    left = g < 2
    inner = (g == 1) | (g == 2)
    outer = jnp.logical_not(inner)
    far_inner = jnp.where(left, 2, 1)
    far_outer = jnp.where(left, 3, 0)
    near_inner = jnp.where(left, 1, 2)
    near_outer = jnp.where(left, 0, 3)
    peer = 1 - b

    def kv_columns(owner, h):
        start = owner * heads_dev // heads_per_group + h
        return pl.ds(pl.multiple_of(start * HEAD_WIDTH, HEAD_WIDTH), HEAD_WIDTH)

    def q_columns(owner, c):
        return pl.ds(pl.multiple_of(owner * columns_dev + c * width, HEAD_WIDTH), width)

    def remote(src, dst, send, recv, **where):
        return pltpu.make_async_remote_copy(
            src_ref=src,
            dst_ref=dst,
            send_sem=send,
            recv_sem=recv,
            device_id=where,
            device_id_type=MESH,
        )

    barrier = pltpu.get_barrier_semaphore()
    greeted = [{"blk": peer}, {"groups": lax.rem(part + 1, parts)}]
    greeted += [{"seq": lax.rem(g + d, seq)} for d in range(1, seq)]
    greeted += [{"seq": lax.rem(g + d, seq), "blk": peer} for d in (1, seq - 1)]
    for device in greeted:
        pl.semaphore_signal(barrier, inc=1, device_id=device, device_id_type=MESH)

    tables = [
        pltpu.make_async_copy(lengths_hbm, lengths_ref, table_sem.at[0]),
        pltpu.make_async_copy(plan_hbm, plan_ref, table_sem.at[1]),
    ]
    for copy in tables:
        copy.start()
    pairs = ((k_ref, k_near), (v_ref, v_near))
    own_kv = [
        pltpu.make_async_copy(
            src.at[:, kv_columns(b, h)], dst.at[h, blk + b], local_sem.at[2 * h + i]
        )
        for h in range(groups_kv)
        for i, (src, dst) in enumerate(pairs)
    ]
    own_q = [
        pltpu.make_async_copy(
            q_ref.at[:, q_columns(b, c)], q_group.at[c, b], local_sem.at[2 * groups_kv + c]
        )
        for c in range(chunks)
    ]
    for copy in own_kv + own_q:
        copy.start()

    def kv_copy(h, i):
        src, dst = pairs[i]
        return remote(
            src.at[:, kv_columns(peer, h)],
            dst.at[h, blk + b],
            kv_send.at[h, i],
            kv_recv.at[h, i],
            blk=peer,
        )

    def near_copy(h, i, e):
        src, dst = pairs[i]
        if e == 0:
            source, origin, to = src.at[:, kv_columns(b, h)], b, b
        elif h < DIRECT_HEADS:
            source, origin, to = src.at[:, kv_columns(peer, h)], b, peer
        else:
            source, origin, to = dst.at[h, blk + peer], peer, b
        return remote(
            source,
            dst.at[h, origin],
            near_send.at[h, i, e],
            near_recv.at[h, i, e],
            seq=lax.rem(g + 1, seq),
            blk=to,
        )

    def q_copy(c):
        return remote(
            q_ref.at[:, q_columns(peer, c)],
            q_group.at[c, b],
            q_send.at[c],
            q_recv.at[c],
            blk=peer,
        )

    @pl.when(g == 0)
    def _():
        for h in range(groups_kv):
            for j in range(blk):
                k_near[h, j] = jnp.zeros(k_near.shape[2:], k_near.dtype)
                v_near[h, j] = jnp.zeros(v_near.shape[2:], v_near.dtype)

    pl.semaphore_wait(barrier, len(greeted))

    def word_copy():
        return remote(word, word_in, word_send, word_recv, groups=lax.rem(part + 1, parts))

    def send_kv(h):
        @pl.when(g < seq - 1)
        def _():
            for e in range(2 if h < DIRECT_HEADS else 1):
                for i in range(2):
                    near_copy(h, i, e).start()

        for i in range(2):
            kv_copy(h, i).start()

    def forward_kv(h):
        for i in range(2):
            kv_copy(h, i).wait_recv()

        if h >= DIRECT_HEADS:

            @pl.when(g < seq - 1)
            def _():
                for i in range(2):
                    near_copy(h, i, 1).start()

    send_kv(0)
    for c in range(min(QUERY_LEAD, chunks)):
        q_copy(c).start()

    for copy in tables:
        copy.wait()

    def has(group, owner):
        return (plan_ref[0, group] == owner) | (plan_ref[1, group] == owner)

    def pick(owner):
        return jnp.where(
            plan_ref[0, g] == owner,
            jnp.int32(0),
            jnp.where(plan_ref[1, g] == owner, jnp.int32(1), jnp.int32(blk)),
        )

    full_right = has(0, 2) & has(0, 3) & has(1, 2) & has(1, 3)
    full_left = has(3, 1) & has(3, 0) & has(2, 1) & has(2, 0)
    spilled = jnp.where(full_right | full_left, jnp.int32(1), jnp.int32(0))
    word[...] = jnp.full(word.shape, spilled, jnp.int32)

    for j in range(blk):
        first_row = g * group_len + j * BLOCK
        row_pos = first_row + lax.broadcasted_iota(jnp.int32, (BLOCK, 1), 0)
        end = jnp.int32(0)
        start = jnp.zeros((BLOCK, 1), jnp.int32)
        for n in range(lengths_ref.shape[0]):
            end = end + lengths_ref[n]
            start = jnp.where(row_pos >= end, end, start)
        key_pos = first_row - group_len + lax.broadcasted_iota(jnp.int32, (BLOCK, window), 1)
        allowed = (key_pos >= start) & (key_pos <= row_pos)
        bias[j] = jnp.where(allowed, 0.0, masked_score)
    block_out[blk] = jnp.zeros(block_out.shape[1:], block_out.dtype)

    forward_kv(0)
    word_copy().start()
    for copy in own_kv:
        copy.wait()

    sender = jnp.where(inner, 1, 0)

    def first_copy(c, which):
        return remote(
            first.at[c],
            land_first.at[c, which],
            first_send.at[c],
            first_recv.at[c, which],
            seq=far_inner,
        )

    def to_near(c):
        return remote(
            second.at[c], land_near.at[c], second_send.at[c], near_x_recv.at[c], seq=near_inner
        )

    def to_far(c):
        return remote(
            second.at[c], land_second.at[c], second_send.at[c], second_recv.at[c], seq=far_inner
        )

    def out_rows(group, half, c):
        slot = lax.rem(group, slots)
        return out_ref.at[
            pl.ds(pl.multiple_of(slot * BLOCK, BLOCK), BLOCK), q_columns(half, c)
        ]

    def home_copy(c, k):
        source = homeward.at[c] if k == 0 else relay.at[c, k - 1]
        group = (near_inner, far_inner, far_outer)[k]
        return remote(
            source,
            out_rows(group, b, c),
            home_send.at[c, k],
            x_recv.at[c, lax.rem(group, slots), b],
            seq=near_outer,
            blk=group // slots,
        )

    def extra_copy(c):
        return pltpu.make_async_copy(spare.at[c], extra_ref.at[c], extra_sem.at[c])

    def place(c, group, waiting):
        source = mine.at[c, group]
        holder = group // slots
        target = out_rows(group, b, c)

        @pl.when(holder == b)
        def _():
            copy = pltpu.make_async_copy(source, target, x_send.at[c, group])
            if waiting:
                copy.wait()
            else:
                copy.start()

        @pl.when(holder != b)
        def _():
            copy = remote(
                source,
                target,
                x_send.at[c, group],
                x_recv.at[c, lax.rem(group, slots), b],
                blk=holder,
            )
            if waiting:
                copy.wait_send()
            else:
                copy.start()

    to_inner, to_outer = pick(far_inner), pick(far_outer)
    both = (to_inner < blk) & (to_outer < blk)
    first_index = jnp.where(to_inner < blk, to_inner, to_outer)
    second_index = jnp.where(both, to_outer, jnp.int32(blk))
    near_index = jnp.where(both, to_outer, pick(near_inner))
    home_index, own_index = pick(near_outer), pick(g)

    near_both = has(near_outer, far_inner) & has(near_outer, far_outer)
    near_here = has(near_outer, g)
    a_here, a_on = has(far_outer, g), has(far_outer, near_outer)
    b_here, b_on = has(far_inner, g), has(far_inner, near_outer)
    nothing = jnp.zeros(block_out.shape[1:], block_out.dtype)

    def attend(c):
        own_q[c].wait()
        q_copy(c).wait_recv()
        if c + QUERY_LEAD < chunks:
            q_copy(c + QUERY_LEAD).start()
        kv_head = c * chunk_heads // heads_per_group
        if c * chunk_heads % heads_per_group == 0:

            @pl.when(g > 0)
            def _():
                for e in range(2):
                    for i in range(2):
                        near_copy(kv_head, i, e).wait_recv()

        for j in range(blk):
            query = q_group[c, j]
            rows = jnp.concatenate(
                [query[:, h * HEAD_WIDTH : (h + 1) * HEAD_WIDTH] for h in range(chunk_heads)], axis=0
            )
            keys = k_near[kv_head, j : j + blk + 1].reshape(window, HEAD_WIDTH)
            values = v_near[kv_head, j : j + blk + 1].reshape(window, HEAD_WIDTH)
            scores = lax.dot_general(
                rows, keys, (((1,), (1,)), ((), ())), preferred_element_type=jnp.float32
            )
            scores = scores.reshape(chunk_heads, BLOCK, window) * scale + bias[j][None]
            top = jnp.max(scores, axis=2, keepdims=True)
            weights = jnp.exp2(scores - top)
            total = jnp.sum(weights, axis=2, keepdims=True)
            mixed = jnp.dot(
                weights.astype(jnp.bfloat16).reshape(chunk_heads * BLOCK, window),
                values,
                preferred_element_type=jnp.float32,
            ).reshape(chunk_heads, BLOCK, HEAD_WIDTH)
            result = (mixed / total).astype(jnp.bfloat16)
            for h in range(chunk_heads):
                block_out[j, :, h * HEAD_WIDTH : (h + 1) * HEAD_WIDTH] = result[h]

    def dispatch(c):
        first[c] = block_out[first_index]
        first_copy(c, sender).start()

        @pl.when(outer)
        def _():
            second[c] = block_out[near_index]
            to_near(c).start()

        @pl.when(inner)
        def _():
            homeward[c] = block_out[home_index]
            home_copy(c, 0).start()
            spare[c] = block_out[second_index]
            extra_copy(c).start()

        mine[c, g] = block_out[own_index]
        place(c, g, False)

    def join(c):
        to_near(c).wait_recv()
        arrived = land_near[c]
        second[c] = jnp.where(near_both, arrived, spare[c])
        to_far(c).start()
        mine[c, near_outer] = jnp.where(near_here, arrived, nothing)
        place(c, near_outer, False)

    def spread(c):
        first_copy(c, 0).wait_recv()
        first_copy(c, 1).wait_recv()
        to_far(c).wait_recv()
        from_outer, from_inner, last = land_first[c, 0], land_first[c, 1], land_second[c]
        relay[c, 1] = jnp.where(a_on, jnp.where(a_here, last, from_outer), nothing)
        home_copy(c, 2).start()
        rest = jnp.where(a_here & a_on, nothing, last)
        relay[c, 0] = jnp.where(b_on, jnp.where(b_here, rest, from_inner), nothing)
        home_copy(c, 1).start()
        mine[c, far_outer] = jnp.where(a_here, from_outer, nothing)
        place(c, far_outer, False)
        mine[c, far_inner] = jnp.where(b_here, from_inner, nothing)
        place(c, far_inner, False)

    def landed(c, s, half):
        remote(
            mine.at[c, 0],
            out_rows(b * slots + s, half, c),
            x_send.at[c, 0],
            x_recv.at[c, s, half],
            blk=peer,
        ).wait_recv()

    for t in range(chunks + max(JOIN_LAG, SPREAD_LAG)):
        if t < chunks:
            attend(t)
            dispatch(t)
            for h in range(1, groups_kv):
                start = h * heads_per_group // chunk_heads
                if t == start - KV_LEAD:
                    send_kv(h)
                if t == start - KV_LEAD + 1:
                    forward_kv(h)

        @pl.when(inner)
        def _():
            if 0 <= t - JOIN_LAG < chunks:
                join(t - JOIN_LAG)
            if 0 <= t - SPREAD_LAG < chunks:
                spread(t - SPREAD_LAG)

    word_copy().wait()
    flag_ref[0, 0] = jnp.maximum(spilled, jnp.max(word_in[...]))

    for c in range(chunks):
        for s in range(slots):
            landed(c, s, peer)

            @pl.when(outer & (b * slots + s != g))
            def _():
                landed(c, s, b)

        place(c, g, True)
        q_copy(c).wait_send()
        first_copy(c, sender).wait_send()

    @pl.when(outer)
    def _():
        for c in range(chunks):
            to_near(c).wait_send()

    @pl.when(inner)
    def _():
        for c in range(chunks):
            to_far(c).wait_send()
            extra_copy(c).wait()
            for k in range(3):
                home_copy(c, k).wait_send()
            for group in (near_outer, far_inner, far_outer):
                place(c, group, True)

    for h in range(groups_kv):
        for i in range(2):
            kv_copy(h, i).wait_send()

    @pl.when(g < seq - 1)
    def _():
        for h in range(groups_kv):
            for e in range(2):
                for i in range(2):
                    near_copy(h, i, e).wait_send()


def spill_kernel(dims, extra_ref, got_ref, send, recv):
    seq, blk, chunks, width, slots = dims
    g = lax.axis_index("seq")
    b = lax.axis_index("blk")
    inner = (g == 1) | (g == 2)
    mate = lax.rem(g + 2, seq)
    barrier = pltpu.get_barrier_semaphore()
    for e in range(blk):
        pl.semaphore_signal(
            barrier, inc=1, device_id={"seq": mate, "blk": e}, device_id_type=MESH
        )
    pl.semaphore_wait(barrier, blk)

    def spill(c, half, holder):
        return pltpu.make_async_remote_copy(
            src_ref=extra_ref.at[c],
            dst_ref=got_ref.at[
                :, pl.ds(pl.multiple_of((half * chunks + c) * width, width), width)
            ],
            send_sem=send.at[c],
            recv_sem=recv.at[c, half],
            device_id={"seq": mate, "blk": holder},
            device_id_type=MESH,
        )

    @pl.when(inner)
    def _():
        for c in range(chunks):
            spill(c, b, g // slots).start()
        for c in range(chunks):
            spill(c, b, g // slots).wait_send()

    @pl.when(jnp.logical_not(inner) & (b == mate // slots))
    def _():
        for c in range(chunks):
            for half in range(blk):
                spill(c, half, b).wait_recv()


def finish(pieces, src_ref, dst_ref, sem):
    rows = src_ref.shape[0] // pieces
    copies = [
        pltpu.make_async_copy(
            src_ref.at[pl.ds(n * rows, rows)], dst_ref.at[pl.ds(n * rows, rows)], sem.at[n]
        )
        for n in range(pieces)
    ]
    for copy in copies:
        copy.start()
    for copy in copies:
        copy.wait()


def finish_spilled(slots, plan_ref, src_ref, got_ref, dst_ref, sem):
    owner = lax.axis_index("seq")
    b = lax.axis_index("blk")

    def has(group, wanted):
        return (plan_ref[0, group] == wanted) | (plan_ref[1, group] == wanted)

    full_right = has(0, 2) & has(0, 3) & has(1, 2) & has(1, 3)
    full_left = has(3, 1) & has(3, 0) & has(2, 1) & has(2, 0)
    for s in range(slots):
        group = b * slots + s
        rows = pl.ds(s * BLOCK, BLOCK)
        spilled = ((group == 1) & (owner == 3) & full_right) | (
            (group == 2) & (owner == 0) & full_left
        )

        @pl.when(spilled)
        def _():
            copy = pltpu.make_async_copy(got_ref, dst_ref.at[rows], sem.at[s])
            copy.start()
            copy.wait()

        @pl.when(jnp.logical_not(spilled))
        def _():
            copy = pltpu.make_async_copy(src_ref.at[rows], dst_ref.at[rows], sem.at[s])
            copy.start()
            copy.wait()


def quad(queries, rotated_keys, head_value_rows, doc_lengths, owner_plan):
    blk = lax.axis_size("blk")
    seq = lax.axis_size("seq")
    parts = lax.axis_size("groups")
    heads_dev = queries.shape[1] // HEAD_WIDTH // blk
    heads_per_group = QUERY_HEADS // KEY_HEADS
    groups_kv = heads_dev // heads_per_group
    chunk_heads = CHUNK_HEADS
    chunks = heads_dev // chunk_heads
    slots = seq // blk
    width = chunk_heads * HEAD_WIDTH
    dims = (seq, blk, heads_dev, groups_kv, heads_per_group, chunk_heads, slots, parts)
    bf16 = jnp.bfloat16
    dma = pltpu.SemaphoreType.DMA
    hbm = pl.BlockSpec(memory_space=pltpu.HBM)
    plan = owner_plan.T
    out_shape = jax.ShapeDtypeStruct((slots * BLOCK, queries.shape[1]), bf16)

    def unit(*lead):
        return pltpu.VMEM(lead + (BLOCK, width), bf16)

    placed, extra, flag = pl.pallas_call(
        functools.partial(quad_kernel, dims),
        out_shape=(
            out_shape,
            jax.ShapeDtypeStruct((chunks, BLOCK, width), bf16),
            jax.ShapeDtypeStruct((1, 1), jnp.int32),
        ),
        in_specs=[hbm] * 5,
        out_specs=(
            pl.BlockSpec(memory_space=pl.ANY),
            pl.BlockSpec(memory_space=pl.ANY),
            pl.BlockSpec(memory_space=pltpu.SMEM),
        ),
        scratch_shapes=[
            unit(chunks, blk),
            pltpu.VMEM((groups_kv, 2 * blk, BLOCK, HEAD_WIDTH), bf16),
            pltpu.VMEM((groups_kv, 2 * blk, BLOCK, HEAD_WIDTH), bf16),
            pltpu.VMEM((blk, BLOCK, (blk + 1) * BLOCK), jnp.float32),
            unit(blk + 1),
            unit(chunks),
            unit(chunks),
            unit(chunks),
            unit(chunks, 2),
            unit(chunks),
            unit(chunks, 2),
            unit(chunks),
            unit(chunks),
            unit(chunks, seq),
            pltpu.VMEM((8, 128), jnp.int32),
            pltpu.VMEM((8, 128), jnp.int32),
            pltpu.SMEM(doc_lengths.shape, jnp.int32),
            pltpu.SMEM(plan.shape, jnp.int32),
            dma((2,)),
            dma((2 * groups_kv + chunks,)),
            dma((chunks,)),
            dma((chunks,)),
            dma((groups_kv, 2)),
            dma((groups_kv, 2)),
            dma((groups_kv, 2, 2)),
            dma((groups_kv, 2, 2)),
            dma((chunks,)),
            dma((chunks, 2)),
            dma((chunks,)),
            dma((chunks,)),
            dma((chunks,)),
            dma((chunks, 3)),
            dma((chunks, seq)),
            dma((chunks, slots, blk)),
            dma((chunks,)),
            dma,
            dma,
        ],
        compiler_params=pltpu.CompilerParams(
            collective_id=0, has_side_effects=True, vmem_limit_bytes=VMEM_MAIN
        ),
    )(doc_lengths, plan, queries, rotated_keys, head_value_rows)

    def plain(placed, extra):
        return pl.pallas_call(
            functools.partial(finish, PIECES),
            out_shape=out_shape,
            in_specs=[pl.BlockSpec(memory_space=pl.ANY)],
            out_specs=hbm,
            scratch_shapes=[dma((PIECES,))],
            compiler_params=pltpu.CompilerParams(vmem_limit_bytes=VMEM_REST),
        )(placed)

    def spilled(placed, extra):
        got = pl.pallas_call(
            functools.partial(spill_kernel, (seq, blk, chunks, width, slots)),
            out_shape=jax.ShapeDtypeStruct((BLOCK, queries.shape[1]), bf16),
            in_specs=[pl.BlockSpec(memory_space=pl.ANY)],
            out_specs=pl.BlockSpec(memory_space=pl.ANY),
            scratch_shapes=[dma((chunks,)), dma((chunks, blk))],
            compiler_params=pltpu.CompilerParams(
                collective_id=1, has_side_effects=True, vmem_limit_bytes=VMEM_REST
            ),
        )(extra)
        return pl.pallas_call(
            functools.partial(finish_spilled, slots),
            out_shape=out_shape,
            in_specs=[pl.BlockSpec(memory_space=pltpu.SMEM)]
            + [pl.BlockSpec(memory_space=pl.ANY)] * 2,
            out_specs=hbm,
            scratch_shapes=[dma((slots,))],
            compiler_params=pltpu.CompilerParams(vmem_limit_bytes=VMEM_REST),
        )(plan, placed, got)

    return lax.cond(flag[0, 0] > 0, spilled, plain, placed, extra)


def per_device(queries, rotated_keys, head_value_rows, doc_lengths, owner_plan):
    blk = lax.axis_size("blk")
    seq = lax.axis_size("seq")
    heads_dev = queries.shape[1] // HEAD_WIDTH // blk
    heads_per_group = QUERY_HEADS // KEY_HEADS
    groups_kv = max(1, heads_dev // heads_per_group)
    chunk_heads = min(CHUNK_HEADS, heads_dev, heads_per_group)
    chunks = heads_dev // chunk_heads
    slots = seq // blk
    if (seq, blk, lax.axis_size("groups")) == (4, 2, 2) and heads_dev % heads_per_group == 0:
        return quad(queries, rotated_keys, head_value_rows, doc_lengths, owner_plan)
    width = chunk_heads * HEAD_WIDTH
    dims = (seq, blk, heads_dev, groups_kv, heads_per_group, chunk_heads, slots)
    bf16 = jnp.bfloat16
    dma = pltpu.SemaphoreType.DMA
    placed = pl.pallas_call(
        functools.partial(kernel, dims),
        out_shape=jax.ShapeDtypeStruct((slots * BLOCK, queries.shape[1]), bf16),
        in_specs=[pl.BlockSpec(memory_space=pltpu.SMEM)] * 2
        + [pl.BlockSpec(memory_space=pl.ANY)] * 3,
        out_specs=pl.BlockSpec(memory_space=pl.ANY),
        scratch_shapes=[
            pltpu.VMEM((chunks, blk, BLOCK, width), bf16),
            pltpu.VMEM((groups_kv, 2 * blk, BLOCK, HEAD_WIDTH), bf16),
            pltpu.VMEM((groups_kv, 2 * blk, BLOCK, HEAD_WIDTH), bf16),
            pltpu.VMEM((blk, BLOCK, (blk + 1) * BLOCK), jnp.float32),
            pltpu.VMEM((blk + 1, BLOCK, width), bf16),
            pltpu.VMEM((chunks, seq, BLOCK, width), bf16),
            pltpu.VMEM((chunks, seq - 1, BLOCK, width), bf16),
            dma((2 * groups_kv + chunks,)),
            dma((chunks, blk - 1)),
            dma((chunks, blk - 1)),
            dma((groups_kv, 2, blk - 1)),
            dma((groups_kv, 2, blk - 1)),
            dma((groups_kv, 2, blk)),
            dma((groups_kv, 2, blk)),
            dma((chunks, seq - 1)),
            dma((chunks, seq - 1)),
            dma((chunks, seq)),
            dma((chunks, slots, blk)),
        ],
        compiler_params=pltpu.CompilerParams(collective_id=0, has_side_effects=True),
    )(doc_lengths, owner_plan.T, queries, rotated_keys, head_value_rows)
    pieces = PIECES
    return pl.pallas_call(
        functools.partial(settle, pieces),
        out_shape=jax.ShapeDtypeStruct(placed.shape, bf16),
        in_specs=[pl.BlockSpec(memory_space=pl.ANY)],
        out_specs=pl.BlockSpec(memory_space=pl.ANY),
        scratch_shapes=[
            pltpu.VMEM((pieces, placed.shape[0] // pieces, placed.shape[1]), bf16),
            dma((pieces,)),
            dma((pieces,)),
        ],
    )(placed)


def solution(mesh):
    in_specs = (
        P(("groups", "seq", "blk"), "tp"),
        P(("groups", "seq", "blk"), "tp"),
        P(("groups", "seq", "blk"), "tp"),
        P("groups"),
        P("groups", None),
    )
    out_specs = P(("groups", "seq", "blk"), "tp")
    return jax.shard_map(
        per_device, mesh=mesh, in_specs=in_specs, out_specs=out_specs, check_vma=False
    )
```

```python
import functools
import math

import jax
import jax.numpy as jnp
from jax import lax
from jax.experimental import pallas as pl
from jax.experimental.pallas import tpu as pltpu
from jax.sharding import PartitionSpec as P

QUERY_HEADS = 64
KEY_HEADS = 8
HEAD_WIDTH = 128
BLOCK = 128
CHUNK_HEADS = 2
HEAD_SPLIT = (2,)
TAIL_SPLIT = (2,)
PIECES = 8

MESH = pl.DeviceIdType.MESH
masked_score = -1e30
JOIN_LAG = 1
LAGS = (3,3)
KV_EARLY = 2
QUERY_SECOND = 2
DIRECT_HEADS = 0
VMEM_MAIN = 58 * 2**20
QUERY_FIRST = 1
QUERY_LEAD = 2
KV_LEAD = 4
VMEM_REST = 4 * 2**20


def kernel(
    dims,
    lengths_ref,
    plan_ref,
    q_ref,
    k_ref,
    v_ref,
    out_ref,
    q_group,
    k_near,
    v_near,
    bias,
    block_out,
    message,
    landed,
    local_sem,
    q_send,
    q_recv,
    kv_send,
    kv_recv,
    near_send,
    near_recv,
    z_send,
    z_recv,
    x_send,
    x_recv,
):
    seq, blk, heads_dev, groups_kv, heads_per_group, chunk_heads, slots = dims
    g = lax.axis_index("seq")
    b = lax.axis_index("blk")
    chunks = heads_dev // chunk_heads
    width = chunk_heads * HEAD_WIDTH
    columns_dev = heads_dev * HEAD_WIDTH
    window = (blk + 1) * BLOCK
    group_len = blk * BLOCK
    scale = 1.0 / math.sqrt(HEAD_WIDTH)

    def kv_columns(owner, h):
        first = owner * heads_dev // heads_per_group + h
        return pl.ds(pl.multiple_of(first * HEAD_WIDTH, HEAD_WIDTH), HEAD_WIDTH)

    def q_columns(owner, c):
        return pl.ds(pl.multiple_of(owner * columns_dev + c * width, HEAD_WIDTH), width)

    barrier = pltpu.get_barrier_semaphore()
    for e in range(1, blk):
        pl.semaphore_signal(
            barrier, inc=1, device_id={"blk": lax.rem(b + e, blk)}, device_id_type=MESH
        )
    for d in range(1, seq):
        pl.semaphore_signal(
            barrier, inc=1, device_id={"seq": lax.rem(g + d, seq)}, device_id_type=MESH
        )

    pairs = ((k_ref, k_near), (v_ref, v_near))
    own_kv = [
        pltpu.make_async_copy(
            src.at[:, kv_columns(b, h)], dst.at[h, blk + b], local_sem.at[2 * h + i]
        )
        for h in range(groups_kv)
        for i, (src, dst) in enumerate(pairs)
    ]
    own_q = [
        pltpu.make_async_copy(
            q_ref.at[:, q_columns(b, c)], q_group.at[c, b], local_sem.at[2 * groups_kv + c]
        )
        for c in range(chunks)
    ]
    for copy in own_kv + own_q:
        copy.start()

    def kv_copy(h, i, e):
        src, dst = pairs[i]
        peer = lax.rem(b + e, blk)
        return pltpu.make_async_remote_copy(
            src_ref=src.at[:, kv_columns(peer, h)],
            dst_ref=dst.at[h, blk + b],
            send_sem=kv_send.at[h, i, e - 1],
            recv_sem=kv_recv.at[h, i, e - 1],
            device_id={"blk": peer},
            device_id_type=MESH,
        )

    def near_copy(h, i, e):
        src, dst = pairs[i]
        origin = lax.rem(b - e + blk, blk)
        if e == 0:
            source = src.at[:, kv_columns(b, h)]
        else:
            source = dst.at[h, blk + origin]
        return pltpu.make_async_remote_copy(
            src_ref=source,
            dst_ref=dst.at[h, origin],
            send_sem=near_send.at[h, i, e],
            recv_sem=near_recv.at[h, i, e],
            device_id={"seq": lax.rem(g + 1, seq)},
            device_id_type=MESH,
        )

    def q_copy(c, e):
        peer = lax.rem(b + e, blk)
        return pltpu.make_async_remote_copy(
            src_ref=q_ref.at[:, q_columns(peer, c)],
            dst_ref=q_group.at[c, b],
            send_sem=q_send.at[c, e - 1],
            recv_sem=q_recv.at[c, e - 1],
            device_id={"blk": peer},
            device_id_type=MESH,
        )

    for j in range(blk):
        first_row = g * group_len + j * BLOCK
        row_pos = first_row + lax.broadcasted_iota(jnp.int32, (BLOCK, 1), 0)
        end = jnp.int32(0)
        start = jnp.zeros((BLOCK, 1), jnp.int32)
        for n in range(lengths_ref.shape[0]):
            end = end + lengths_ref[n]
            start = jnp.where(row_pos >= end, end, start)
        key_pos = first_row - group_len + lax.broadcasted_iota(jnp.int32, (BLOCK, window), 1)
        allowed = (key_pos >= start) & (key_pos <= row_pos)
        bias[j] = jnp.where(allowed, 0.0, masked_score)
    block_out[blk] = jnp.zeros(block_out.shape[1:], block_out.dtype)

    @pl.when(g == 0)
    def _():
        for h in range(groups_kv):
            for j in range(blk):
                k_near[h, j] = jnp.zeros(k_near.shape[2:], k_near.dtype)
                v_near[h, j] = jnp.zeros(v_near.shape[2:], v_near.dtype)

    pl.semaphore_wait(barrier, blk - 1 + seq - 1)

    def send_kv(h):
        for e in range(1, blk):
            for i in range(2):
                kv_copy(h, i, e).start()

    def send_q(c):
        for e in range(1, blk):
            q_copy(c, e).start()

    def forward_kv(h):
        for e in range(1, blk):
            for i in range(2):
                kv_copy(h, i, e).wait_recv()

        @pl.when(g < seq - 1)
        def _():
            for e in range(1, blk):
                for i in range(2):
                    near_copy(h, i, e).start()

    def wait_near(h):
        @pl.when(g > 0)
        def _():
            for e in range(blk):
                for i in range(2):
                    near_copy(h, i, e).wait_recv()

    send_kv(0)

    @pl.when(g < seq - 1)
    def _():
        for h in range(groups_kv):
            for i in range(2):
                near_copy(h, i, 0).start()

    send_q(0)
    for h in range(1, groups_kv):
        send_kv(h)
    for c in range(1, chunks):
        send_q(c)

    forward_kv(0)
    for copy in own_kv:
        copy.wait()

    half = seq // 2
    side, place_in = g // half, lax.rem(g, half)

    def target(k):
        if k < half:
            return side * half + lax.rem(place_in + k, half)
        return (1 - side) * half + lax.rem(place_in + k - half, half)

    def origin_of(k):
        if k < half:
            return side * half + lax.rem(place_in - k + half, half)
        return (1 - side) * half + lax.rem(place_in - (k - half) + half, half)

    picked = []
    for d in range(seq):
        owner = target(d)
        index = jnp.int32(blk)
        for j in range(blk):
            index = jnp.where(plan_ref[j, g] == owner, jnp.int32(j), index)
        picked.append(index)

    def z_copy(c, d):
        return pltpu.make_async_remote_copy(
            src_ref=message.at[c, d],
            dst_ref=landed.at[c, d - 1],
            send_sem=z_send.at[c, d - 1],
            recv_sem=z_recv.at[c, d - 1],
            device_id={"seq": target(d)},
            device_id_type=MESH,
        )

    near, far = list(range(1, half)), list(range(half, seq))
    sends = [[] for _ in range(chunks)]
    for c in range(chunks):
        if c > 0:
            sends[c] += [(c, k) for k in near]
        if c in (0, chunks - 1):
            sends[c] += [(m, k) for m in range(max(c - 1, min(c, 1)), c + 1) for k in far]
        elif c > 1:
            sends[c] += [(c - 1, k) for k in far]
        if c == 0:
            sends[c] += [(c, k) for k in near]
    arrivals = [message for row in sends for message in row]
    for c in range(chunks):
        own_q[c].wait()
        for e in range(1, blk):
            q_copy(c, e).wait_recv()
        kv_head = c * chunk_heads // heads_per_group
        if c * chunk_heads % heads_per_group == 0 or c == 0:
            wait_near(kv_head)
        for j in range(blk):
            query = q_group[c, j]
            rows = jnp.concatenate(
                [query[:, h * HEAD_WIDTH : (h + 1) * HEAD_WIDTH] for h in range(chunk_heads)], axis=0
            )
            keys = k_near[kv_head, j : j + blk + 1].reshape(window, HEAD_WIDTH)
            values = v_near[kv_head, j : j + blk + 1].reshape(window, HEAD_WIDTH)
            scores = lax.dot_general(
                rows, keys, (((1,), (1,)), ((), ())), preferred_element_type=jnp.float32
            )
            scores = scores.reshape(chunk_heads, BLOCK, window) * scale + bias[j][None]
            top = jnp.max(scores, axis=2, keepdims=True)
            weights = jnp.exp(scores - top)
            total = jnp.sum(weights, axis=2, keepdims=True)
            mixed = jnp.dot(
                weights.astype(jnp.bfloat16).reshape(chunk_heads * BLOCK, window),
                values,
                preferred_element_type=jnp.float32,
            ).reshape(chunk_heads, BLOCK, HEAD_WIDTH)
            result = (mixed / total).astype(jnp.bfloat16)
            for h in range(chunk_heads):
                block_out[j, :, h * HEAD_WIDTH : (h + 1) * HEAD_WIDTH] = result[h]
        for d in range(seq):
            message[c, d] = block_out[picked[d]]
        for m, k in sends[c]:
            z_copy(m, k).start()
        if c == 0:
            for h in range(1, groups_kv):
                forward_kv(h)

    def place(c, d, waiting):
        origin = origin_of(d)
        source = message.at[c, 0] if d == 0 else landed.at[c, d - 1]
        holder = origin // slots
        slot = lax.rem(origin, slots)
        target = out_ref.at[
            pl.ds(pl.multiple_of(slot * BLOCK, BLOCK), BLOCK), q_columns(b, c)
        ]
        hop = lax.rem(holder - b + blk, blk)

        @pl.when(holder == b)
        def _():
            copy = pltpu.make_async_copy(source, target, x_send.at[c, d])
            if waiting:
                copy.wait()
            else:
                copy.start()

        @pl.when(holder != b)
        def _():
            copy = pltpu.make_async_remote_copy(
                src_ref=source,
                dst_ref=target,
                send_sem=x_send.at[c, d],
                recv_sem=x_recv.at[c, slot, lax.rem(hop - 1 + blk, blk)],
                device_id={"blk": holder},
                device_id_type=MESH,
            )
            if waiting:
                copy.wait_send()
            else:
                copy.start()

    for c in range(chunks):
        place(c, 0, False)
    for c, d in arrivals:
        z_copy(c, d).wait_recv()
        place(c, d, False)

    for c in range(chunks):
        for s in range(slots):
            for e in range(1, blk):
                sender = lax.rem(b - e + blk, blk)
                pltpu.make_async_remote_copy(
                    src_ref=message.at[c, 0],
                    dst_ref=out_ref.at[s * BLOCK : (s + 1) * BLOCK, q_columns(sender, c)],
                    send_sem=x_send.at[c, 0],
                    recv_sem=x_recv.at[c, s, e - 1],
                    device_id={"blk": sender},
                    device_id_type=MESH,
                ).wait_recv()
        for d in range(seq):
            place(c, d, True)
            if d > 0:
                z_copy(c, d).wait_send()
        for e in range(1, blk):
            q_copy(c, e).wait_send()
    for h in range(groups_kv):
        for i in range(2):
            for e in range(1, blk):
                kv_copy(h, i, e).wait_send()

    @pl.when(g < seq - 1)
    def _():
        for h in range(groups_kv):
            for e in range(blk):
                for i in range(2):
                    near_copy(h, i, e).wait_send()


def settle(pieces, src_ref, dst_ref, held, in_sem, out_sem):
    rows = src_ref.shape[0] // pieces
    taken = [
        pltpu.make_async_copy(src_ref.at[pl.ds(n * rows, rows)], held.at[n], in_sem.at[n])
        for n in range(pieces)
    ]
    put = [
        pltpu.make_async_copy(held.at[n], dst_ref.at[pl.ds(n * rows, rows)], out_sem.at[n])
        for n in range(pieces)
    ]
    for copy in taken:
        copy.start()
    for n in range(pieces):
        taken[n].wait()
        put[n].start()
    for copy in put:
        copy.wait()


def quad_kernel(
    dims,
    lengths_hbm,
    plan_hbm,
    q_ref,
    k_ref,
    v_ref,
    out_ref,
    extra_ref,
    flag_ref,
    q_group,
    k_near,
    v_near,
    bias,
    block_out,
    first,
    second,
    homeward,
    relay,
    spare,
    land_first,
    land_near,
    land_second,
    mine,
    word,
    word_in,
    lengths_ref,
    plan_ref,
    table_sem,
    local_sem,
    q_send,
    q_recv,
    kv_send,
    kv_recv,
    near_send,
    near_recv,
    first_send,
    first_recv,
    second_send,
    near_x_recv,
    second_recv,
    home_send,
    x_send,
    x_recv,
    extra_sem,
    word_send,
    word_recv,
    credit,
):
    seq, blk, heads_dev, groups_kv, heads_per_group, pieces, slots, parts = dims
    g = lax.axis_index("seq")
    b = lax.axis_index("blk")
    part = lax.axis_index("groups")
    tp = lax.axis_index("tp")
    chunks = len(pieces)
    columns_dev = heads_dev * HEAD_WIDTH
    window = (blk + 1) * BLOCK
    group_len = blk * BLOCK
    scale = math.log2(math.e) / math.sqrt(HEAD_WIDTH)

    left = g < 2
    inner = (g == 1) | (g == 2)
    outer = jnp.logical_not(inner)
    far_inner = jnp.where(left, 2, 1)
    far_outer = jnp.where(left, 3, 0)
    near_inner = jnp.where(left, 1, 2)
    near_outer = jnp.where(left, 0, 3)
    peer = 1 - b

    def kv_columns(owner, h):
        start = owner * heads_dev // heads_per_group + h
        return pl.ds(pl.multiple_of(start * HEAD_WIDTH, HEAD_WIDTH), HEAD_WIDTH)

    def q_columns(owner, c):
        start, heads = pieces[c]
        return pl.ds(
            pl.multiple_of(owner * columns_dev + start * HEAD_WIDTH, HEAD_WIDTH),
            heads * HEAD_WIDTH,
        )

    def unit(ref, c, *index):
        return ref.at[(c,) + index + (slice(None), slice(0, pieces[c][1] * HEAD_WIDTH))]

    def chosen(c, index):
        return block_out[index, :, : pieces[c][1] * HEAD_WIDTH]

    def remote(src, dst, send, recv, **where):
        return pltpu.make_async_remote_copy(
            src_ref=src,
            dst_ref=dst,
            send_sem=send,
            recv_sem=recv,
            device_id=where,
            device_id_type=MESH,
        )

    barrier = pltpu.get_barrier_semaphore()
    everyone = [
        {"blk": peer},
        {"groups": lax.rem(part + 1, parts)},
        {"seq": lax.rem(g + 2, seq)},
        {"seq": jnp.where(inner, near_outer, near_inner)},
        {"seq": jnp.where(inner, near_outer, near_inner), "blk": peer},
    ]
    across = [{"seq": far_inner}, {"seq": far_inner, "blk": peer}]

    def greet(devices):
        for device in devices:
            pl.semaphore_signal(barrier, inc=1, device_id=device, device_id_type=MESH)

    greet(everyone)

    @pl.when(inner)
    def _():
        greet(across)

    tables = [
        pltpu.make_async_copy(lengths_hbm, lengths_ref, table_sem.at[0]),
        pltpu.make_async_copy(plan_hbm, plan_ref, table_sem.at[1]),
    ]
    for copy in tables:
        copy.start()
    pairs = ((k_ref, k_near), (v_ref, v_near))
    own_kv = [
        pltpu.make_async_copy(
            src.at[:, kv_columns(b, h)], dst.at[h, blk + b], local_sem.at[2 * h + i]
        )
        for h in range(groups_kv)
        for i, (src, dst) in enumerate(pairs)
    ]
    own_q = [
        pltpu.make_async_copy(
            q_ref.at[:, q_columns(b, c)], unit(q_group, c, b), local_sem.at[2 * groups_kv + c]
        )
        for c in range(chunks)
    ]
    for copy in own_kv + own_q:
        copy.start()

    def kv_copy(h, i):
        src, dst = pairs[i]
        return remote(
            src.at[:, kv_columns(peer, h)],
            dst.at[h, blk + b],
            kv_send.at[h, i],
            kv_recv.at[h, i],
            blk=peer,
        )

    def near_copy(h, i, e):
        src, dst = pairs[i]
        if e == 0:
            source, origin, to = src.at[:, kv_columns(b, h)], b, b
        elif h < DIRECT_HEADS:
            source, origin, to = src.at[:, kv_columns(peer, h)], b, peer
        else:
            source, origin, to = dst.at[h, blk + peer], peer, b
        return remote(
            source,
            dst.at[h, origin],
            near_send.at[h, i, e],
            near_recv.at[h, i, e],
            seq=lax.rem(g + 1, seq),
            blk=to,
        )

    def q_copy(c):
        return remote(
            q_ref.at[:, q_columns(peer, c)],
            unit(q_group, c, b),
            q_send.at[c],
            q_recv.at[c],
            blk=peer,
        )

    @pl.when(g == 0)
    def _():
        for h in range(groups_kv):
            for j in range(blk):
                k_near[h, j] = jnp.zeros(k_near.shape[2:], k_near.dtype)
                v_near[h, j] = jnp.zeros(v_near.shape[2:], v_near.dtype)

    @pl.when(inner)
    def _():
        pl.semaphore_wait(barrier, len(everyone) + len(across))

    @pl.when(outer)
    def _():
        pl.semaphore_wait(barrier, len(everyone))


    def word_copy():
        return remote(word, word_in, word_send, word_recv, groups=lax.rem(part + 1, parts))

    def send_kv(h):
        @pl.when(g < seq - 1)
        def _():
            for e in range(2 if h < DIRECT_HEADS else 1):
                for i in range(2):
                    near_copy(h, i, e).start()

        for i in range(2):
            kv_copy(h, i).start()

    def forward_kv(h):
        for i in range(2):
            kv_copy(h, i).wait_recv()

        if h >= DIRECT_HEADS:

            @pl.when(g < seq - 1)
            def _():
                for i in range(2):
                    near_copy(h, i, 1).start()

    send_kv(0)
    for c in range(QUERY_FIRST):
        q_copy(c).start()

    for copy in tables:
        copy.wait()

    def has(group, owner):
        return (plan_ref[0, group] == owner) | (plan_ref[1, group] == owner)

    def pick(owner):
        return jnp.where(
            plan_ref[0, g] == owner,
            jnp.int32(0),
            jnp.where(plan_ref[1, g] == owner, jnp.int32(1), jnp.int32(blk)),
        )

    full_right = has(0, 2) & has(0, 3) & has(1, 2) & has(1, 3)
    full_left = has(3, 1) & has(3, 0) & has(2, 1) & has(2, 0)
    spilled = jnp.where(full_right | full_left, jnp.int32(1), jnp.int32(0))
    word[...] = jnp.full(word.shape, spilled, jnp.int32)

    for j in range(blk):
        first_row = g * group_len + j * BLOCK
        row_pos = first_row + lax.broadcasted_iota(jnp.int32, (BLOCK, 1), 0)
        end = jnp.int32(0)
        start = jnp.zeros((BLOCK, 1), jnp.int32)
        for n in range(lengths_ref.shape[0]):
            end = end + lengths_ref[n]
            start = jnp.where(row_pos >= end, end, start)
        key_pos = first_row - group_len + lax.broadcasted_iota(jnp.int32, (BLOCK, window), 1)
        allowed = (key_pos >= start) & (key_pos <= row_pos)
        bias[j] = jnp.where(allowed, 0.0, masked_score)
    block_out[blk] = jnp.zeros(block_out.shape[1:], block_out.dtype)

    forward_kv(0)
    for c in range(QUERY_FIRST, QUERY_SECOND):
        q_copy(c).start()
    if KV_EARLY:
        send_kv(1)
    word_copy().start()
    for copy in own_kv:
        copy.wait()

    sender = jnp.where(inner, 1, 0)

    def first_copy(c, which):
        return remote(
            unit(first, c),
            unit(land_first, c, which),
            first_send.at[c],
            first_recv.at[c, which],
            seq=far_inner,
        )

    def to_near(c):
        return remote(
            unit(second, c), unit(land_near, c), second_send.at[c], near_x_recv.at[c], seq=near_inner
        )

    def to_far(c):
        return remote(
            unit(second, c), unit(land_second, c), second_send.at[c], second_recv.at[c], seq=far_inner
        )

    def out_rows(group, half, c):
        slot = lax.rem(group, slots)
        return out_ref.at[
            pl.ds(pl.multiple_of(slot * BLOCK, BLOCK), BLOCK), q_columns(half, c)
        ]

    def home_copy(c, k):
        source = unit(homeward, c) if k == 0 else unit(relay, c, k - 1)
        group = (near_inner, far_inner, far_outer)[k]
        return remote(
            source,
            out_rows(group, b, c),
            home_send.at[c, k],
            x_recv.at[c, lax.rem(group, slots), b],
            seq=near_outer,
            blk=group // slots,
        )

    def extra_copy(c):
        return pltpu.make_async_copy(unit(spare, c), unit(extra_ref, c), extra_sem.at[c])

    def place(c, group, waiting):
        source = unit(mine, c, group)
        holder = group // slots
        target = out_rows(group, b, c)

        @pl.when(holder == b)
        def _():
            copy = pltpu.make_async_copy(source, target, x_send.at[c, group])
            if waiting:
                copy.wait()
            else:
                copy.start()

        @pl.when(holder != b)
        def _():
            copy = remote(
                source,
                target,
                x_send.at[c, group],
                x_recv.at[c, lax.rem(group, slots), b],
                blk=holder,
            )
            if waiting:
                copy.wait_send()
            else:
                copy.start()

    to_inner, to_outer = pick(far_inner), pick(far_outer)
    both = (to_inner < blk) & (to_outer < blk)
    first_index = jnp.where(to_inner < blk, to_inner, to_outer)
    second_index = jnp.where(both, to_outer, jnp.int32(blk))
    near_index = jnp.where(both, to_outer, pick(near_inner))
    home_index, own_index = pick(near_outer), pick(g)

    near_both = has(near_outer, far_inner) & has(near_outer, far_outer)
    near_here = has(near_outer, g)
    a_here, a_on = has(far_outer, g), has(far_outer, near_outer)
    b_here, b_on = has(far_inner, g), has(far_inner, near_outer)

    def attend(c):
        own_q[c].wait()
        q_copy(c).wait_recv()
        for m in range(max(QUERY_SECOND, c and c + QUERY_LEAD), min(c + QUERY_LEAD + 1, chunks)):
            q_copy(m).start()
        begin, chunk_heads = pieces[c]
        kv_head = begin // heads_per_group
        if begin % heads_per_group == 0:

            @pl.when(g > 0)
            def _():
                for e in range(2):
                    for i in range(2):
                        near_copy(kv_head, i, e).wait_recv()

        for j in range(blk):
            query = unit(q_group, c, j)[...]
            rows = jnp.concatenate(
                [query[:, h * HEAD_WIDTH : (h + 1) * HEAD_WIDTH] for h in range(chunk_heads)], axis=0
            )
            keys = k_near[kv_head, j : j + blk + 1].reshape(window, HEAD_WIDTH)
            values = v_near[kv_head, j : j + blk + 1].reshape(window, HEAD_WIDTH)
            scores = lax.dot_general(
                rows, keys, (((1,), (1,)), ((), ())), preferred_element_type=jnp.float32
            )
            scores = scores.reshape(chunk_heads, BLOCK, window) * scale + bias[j][None]
            top = jnp.max(scores, axis=2, keepdims=True)
            weights = jnp.exp2(scores - top)
            total = jnp.sum(weights, axis=2, keepdims=True)
            mixed = jnp.dot(
                weights.astype(jnp.bfloat16).reshape(chunk_heads * BLOCK, window),
                values,
                preferred_element_type=jnp.float32,
            ).reshape(chunk_heads, BLOCK, HEAD_WIDTH)
            result = (mixed / total).astype(jnp.bfloat16)
            for h in range(chunk_heads):
                block_out[j, :, h * HEAD_WIDTH : (h + 1) * HEAD_WIDTH] = result[h]

    def dispatch(c):
        unit(first, c)[...] = chosen(c, first_index)

        @pl.when(outer)
        def _():
            unit(second, c)[...] = chosen(c, near_index)
            to_near(c).start()
            for core, lag in enumerate(LAGS):
                if c >= lag:

                    @pl.when(tp == core)
                    def _():
                        pl.semaphore_wait(credit, 1)


        first_copy(c, sender).start()

        @pl.when(inner)
        def _():
            unit(homeward, c)[...] = chosen(c, home_index)
            home_copy(c, 0).start()
            unit(spare, c)[...] = chosen(c, second_index)
            extra_copy(c).start()

        unit(mine, c, g)[...] = chosen(c, own_index)
        place(c, g, False)

    def join(c):
        to_near(c).wait_recv()
        arrived = unit(land_near, c)[...]
        unit(second, c)[...] = jnp.where(near_both, arrived, unit(spare, c)[...])
        to_far(c).start()
        unit(mine, c, near_outer)[...] = jnp.where(near_here, arrived, jnp.zeros_like(arrived))
        place(c, near_outer, False)

    def spread(c, lag):
        first_copy(c, 0).wait_recv()
        first_copy(c, 1).wait_recv()
        to_far(c).wait_recv()
        if c + lag < chunks:
            pl.semaphore_signal(
                credit, inc=1, device_id={"seq": far_outer}, device_id_type=MESH
            )
        from_outer = unit(land_first, c, 0)[...]
        from_inner = unit(land_first, c, 1)[...]
        last = unit(land_second, c)[...]
        nothing = jnp.zeros_like(last)
        unit(relay, c, 1)[...] = jnp.where(a_on, jnp.where(a_here, last, from_outer), nothing)
        home_copy(c, 2).start()
        rest = jnp.where(a_here & a_on, nothing, last)
        unit(relay, c, 0)[...] = jnp.where(b_on, jnp.where(b_here, rest, from_inner), nothing)
        home_copy(c, 1).start()
        unit(mine, c, far_outer)[...] = jnp.where(a_here, from_outer, nothing)
        place(c, far_outer, False)
        unit(mine, c, far_inner)[...] = jnp.where(b_here, from_inner, nothing)
        place(c, far_inner, False)

    def landed(c, s, half):
        remote(
            unit(mine, c, 0),
            out_rows(b * slots + s, half, c),
            x_send.at[c, 0],
            x_recv.at[c, s, half],
            blk=peer,
        ).wait_recv()

    for t in range(chunks + max(JOIN_LAG, *LAGS)):
        if t < chunks:
            attend(t)
            dispatch(t)
            if KV_EARLY and t == KV_EARLY - 1:
                forward_kv(1)
            for h in range(2 if KV_EARLY else 1, groups_kv):
                start = [begin for begin, _ in pieces].index(h * heads_per_group)
                if t == start - KV_LEAD:
                    send_kv(h)
                if t == start - KV_LEAD + 1:
                    forward_kv(h)

        @pl.when(inner)
        def _():
            if 0 <= t - JOIN_LAG < chunks:
                join(t - JOIN_LAG)

        for core, lag in enumerate(LAGS):
            if 0 <= t - lag < chunks:

                @pl.when(inner & (tp == core))
                def _():
                    spread(t - lag, lag)

    word_copy().wait()
    flag_ref[0, 0] = jnp.maximum(spilled, jnp.max(word_in[...]))

    for h in range(groups_kv):
        for i in range(2):
            kv_copy(h, i).wait_send()

    @pl.when(g < seq - 1)
    def _():
        for h in range(groups_kv):
            for e in range(2):
                for i in range(2):
                    near_copy(h, i, e).wait_send()

    for c in range(chunks):
        q_copy(c).wait_send()
        first_copy(c, sender).wait_send()

        @pl.when(outer)
        def _():
            to_near(c).wait_send()

        @pl.when(inner)
        def _():
            to_far(c).wait_send()
            extra_copy(c).wait()
            for k in range(3):
                home_copy(c, k).wait_send()
            for group in (near_outer, far_inner, far_outer):
                place(c, group, True)

        place(c, g, True)
        for s in range(slots):
            landed(c, s, peer)

            @pl.when(outer & (b * slots + s != g))
            def _():
                landed(c, s, b)


def spill_kernel(dims, extra_ref, got_ref, send, recv):
    seq, blk, columns_dev, pieces, slots = dims
    chunks = len(pieces)
    g = lax.axis_index("seq")
    b = lax.axis_index("blk")
    inner = (g == 1) | (g == 2)
    mate = lax.rem(g + 2, seq)
    barrier = pltpu.get_barrier_semaphore()
    for e in range(blk):
        pl.semaphore_signal(
            barrier, inc=1, device_id={"seq": mate, "blk": e}, device_id_type=MESH
        )
    pl.semaphore_wait(barrier, blk)

    def spill(c, half, holder):
        start, width = pieces[c][0] * HEAD_WIDTH, pieces[c][1] * HEAD_WIDTH
        return pltpu.make_async_remote_copy(
            src_ref=extra_ref.at[c, :, :width],
            dst_ref=got_ref.at[
                :, pl.ds(pl.multiple_of(half * columns_dev + start, HEAD_WIDTH), width)
            ],
            send_sem=send.at[c],
            recv_sem=recv.at[c, half],
            device_id={"seq": mate, "blk": holder},
            device_id_type=MESH,
        )

    @pl.when(inner)
    def _():
        for c in range(chunks):
            spill(c, b, g // slots).start()
        for c in range(chunks):
            spill(c, b, g // slots).wait_send()

    @pl.when(jnp.logical_not(inner) & (b == mate // slots))
    def _():
        for c in range(chunks):
            for half in range(blk):
                spill(c, half, b).wait_recv()


def finish_spilled(slots, plan_ref, src_ref, got_ref, dst_ref, sem):
    owner = lax.axis_index("seq")
    b = lax.axis_index("blk")

    def has(group, wanted):
        return (plan_ref[0, group] == wanted) | (plan_ref[1, group] == wanted)

    full_right = has(0, 2) & has(0, 3) & has(1, 2) & has(1, 3)
    full_left = has(3, 1) & has(3, 0) & has(2, 1) & has(2, 0)
    for s in range(slots):
        group = b * slots + s
        rows = pl.ds(s * BLOCK, BLOCK)
        spilled = ((group == 1) & (owner == 3) & full_right) | (
            (group == 2) & (owner == 0) & full_left
        )

        @pl.when(spilled)
        def _():
            copy = pltpu.make_async_copy(got_ref, dst_ref.at[rows], sem.at[s])
            copy.start()
            copy.wait()

        @pl.when(jnp.logical_not(spilled))
        def _():
            copy = pltpu.make_async_copy(src_ref.at[rows], dst_ref.at[rows], sem.at[s])
            copy.start()
            copy.wait()


def quad(queries, rotated_keys, head_value_rows, doc_lengths, owner_plan):
    blk = lax.axis_size("blk")
    seq = lax.axis_size("seq")
    parts = lax.axis_size("groups")
    heads_dev = queries.shape[1] // HEAD_WIDTH // blk
    heads_per_group = QUERY_HEADS // KEY_HEADS
    groups_kv = heads_dev // heads_per_group
    sizes = []
    for h in range(groups_kv):
        row = [CHUNK_HEADS] * (heads_per_group // CHUNK_HEADS)
        if h == 0:
            row = list(HEAD_SPLIT) + row[1:]
        if h == groups_kv - 1:
            row = row[:-1] + list(TAIL_SPLIT)
        sizes += row
    pieces = [(sum(sizes[:c]), sizes[c]) for c in range(len(sizes))]
    chunks = len(pieces)
    slots = seq // blk
    width = max(sizes) * HEAD_WIDTH
    dims = (seq, blk, heads_dev, groups_kv, heads_per_group, pieces, slots, parts)
    bf16 = jnp.bfloat16
    dma = pltpu.SemaphoreType.DMA
    hbm = pl.BlockSpec(memory_space=pltpu.HBM)
    plan = owner_plan.T
    out_shape = jax.ShapeDtypeStruct((slots * BLOCK, queries.shape[1]), bf16)

    def unit(*lead):
        return pltpu.VMEM(lead + (BLOCK, width), bf16)

    placed, extra, flag = pl.pallas_call(
        functools.partial(quad_kernel, dims),
        out_shape=(
            out_shape,
            jax.ShapeDtypeStruct((chunks, BLOCK, width), bf16),
            jax.ShapeDtypeStruct((1, 1), jnp.int32),
        ),
        in_specs=[hbm] * 5,
        out_specs=(
            pl.BlockSpec(memory_space=pl.ANY),
            pl.BlockSpec(memory_space=pl.ANY),
            pl.BlockSpec(memory_space=pltpu.SMEM),
        ),
        scratch_shapes=[
            unit(chunks, blk),
            pltpu.VMEM((groups_kv, 2 * blk, BLOCK, HEAD_WIDTH), bf16),
            pltpu.VMEM((groups_kv, 2 * blk, BLOCK, HEAD_WIDTH), bf16),
            pltpu.VMEM((blk, BLOCK, (blk + 1) * BLOCK), jnp.float32),
            unit(blk + 1),
            unit(chunks),
            unit(chunks),
            unit(chunks),
            unit(chunks, 2),
            unit(chunks),
            unit(chunks, 2),
            unit(chunks),
            unit(chunks),
            unit(chunks, seq),
            pltpu.VMEM((8, 128), jnp.int32),
            pltpu.VMEM((8, 128), jnp.int32),
            pltpu.SMEM(doc_lengths.shape, jnp.int32),
            pltpu.SMEM(plan.shape, jnp.int32),
            dma((2,)),
            dma((2 * groups_kv + chunks,)),
            dma((chunks,)),
            dma((chunks,)),
            dma((groups_kv, 2)),
            dma((groups_kv, 2)),
            dma((groups_kv, 2, 2)),
            dma((groups_kv, 2, 2)),
            dma((chunks,)),
            dma((chunks, 2)),
            dma((chunks,)),
            dma((chunks,)),
            dma((chunks,)),
            dma((chunks, 3)),
            dma((chunks, seq)),
            dma((chunks, slots, blk)),
            dma((chunks,)),
            dma,
            dma,
            pltpu.SemaphoreType.REGULAR,
        ],
        compiler_params=pltpu.CompilerParams(
            collective_id=0, has_side_effects=True, vmem_limit_bytes=VMEM_MAIN
        ),
    )(doc_lengths, plan, queries, rotated_keys, head_value_rows)

    def plain(placed, extra):
        return placed

    def spilled(placed, extra):
        got = pl.pallas_call(
            functools.partial(spill_kernel, (seq, blk, heads_dev * HEAD_WIDTH, pieces, slots)),
            out_shape=jax.ShapeDtypeStruct((BLOCK, queries.shape[1]), bf16),
            in_specs=[pl.BlockSpec(memory_space=pl.ANY)],
            out_specs=pl.BlockSpec(memory_space=pl.ANY),
            scratch_shapes=[dma((chunks,)), dma((chunks, blk))],
            compiler_params=pltpu.CompilerParams(
                collective_id=1, has_side_effects=True, vmem_limit_bytes=VMEM_REST
            ),
        )(extra)
        return pl.pallas_call(
            functools.partial(finish_spilled, slots),
            out_shape=out_shape,
            in_specs=[pl.BlockSpec(memory_space=pltpu.SMEM)]
            + [pl.BlockSpec(memory_space=pl.ANY)] * 2,
            out_specs=hbm,
            scratch_shapes=[dma((slots,))],
            compiler_params=pltpu.CompilerParams(vmem_limit_bytes=VMEM_REST),
        )(plan, placed, got)

    return lax.cond(flag[0, 0] > 0, spilled, plain, placed, extra)


def per_device(queries, rotated_keys, head_value_rows, doc_lengths, owner_plan):
    blk = lax.axis_size("blk")
    seq = lax.axis_size("seq")
    heads_dev = queries.shape[1] // HEAD_WIDTH // blk
    heads_per_group = QUERY_HEADS // KEY_HEADS
    groups_kv = max(1, heads_dev // heads_per_group)
    chunk_heads = min(CHUNK_HEADS, heads_dev, heads_per_group)
    chunks = heads_dev // chunk_heads
    slots = seq // blk
    if (seq, blk, lax.axis_size("groups")) == (4, 2, 2) and heads_dev % heads_per_group == 0:
        return quad(queries, rotated_keys, head_value_rows, doc_lengths, owner_plan)
    width = chunk_heads * HEAD_WIDTH
    dims = (seq, blk, heads_dev, groups_kv, heads_per_group, chunk_heads, slots)
    bf16 = jnp.bfloat16
    dma = pltpu.SemaphoreType.DMA
    placed = pl.pallas_call(
        functools.partial(kernel, dims),
        out_shape=jax.ShapeDtypeStruct((slots * BLOCK, queries.shape[1]), bf16),
        in_specs=[pl.BlockSpec(memory_space=pltpu.SMEM)] * 2
        + [pl.BlockSpec(memory_space=pl.ANY)] * 3,
        out_specs=pl.BlockSpec(memory_space=pl.ANY),
        scratch_shapes=[
            pltpu.VMEM((chunks, blk, BLOCK, width), bf16),
            pltpu.VMEM((groups_kv, 2 * blk, BLOCK, HEAD_WIDTH), bf16),
            pltpu.VMEM((groups_kv, 2 * blk, BLOCK, HEAD_WIDTH), bf16),
            pltpu.VMEM((blk, BLOCK, (blk + 1) * BLOCK), jnp.float32),
            pltpu.VMEM((blk + 1, BLOCK, width), bf16),
            pltpu.VMEM((chunks, seq, BLOCK, width), bf16),
            pltpu.VMEM((chunks, seq - 1, BLOCK, width), bf16),
            dma((2 * groups_kv + chunks,)),
            dma((chunks, blk - 1)),
            dma((chunks, blk - 1)),
            dma((groups_kv, 2, blk - 1)),
            dma((groups_kv, 2, blk - 1)),
            dma((groups_kv, 2, blk)),
            dma((groups_kv, 2, blk)),
            dma((chunks, seq - 1)),
            dma((chunks, seq - 1)),
            dma((chunks, seq)),
            dma((chunks, slots, blk)),
        ],
        compiler_params=pltpu.CompilerParams(collective_id=0, has_side_effects=True),
    )(doc_lengths, owner_plan.T, queries, rotated_keys, head_value_rows)
    pieces = PIECES
    return pl.pallas_call(
        functools.partial(settle, pieces),
        out_shape=jax.ShapeDtypeStruct(placed.shape, bf16),
        in_specs=[pl.BlockSpec(memory_space=pl.ANY)],
        out_specs=pl.BlockSpec(memory_space=pl.ANY),
        scratch_shapes=[
            pltpu.VMEM((pieces, placed.shape[0] // pieces, placed.shape[1]), bf16),
            dma((pieces,)),
            dma((pieces,)),
        ],
    )(placed)


def solution(mesh):
    in_specs = (
        P(("groups", "seq", "blk"), "tp"),
        P(("groups", "seq", "blk"), "tp"),
        P(("groups", "seq", "blk"), "tp"),
        P("groups"),
        P("groups", None),
    )
    out_specs = P(("groups", "seq", "blk"), "tp")
    return jax.shard_map(
        per_device, mesh=mesh, in_specs=in_specs, out_specs=out_specs, check_vma=False
    )
```

```python
import functools
import math

import jax
import jax.numpy as jnp
from jax import lax
from jax.experimental import pallas as pl
from jax.experimental.pallas import tpu as pltpu
from jax.sharding import PartitionSpec as P

QUERY_HEADS = 64
KEY_HEADS = 8
HEAD_WIDTH = 128
BLOCK = 128
CHUNK_HEADS = 2
HEAD_SPLIT = (2,)
TAIL_SPLIT = (2,)
PIECES = 8

MESH = pl.DeviceIdType.MESH
masked_score = -1e30
JOIN_LAG = 1
LAGS = (3,3)
KV_EARLY = 2
DETOUR = 2
QUERY_SECOND = 2
DIRECT_HEADS = 0
VMEM_MAIN = 58 * 2**20
QUERY_FIRST = 1
QUERY_LEAD = 2
KV_LEAD = 4
VMEM_REST = 4 * 2**20


def kernel(
    dims,
    lengths_ref,
    plan_ref,
    q_ref,
    k_ref,
    v_ref,
    out_ref,
    q_group,
    k_near,
    v_near,
    bias,
    block_out,
    message,
    landed,
    local_sem,
    q_send,
    q_recv,
    kv_send,
    kv_recv,
    near_send,
    near_recv,
    z_send,
    z_recv,
    x_send,
    x_recv,
):
    seq, blk, heads_dev, groups_kv, heads_per_group, chunk_heads, slots = dims
    g = lax.axis_index("seq")
    b = lax.axis_index("blk")
    chunks = heads_dev // chunk_heads
    width = chunk_heads * HEAD_WIDTH
    columns_dev = heads_dev * HEAD_WIDTH
    window = (blk + 1) * BLOCK
    group_len = blk * BLOCK
    scale = 1.0 / math.sqrt(HEAD_WIDTH)

    def kv_columns(owner, h):
        first = owner * heads_dev // heads_per_group + h
        return pl.ds(pl.multiple_of(first * HEAD_WIDTH, HEAD_WIDTH), HEAD_WIDTH)

    def q_columns(owner, c):
        return pl.ds(pl.multiple_of(owner * columns_dev + c * width, HEAD_WIDTH), width)

    barrier = pltpu.get_barrier_semaphore()
    for e in range(1, blk):
        pl.semaphore_signal(
            barrier, inc=1, device_id={"blk": lax.rem(b + e, blk)}, device_id_type=MESH
        )
    for d in range(1, seq):
        pl.semaphore_signal(
            barrier, inc=1, device_id={"seq": lax.rem(g + d, seq)}, device_id_type=MESH
        )

    pairs = ((k_ref, k_near), (v_ref, v_near))
    own_kv = [
        pltpu.make_async_copy(
            src.at[:, kv_columns(b, h)], dst.at[h, blk + b], local_sem.at[2 * h + i]
        )
        for h in range(groups_kv)
        for i, (src, dst) in enumerate(pairs)
    ]
    own_q = [
        pltpu.make_async_copy(
            q_ref.at[:, q_columns(b, c)], q_group.at[c, b], local_sem.at[2 * groups_kv + c]
        )
        for c in range(chunks)
    ]
    for copy in own_kv + own_q:
        copy.start()

    def kv_copy(h, i, e):
        src, dst = pairs[i]
        peer = lax.rem(b + e, blk)
        return pltpu.make_async_remote_copy(
            src_ref=src.at[:, kv_columns(peer, h)],
            dst_ref=dst.at[h, blk + b],
            send_sem=kv_send.at[h, i, e - 1],
            recv_sem=kv_recv.at[h, i, e - 1],
            device_id={"blk": peer},
            device_id_type=MESH,
        )

    def near_copy(h, i, e):
        src, dst = pairs[i]
        origin = lax.rem(b - e + blk, blk)
        if e == 0:
            source = src.at[:, kv_columns(b, h)]
        else:
            source = dst.at[h, blk + origin]
        return pltpu.make_async_remote_copy(
            src_ref=source,
            dst_ref=dst.at[h, origin],
            send_sem=near_send.at[h, i, e],
            recv_sem=near_recv.at[h, i, e],
            device_id={"seq": lax.rem(g + 1, seq)},
            device_id_type=MESH,
        )

    def q_copy(c, e):
        peer = lax.rem(b + e, blk)
        return pltpu.make_async_remote_copy(
            src_ref=q_ref.at[:, q_columns(peer, c)],
            dst_ref=q_group.at[c, b],
            send_sem=q_send.at[c, e - 1],
            recv_sem=q_recv.at[c, e - 1],
            device_id={"blk": peer},
            device_id_type=MESH,
        )

    for j in range(blk):
        first_row = g * group_len + j * BLOCK
        row_pos = first_row + lax.broadcasted_iota(jnp.int32, (BLOCK, 1), 0)
        end = jnp.int32(0)
        start = jnp.zeros((BLOCK, 1), jnp.int32)
        for n in range(lengths_ref.shape[0]):
            end = end + lengths_ref[n]
            start = jnp.where(row_pos >= end, end, start)
        key_pos = first_row - group_len + lax.broadcasted_iota(jnp.int32, (BLOCK, window), 1)
        allowed = (key_pos >= start) & (key_pos <= row_pos)
        bias[j] = jnp.where(allowed, 0.0, masked_score)
    block_out[blk] = jnp.zeros(block_out.shape[1:], block_out.dtype)

    @pl.when(g == 0)
    def _():
        for h in range(groups_kv):
            for j in range(blk):
                k_near[h, j] = jnp.zeros(k_near.shape[2:], k_near.dtype)
                v_near[h, j] = jnp.zeros(v_near.shape[2:], v_near.dtype)

    pl.semaphore_wait(barrier, blk - 1 + seq - 1)

    def send_kv(h):
        for e in range(1, blk):
            for i in range(2):
                kv_copy(h, i, e).start()

    def send_q(c):
        for e in range(1, blk):
            q_copy(c, e).start()

    def forward_kv(h):
        for e in range(1, blk):
            for i in range(2):
                kv_copy(h, i, e).wait_recv()

        @pl.when(g < seq - 1)
        def _():
            for e in range(1, blk):
                for i in range(2):
                    near_copy(h, i, e).start()

    def wait_near(h):
        @pl.when(g > 0)
        def _():
            for e in range(blk):
                for i in range(2):
                    near_copy(h, i, e).wait_recv()

    send_kv(0)

    @pl.when(g < seq - 1)
    def _():
        for h in range(groups_kv):
            for i in range(2):
                near_copy(h, i, 0).start()

    send_q(0)
    for h in range(1, groups_kv):
        send_kv(h)
    for c in range(1, chunks):
        send_q(c)

    forward_kv(0)
    for copy in own_kv:
        copy.wait()

    half = seq // 2
    side, place_in = g // half, lax.rem(g, half)

    def target(k):
        if k < half:
            return side * half + lax.rem(place_in + k, half)
        return (1 - side) * half + lax.rem(place_in + k - half, half)

    def origin_of(k):
        if k < half:
            return side * half + lax.rem(place_in - k + half, half)
        return (1 - side) * half + lax.rem(place_in - (k - half) + half, half)

    picked = []
    for d in range(seq):
        owner = target(d)
        index = jnp.int32(blk)
        for j in range(blk):
            index = jnp.where(plan_ref[j, g] == owner, jnp.int32(j), index)
        picked.append(index)

    def z_copy(c, d):
        return pltpu.make_async_remote_copy(
            src_ref=message.at[c, d],
            dst_ref=landed.at[c, d - 1],
            send_sem=z_send.at[c, d - 1],
            recv_sem=z_recv.at[c, d - 1],
            device_id={"seq": target(d)},
            device_id_type=MESH,
        )

    near, far = list(range(1, half)), list(range(half, seq))
    sends = [[] for _ in range(chunks)]
    for c in range(chunks):
        if c > 0:
            sends[c] += [(c, k) for k in near]
        if c in (0, chunks - 1):
            sends[c] += [(m, k) for m in range(max(c - 1, min(c, 1)), c + 1) for k in far]
        elif c > 1:
            sends[c] += [(c - 1, k) for k in far]
        if c == 0:
            sends[c] += [(c, k) for k in near]
    arrivals = [message for row in sends for message in row]
    for c in range(chunks):
        own_q[c].wait()
        for e in range(1, blk):
            q_copy(c, e).wait_recv()
        kv_head = c * chunk_heads // heads_per_group
        if c * chunk_heads % heads_per_group == 0 or c == 0:
            wait_near(kv_head)
        for j in range(blk):
            query = q_group[c, j]
            rows = jnp.concatenate(
                [query[:, h * HEAD_WIDTH : (h + 1) * HEAD_WIDTH] for h in range(chunk_heads)], axis=0
            )
            keys = k_near[kv_head, j : j + blk + 1].reshape(window, HEAD_WIDTH)
            values = v_near[kv_head, j : j + blk + 1].reshape(window, HEAD_WIDTH)
            scores = lax.dot_general(
                rows, keys, (((1,), (1,)), ((), ())), preferred_element_type=jnp.float32
            )
            scores = scores.reshape(chunk_heads, BLOCK, window) * scale + bias[j][None]
            top = jnp.max(scores, axis=2, keepdims=True)
            weights = jnp.exp(scores - top)
            total = jnp.sum(weights, axis=2, keepdims=True)
            mixed = jnp.dot(
                weights.astype(jnp.bfloat16).reshape(chunk_heads * BLOCK, window),
                values,
                preferred_element_type=jnp.float32,
            ).reshape(chunk_heads, BLOCK, HEAD_WIDTH)
            result = (mixed / total).astype(jnp.bfloat16)
            for h in range(chunk_heads):
                block_out[j, :, h * HEAD_WIDTH : (h + 1) * HEAD_WIDTH] = result[h]
        for d in range(seq):
            message[c, d] = block_out[picked[d]]
        for m, k in sends[c]:
            z_copy(m, k).start()
        if c == 0:
            for h in range(1, groups_kv):
                forward_kv(h)

    def place(c, d, waiting):
        origin = origin_of(d)
        source = message.at[c, 0] if d == 0 else landed.at[c, d - 1]
        holder = origin // slots
        slot = lax.rem(origin, slots)
        target = out_ref.at[
            pl.ds(pl.multiple_of(slot * BLOCK, BLOCK), BLOCK), q_columns(b, c)
        ]
        hop = lax.rem(holder - b + blk, blk)

        @pl.when(holder == b)
        def _():
            copy = pltpu.make_async_copy(source, target, x_send.at[c, d])
            if waiting:
                copy.wait()
            else:
                copy.start()

        @pl.when(holder != b)
        def _():
            copy = pltpu.make_async_remote_copy(
                src_ref=source,
                dst_ref=target,
                send_sem=x_send.at[c, d],
                recv_sem=x_recv.at[c, slot, lax.rem(hop - 1 + blk, blk)],
                device_id={"blk": holder},
                device_id_type=MESH,
            )
            if waiting:
                copy.wait_send()
            else:
                copy.start()

    for c in range(chunks):
        place(c, 0, False)
    for c, d in arrivals:
        z_copy(c, d).wait_recv()
        place(c, d, False)

    for c in range(chunks):
        for s in range(slots):
            for e in range(1, blk):
                sender = lax.rem(b - e + blk, blk)
                pltpu.make_async_remote_copy(
                    src_ref=message.at[c, 0],
                    dst_ref=out_ref.at[s * BLOCK : (s + 1) * BLOCK, q_columns(sender, c)],
                    send_sem=x_send.at[c, 0],
                    recv_sem=x_recv.at[c, s, e - 1],
                    device_id={"blk": sender},
                    device_id_type=MESH,
                ).wait_recv()
        for d in range(seq):
            place(c, d, True)
            if d > 0:
                z_copy(c, d).wait_send()
        for e in range(1, blk):
            q_copy(c, e).wait_send()
    for h in range(groups_kv):
        for i in range(2):
            for e in range(1, blk):
                kv_copy(h, i, e).wait_send()

    @pl.when(g < seq - 1)
    def _():
        for h in range(groups_kv):
            for e in range(blk):
                for i in range(2):
                    near_copy(h, i, e).wait_send()


def settle(pieces, src_ref, dst_ref, held, in_sem, out_sem):
    rows = src_ref.shape[0] // pieces
    taken = [
        pltpu.make_async_copy(src_ref.at[pl.ds(n * rows, rows)], held.at[n], in_sem.at[n])
        for n in range(pieces)
    ]
    put = [
        pltpu.make_async_copy(held.at[n], dst_ref.at[pl.ds(n * rows, rows)], out_sem.at[n])
        for n in range(pieces)
    ]
    for copy in taken:
        copy.start()
    for n in range(pieces):
        taken[n].wait()
        put[n].start()
    for copy in put:
        copy.wait()


def quad_kernel(
    dims,
    lengths_hbm,
    plan_hbm,
    q_ref,
    k_ref,
    v_ref,
    out_ref,
    extra_ref,
    flag_ref,
    q_group,
    k_near,
    v_near,
    bias,
    block_out,
    first,
    second,
    homeward,
    relay,
    spare,
    land_first,
    land_near,
    land_second,
    mine,
    word,
    word_in,
    lengths_ref,
    plan_ref,
    table_sem,
    local_sem,
    q_send,
    q_recv,
    kv_send,
    kv_recv,
    near_send,
    near_recv,
    first_send,
    first_recv,
    second_send,
    near_x_recv,
    second_recv,
    home_send,
    x_send,
    x_recv,
    extra_sem,
    word_send,
    word_recv,
    credit,
):
    seq, blk, heads_dev, groups_kv, heads_per_group, pieces, slots, parts = dims
    g = lax.axis_index("seq")
    b = lax.axis_index("blk")
    part = lax.axis_index("groups")
    tp = lax.axis_index("tp")
    chunks = len(pieces)
    columns_dev = heads_dev * HEAD_WIDTH
    window = (blk + 1) * BLOCK
    group_len = blk * BLOCK
    scale = math.log2(math.e) / math.sqrt(HEAD_WIDTH)

    left = g < 2
    inner = (g == 1) | (g == 2)
    outer = jnp.logical_not(inner)
    far_inner = jnp.where(left, 2, 1)
    far_outer = jnp.where(left, 3, 0)
    near_inner = jnp.where(left, 1, 2)
    near_outer = jnp.where(left, 0, 3)
    peer = 1 - b

    def kv_columns(owner, h):
        start = owner * heads_dev // heads_per_group + h
        return pl.ds(pl.multiple_of(start * HEAD_WIDTH, HEAD_WIDTH), HEAD_WIDTH)

    def q_columns(owner, c):
        start, heads = pieces[c]
        return pl.ds(
            pl.multiple_of(owner * columns_dev + start * HEAD_WIDTH, HEAD_WIDTH),
            heads * HEAD_WIDTH,
        )

    def unit(ref, c, *index):
        return ref.at[(c,) + index + (slice(None), slice(0, pieces[c][1] * HEAD_WIDTH))]

    def chosen(c, index):
        return block_out[index, :, : pieces[c][1] * HEAD_WIDTH]

    def remote(src, dst, send, recv, **where):
        return pltpu.make_async_remote_copy(
            src_ref=src,
            dst_ref=dst,
            send_sem=send,
            recv_sem=recv,
            device_id=where,
            device_id_type=MESH,
        )

    barrier = pltpu.get_barrier_semaphore()
    everyone = [
        {"blk": peer},
        {"groups": lax.rem(part + 1, parts)},
        {"seq": lax.rem(g + 2, seq)},
        {"seq": jnp.where(inner, near_outer, near_inner)},
        {"seq": jnp.where(inner, near_outer, near_inner), "blk": peer},
    ]
    across = [{"seq": far_inner}, {"seq": far_inner, "blk": peer}]

    def greet(devices):
        for device in devices:
            pl.semaphore_signal(barrier, inc=1, device_id=device, device_id_type=MESH)

    greet(everyone)

    @pl.when(inner)
    def _():
        greet(across)

    tables = [
        pltpu.make_async_copy(lengths_hbm, lengths_ref, table_sem.at[0]),
        pltpu.make_async_copy(plan_hbm, plan_ref, table_sem.at[1]),
    ]
    for copy in tables:
        copy.start()
    pairs = ((k_ref, k_near), (v_ref, v_near))
    own_kv = [
        pltpu.make_async_copy(
            src.at[:, kv_columns(b, h)], dst.at[h, blk + b], local_sem.at[2 * h + i]
        )
        for h in range(groups_kv)
        for i, (src, dst) in enumerate(pairs)
    ]
    own_q = [
        pltpu.make_async_copy(
            q_ref.at[:, q_columns(b, c)], unit(q_group, c, b), local_sem.at[2 * groups_kv + c]
        )
        for c in range(chunks)
    ]
    for copy in own_kv + own_q:
        copy.start()

    def kv_copy(h, i):
        src, dst = pairs[i]
        return remote(
            src.at[:, kv_columns(peer, h)],
            dst.at[h, blk + b],
            kv_send.at[h, i],
            kv_recv.at[h, i],
            blk=peer,
        )

    def near_copy(h, i, e):
        src, dst = pairs[i]
        if e == 0:
            source, origin, to = src.at[:, kv_columns(b, h)], b, b
        elif h < DIRECT_HEADS:
            source, origin, to = src.at[:, kv_columns(peer, h)], b, peer
        else:
            source, origin, to = dst.at[h, blk + peer], peer, b
        return remote(
            source,
            dst.at[h, origin],
            near_send.at[h, i, e],
            near_recv.at[h, i, e],
            seq=lax.rem(g + 1, seq),
            blk=to,
        )

    def q_copy(c):
        return remote(
            q_ref.at[:, q_columns(peer, c)],
            unit(q_group, c, b),
            q_send.at[c],
            q_recv.at[c],
            blk=peer,
        )

    @pl.when(g == 0)
    def _():
        for h in range(groups_kv):
            for j in range(blk):
                k_near[h, j] = jnp.zeros(k_near.shape[2:], k_near.dtype)
                v_near[h, j] = jnp.zeros(v_near.shape[2:], v_near.dtype)

    @pl.when(inner)
    def _():
        pl.semaphore_wait(barrier, len(everyone) + len(across))

    @pl.when(outer)
    def _():
        pl.semaphore_wait(barrier, len(everyone))


    def word_copy():
        return remote(word, word_in, word_send, word_recv, groups=lax.rem(part + 1, parts))

    def send_kv(h):
        @pl.when(g < seq - 1)
        def _():
            for e in range(2 if h < DIRECT_HEADS else 1):
                for i in range(2):
                    near_copy(h, i, e).start()

        for i in range(2):
            kv_copy(h, i).start()

    def forward_kv(h):
        for i in range(2):
            kv_copy(h, i).wait_recv()

        if h >= DIRECT_HEADS:

            @pl.when(g < seq - 1)
            def _():
                for i in range(2):
                    near_copy(h, i, 1).start()

    send_kv(0)
    for c in range(QUERY_FIRST):
        q_copy(c).start()

    for copy in tables:
        copy.wait()

    def has(group, owner):
        return (plan_ref[0, group] == owner) | (plan_ref[1, group] == owner)

    def pick(owner):
        return jnp.where(
            plan_ref[0, g] == owner,
            jnp.int32(0),
            jnp.where(plan_ref[1, g] == owner, jnp.int32(1), jnp.int32(blk)),
        )

    full_right = has(0, 2) & has(0, 3) & has(1, 2) & has(1, 3)
    full_left = has(3, 1) & has(3, 0) & has(2, 1) & has(2, 0)
    spilled = jnp.where(full_right | full_left, jnp.int32(1), jnp.int32(0))
    word[...] = jnp.full(word.shape, spilled, jnp.int32)

    for j in range(blk):
        first_row = g * group_len + j * BLOCK
        row_pos = first_row + lax.broadcasted_iota(jnp.int32, (BLOCK, 1), 0)
        end = jnp.int32(0)
        start = jnp.zeros((BLOCK, 1), jnp.int32)
        for n in range(lengths_ref.shape[0]):
            end = end + lengths_ref[n]
            start = jnp.where(row_pos >= end, end, start)
        key_pos = first_row - group_len + lax.broadcasted_iota(jnp.int32, (BLOCK, window), 1)
        allowed = (key_pos >= start) & (key_pos <= row_pos)
        bias[j] = jnp.where(allowed, 0.0, masked_score)
    block_out[blk] = jnp.zeros(block_out.shape[1:], block_out.dtype)

    forward_kv(0)
    for c in range(QUERY_FIRST, QUERY_SECOND):
        q_copy(c).start()
    if KV_EARLY:
        send_kv(1)
    word_copy().start()
    for copy in own_kv:
        copy.wait()

    sender = jnp.where(inner, 1, 0)

    def first_copy(c, which):
        return remote(
            unit(first, c),
            unit(land_first, c, which),
            first_send.at[c],
            first_recv.at[c, which],
            seq=far_inner,
        )

    def to_near(c):
        return remote(
            unit(second, c), unit(land_near, c), second_send.at[c], near_x_recv.at[c], seq=near_inner
        )

    def to_far(c):
        return remote(
            unit(second, c), unit(land_second, c), second_send.at[c], second_recv.at[c], seq=far_inner
        )

    def out_rows(group, half, c):
        slot = lax.rem(group, slots)
        return out_ref.at[
            pl.ds(pl.multiple_of(slot * BLOCK, BLOCK), BLOCK), q_columns(half, c)
        ]

    def home_copy(c, k):
        source = unit(homeward, c) if k == 0 else unit(relay, c, k - 1)
        group = (near_inner, far_inner, far_outer)[k]
        return remote(
            source,
            out_rows(group, b, c),
            home_send.at[c, k],
            x_recv.at[c, lax.rem(group, slots), b],
            seq=near_outer,
            blk=group // slots,
        )

    def extra_copy(c):
        return pltpu.make_async_copy(unit(spare, c), unit(extra_ref, c), extra_sem.at[c])

    def place(c, group, waiting):
        source = unit(mine, c, group)
        holder = group // slots
        target = out_rows(group, b, c)

        @pl.when(holder == b)
        def _():
            copy = pltpu.make_async_copy(source, target, x_send.at[c, group])
            if waiting:
                copy.wait()
            else:
                copy.start()

        @pl.when(holder != b)
        def _():
            copy = remote(
                source,
                target,
                x_send.at[c, group],
                x_recv.at[c, lax.rem(group, slots), b],
                blk=holder,
            )
            if waiting:
                copy.wait_send()
            else:
                copy.start()

    to_inner, to_outer = pick(far_inner), pick(far_outer)
    both = (to_inner < blk) & (to_outer < blk)
    first_index = jnp.where(to_inner < blk, to_inner, to_outer)
    second_index = jnp.where(both, to_outer, jnp.int32(blk))
    near_index = jnp.where(both, to_outer, pick(near_inner))
    home_index, own_index = pick(near_outer), pick(g)

    near_both = has(near_outer, far_inner) & has(near_outer, far_outer)
    near_here = has(near_outer, g)
    a_here, a_on = has(far_outer, g), has(far_outer, near_outer)
    b_here, b_on = has(far_inner, g), has(far_inner, near_outer)

    def attend(c):
        own_q[c].wait()
        q_copy(c).wait_recv()
        for m in range(max(QUERY_SECOND, c and c + QUERY_LEAD), min(c + QUERY_LEAD + 1, chunks)):
            q_copy(m).start()
        begin, chunk_heads = pieces[c]
        kv_head = begin // heads_per_group
        if begin % heads_per_group == 0:

            @pl.when(g > 0)
            def _():
                for e in range(2):
                    for i in range(2):
                        near_copy(kv_head, i, e).wait_recv()

        for j in range(blk):
            query = unit(q_group, c, j)[...]
            rows = jnp.concatenate(
                [query[:, h * HEAD_WIDTH : (h + 1) * HEAD_WIDTH] for h in range(chunk_heads)], axis=0
            )
            keys = k_near[kv_head, j : j + blk + 1].reshape(window, HEAD_WIDTH)
            values = v_near[kv_head, j : j + blk + 1].reshape(window, HEAD_WIDTH)
            scores = lax.dot_general(
                rows, keys, (((1,), (1,)), ((), ())), preferred_element_type=jnp.float32
            )
            scores = scores.reshape(chunk_heads, BLOCK, window) * scale + bias[j][None]
            top = jnp.max(scores, axis=2, keepdims=True)
            weights = jnp.exp2(scores - top)
            total = jnp.sum(weights, axis=2, keepdims=True)
            mixed = jnp.dot(
                weights.astype(jnp.bfloat16).reshape(chunk_heads * BLOCK, window),
                values,
                preferred_element_type=jnp.float32,
            ).reshape(chunk_heads, BLOCK, HEAD_WIDTH)
            result = (mixed / total).astype(jnp.bfloat16)
            for h in range(chunk_heads):
                block_out[j, :, h * HEAD_WIDTH : (h + 1) * HEAD_WIDTH] = result[h]

    def dispatch(c):
        unit(first, c)[...] = chosen(c, first_index)

        @pl.when(outer)
        def _():
            unit(second, c)[...] = chosen(c, near_index)
            to_near(c).start()
            for core, lag in enumerate(LAGS):
                if c >= lag:

                    @pl.when(tp == core)
                    def _():
                        pl.semaphore_wait(credit, 1)


        first_copy(c, sender).start()

        @pl.when(inner)
        def _():
            unit(homeward, c)[...] = chosen(c, home_index)
            home_copy(c, 0).start()
            unit(spare, c)[...] = chosen(c, second_index)
            extra_copy(c).start()

        unit(mine, c, g)[...] = chosen(c, own_index)
        place(c, g, False)

    def join(c):
        to_near(c).wait_recv()
        arrived = unit(land_near, c)[...]
        unit(second, c)[...] = jnp.where(near_both, arrived, unit(spare, c)[...])
        to_far(c).start()
        unit(mine, c, near_outer)[...] = jnp.where(near_here, arrived, jnp.zeros_like(arrived))
        place(c, near_outer, False)

    def spread(c, lag):
        first_copy(c, 0).wait_recv()
        first_copy(c, 1).wait_recv()
        to_far(c).wait_recv()
        if c + lag < chunks:
            pl.semaphore_signal(
                credit, inc=1, device_id={"seq": far_outer}, device_id_type=MESH
            )
        from_outer = unit(land_first, c, 0)[...]
        from_inner = unit(land_first, c, 1)[...]
        last = unit(land_second, c)[...]
        nothing = jnp.zeros_like(last)
        unit(relay, c, 1)[...] = jnp.where(a_on, jnp.where(a_here, last, from_outer), nothing)
        home_copy(c, 2).start()
        rest = jnp.where(a_here & a_on, nothing, last)
        unit(relay, c, 0)[...] = jnp.where(b_on, jnp.where(b_here, rest, from_inner), nothing)
        home_copy(c, 1).start()
        unit(mine, c, far_outer)[...] = jnp.where(a_here, from_outer, nothing)
        place(c, far_outer, False)
        unit(mine, c, far_inner)[...] = jnp.where(b_here, from_inner, nothing)
        place(c, far_inner, False)

    def landed(c, s, half):
        remote(
            unit(mine, c, 0),
            out_rows(b * slots + s, half, c),
            x_send.at[c, 0],
            x_recv.at[c, s, half],
            blk=peer,
        ).wait_recv()

    for t in range(chunks + max(JOIN_LAG, *LAGS)):
        if t < chunks:
            attend(t)
            dispatch(t)
            if KV_EARLY and t == KV_EARLY - 1:
                forward_kv(1)
            for h in range(2 if KV_EARLY else 1, groups_kv):
                start = [begin for begin, _ in pieces].index(h * heads_per_group)
                if t == start - KV_LEAD:
                    send_kv(h)
                if t == start - KV_LEAD + 1:
                    forward_kv(h)

        @pl.when(inner)
        def _():
            if 0 <= t - JOIN_LAG < chunks:
                join(t - JOIN_LAG)

        for core, lag in enumerate(LAGS):
            if 0 <= t - lag < chunks:

                @pl.when(inner & (tp == core))
                def _():
                    spread(t - lag, lag)

    word_copy().wait()
    flag_ref[0, 0] = spilled * (1 + part) + jnp.max(word_in[...]) * (2 - part)

    for h in range(groups_kv):
        for i in range(2):
            kv_copy(h, i).wait_send()

    @pl.when(g < seq - 1)
    def _():
        for h in range(groups_kv):
            for e in range(2):
                for i in range(2):
                    near_copy(h, i, e).wait_send()

    for c in range(chunks):
        q_copy(c).wait_send()
        first_copy(c, sender).wait_send()

        @pl.when(outer)
        def _():
            to_near(c).wait_send()

        @pl.when(inner)
        def _():
            to_far(c).wait_send()
            extra_copy(c).wait()
            for k in range(3):
                home_copy(c, k).wait_send()
            for group in (near_outer, far_inner, far_outer):
                place(c, group, True)

        place(c, g, True)
        for s in range(slots):
            landed(c, s, peer)

            @pl.when(outer & (b * slots + s != g))
            def _():
                landed(c, s, b)


def spill_kernel(dims, active, extra_ref, got_ref, via, send, recv, via_recv):
    seq, blk, columns_dev, pieces, slots, parts = dims
    chunks = len(pieces)
    part = lax.axis_index("groups")
    g = lax.axis_index("seq")
    b = lax.axis_index("blk")
    inner = (g == 1) | (g == 2)
    mate = lax.rem(g + 2, seq)
    other = lax.rem(part + 1, parts)
    direct = chunks if active is None else chunks - DETOUR
    barrier = pltpu.get_barrier_semaphore()
    greeted = [{"seq": mate, "blk": e} for e in range(blk)]
    greeted += [{"groups": other, "seq": mate, "blk": e} for e in range(blk)]
    greeted += [{"groups": other}]
    for device in greeted:
        pl.semaphore_signal(barrier, inc=1, device_id=device, device_id_type=MESH)
    pl.semaphore_wait(barrier, len(greeted))

    def spill(c, half, holder, source, owner_part):
        start, width = pieces[c][0] * HEAD_WIDTH, pieces[c][1] * HEAD_WIDTH
        return pltpu.make_async_remote_copy(
            src_ref=source.at[c, :, :width],
            dst_ref=got_ref.at[
                :, pl.ds(pl.multiple_of(half * columns_dev + start, HEAD_WIDTH), width)
            ],
            send_sem=send.at[c],
            recv_sem=recv.at[c, half],
            device_id={"groups": owner_part, "seq": mate, "blk": holder},
            device_id_type=MESH,
        )

    def to_side(c):
        return pltpu.make_async_remote_copy(
            src_ref=extra_ref.at[c],
            dst_ref=via.at[c],
            send_sem=send.at[c],
            recv_sem=via_recv.at[c],
            device_id={"groups": other},
            device_id_type=MESH,
        )

    mine = part < parts if active is None else part == active

    @pl.when(mine & inner)
    def _():
        for c in range(direct, chunks):
            to_side(c).start()
        for c in range(direct):
            spill(c, b, g // slots, extra_ref, part).start()
        for c in range(direct, chunks):
            to_side(c).wait_send()
        for c in range(direct):
            spill(c, b, g // slots, extra_ref, part).wait_send()

    @pl.when(jnp.logical_not(mine) & inner)
    def _():
        for c in range(direct, chunks):
            to_side(c).wait_recv()
            spill(c, b, g // slots, via, other).start()
        for c in range(direct, chunks):
            spill(c, b, g // slots, via, other).wait_send()

    @pl.when(mine & jnp.logical_not(inner) & (b == mate // slots))
    def _():
        for c in range(chunks):
            for half in range(blk):
                spill(c, half, b, extra_ref, part).wait_recv()


def finish_spilled(slots, plan_ref, src_ref, got_ref, dst_ref, sem):
    owner = lax.axis_index("seq")
    b = lax.axis_index("blk")

    def has(group, wanted):
        return (plan_ref[0, group] == wanted) | (plan_ref[1, group] == wanted)

    full_right = has(0, 2) & has(0, 3) & has(1, 2) & has(1, 3)
    full_left = has(3, 1) & has(3, 0) & has(2, 1) & has(2, 0)
    for s in range(slots):
        group = b * slots + s
        rows = pl.ds(s * BLOCK, BLOCK)
        spilled = ((group == 1) & (owner == 3) & full_right) | (
            (group == 2) & (owner == 0) & full_left
        )

        @pl.when(spilled)
        def _():
            copy = pltpu.make_async_copy(got_ref, dst_ref.at[rows], sem.at[s])
            copy.start()
            copy.wait()

        @pl.when(jnp.logical_not(spilled))
        def _():
            copy = pltpu.make_async_copy(src_ref.at[rows], dst_ref.at[rows], sem.at[s])
            copy.start()
            copy.wait()


def quad(queries, rotated_keys, head_value_rows, doc_lengths, owner_plan):
    blk = lax.axis_size("blk")
    seq = lax.axis_size("seq")
    parts = lax.axis_size("groups")
    heads_dev = queries.shape[1] // HEAD_WIDTH // blk
    heads_per_group = QUERY_HEADS // KEY_HEADS
    groups_kv = heads_dev // heads_per_group
    sizes = []
    for h in range(groups_kv):
        row = [CHUNK_HEADS] * (heads_per_group // CHUNK_HEADS)
        if h == 0:
            row = list(HEAD_SPLIT) + row[1:]
        if h == groups_kv - 1:
            row = row[:-1] + list(TAIL_SPLIT)
        sizes += row
    pieces = [(sum(sizes[:c]), sizes[c]) for c in range(len(sizes))]
    chunks = len(pieces)
    slots = seq // blk
    width = max(sizes) * HEAD_WIDTH
    dims = (seq, blk, heads_dev, groups_kv, heads_per_group, pieces, slots, parts)
    bf16 = jnp.bfloat16
    dma = pltpu.SemaphoreType.DMA
    hbm = pl.BlockSpec(memory_space=pltpu.HBM)
    plan = owner_plan.T
    out_shape = jax.ShapeDtypeStruct((slots * BLOCK, queries.shape[1]), bf16)

    def unit(*lead):
        return pltpu.VMEM(lead + (BLOCK, width), bf16)

    placed, extra, flag = pl.pallas_call(
        functools.partial(quad_kernel, dims),
        out_shape=(
            out_shape,
            jax.ShapeDtypeStruct((chunks, BLOCK, width), bf16),
            jax.ShapeDtypeStruct((1, 1), jnp.int32),
        ),
        in_specs=[hbm] * 5,
        out_specs=(
            pl.BlockSpec(memory_space=pl.ANY),
            pl.BlockSpec(memory_space=pl.ANY),
            pl.BlockSpec(memory_space=pltpu.SMEM),
        ),
        scratch_shapes=[
            unit(chunks, blk),
            pltpu.VMEM((groups_kv, 2 * blk, BLOCK, HEAD_WIDTH), bf16),
            pltpu.VMEM((groups_kv, 2 * blk, BLOCK, HEAD_WIDTH), bf16),
            pltpu.VMEM((blk, BLOCK, (blk + 1) * BLOCK), jnp.float32),
            unit(blk + 1),
            unit(chunks),
            unit(chunks),
            unit(chunks),
            unit(chunks, 2),
            unit(chunks),
            unit(chunks, 2),
            unit(chunks),
            unit(chunks),
            unit(chunks, seq),
            pltpu.VMEM((8, 128), jnp.int32),
            pltpu.VMEM((8, 128), jnp.int32),
            pltpu.SMEM(doc_lengths.shape, jnp.int32),
            pltpu.SMEM(plan.shape, jnp.int32),
            dma((2,)),
            dma((2 * groups_kv + chunks,)),
            dma((chunks,)),
            dma((chunks,)),
            dma((groups_kv, 2)),
            dma((groups_kv, 2)),
            dma((groups_kv, 2, 2)),
            dma((groups_kv, 2, 2)),
            dma((chunks,)),
            dma((chunks, 2)),
            dma((chunks,)),
            dma((chunks,)),
            dma((chunks,)),
            dma((chunks, 3)),
            dma((chunks, seq)),
            dma((chunks, slots, blk)),
            dma((chunks,)),
            dma,
            dma,
            pltpu.SemaphoreType.REGULAR,
        ],
        compiler_params=pltpu.CompilerParams(
            collective_id=0, has_side_effects=True, vmem_limit_bytes=VMEM_MAIN
        ),
    )(doc_lengths, plan, queries, rotated_keys, head_value_rows)

    def plain(placed, extra):
        return placed

    def spilled(active, collective_id, placed, extra):
        got = pl.pallas_call(
            functools.partial(
                spill_kernel, (seq, blk, heads_dev * HEAD_WIDTH, pieces, slots, parts), active
            ),
            out_shape=jax.ShapeDtypeStruct((BLOCK, queries.shape[1]), bf16),
            in_specs=[pl.BlockSpec(memory_space=pl.ANY)],
            out_specs=pl.BlockSpec(memory_space=pl.ANY),
            scratch_shapes=[unit(chunks), dma((chunks,)), dma((chunks, blk)), dma((chunks,))],
            compiler_params=pltpu.CompilerParams(
                collective_id=collective_id, has_side_effects=True, vmem_limit_bytes=VMEM_REST
            ),
        )(extra)
        return pl.pallas_call(
            functools.partial(finish_spilled, slots),
            out_shape=out_shape,
            in_specs=[pl.BlockSpec(memory_space=pltpu.SMEM)]
            + [pl.BlockSpec(memory_space=pl.ANY)] * 2,
            out_specs=hbm,
            scratch_shapes=[dma((slots,))],
            compiler_params=pltpu.CompilerParams(vmem_limit_bytes=VMEM_REST),
        )(plan, placed, got)

    branches = [plain] + [
        functools.partial(spilled, active, 1 + n) for n, active in enumerate((0, 1, None))
    ]
    return lax.switch(flag[0, 0], branches, placed, extra)


def per_device(queries, rotated_keys, head_value_rows, doc_lengths, owner_plan):
    blk = lax.axis_size("blk")
    seq = lax.axis_size("seq")
    heads_dev = queries.shape[1] // HEAD_WIDTH // blk
    heads_per_group = QUERY_HEADS // KEY_HEADS
    groups_kv = max(1, heads_dev // heads_per_group)
    chunk_heads = min(CHUNK_HEADS, heads_dev, heads_per_group)
    chunks = heads_dev // chunk_heads
    slots = seq // blk
    if (seq, blk, lax.axis_size("groups")) == (4, 2, 2) and heads_dev % heads_per_group == 0:
        return quad(queries, rotated_keys, head_value_rows, doc_lengths, owner_plan)
    width = chunk_heads * HEAD_WIDTH
    dims = (seq, blk, heads_dev, groups_kv, heads_per_group, chunk_heads, slots)
    bf16 = jnp.bfloat16
    dma = pltpu.SemaphoreType.DMA
    placed = pl.pallas_call(
        functools.partial(kernel, dims),
        out_shape=jax.ShapeDtypeStruct((slots * BLOCK, queries.shape[1]), bf16),
        in_specs=[pl.BlockSpec(memory_space=pltpu.SMEM)] * 2
        + [pl.BlockSpec(memory_space=pl.ANY)] * 3,
        out_specs=pl.BlockSpec(memory_space=pl.ANY),
        scratch_shapes=[
            pltpu.VMEM((chunks, blk, BLOCK, width), bf16),
            pltpu.VMEM((groups_kv, 2 * blk, BLOCK, HEAD_WIDTH), bf16),
            pltpu.VMEM((groups_kv, 2 * blk, BLOCK, HEAD_WIDTH), bf16),
            pltpu.VMEM((blk, BLOCK, (blk + 1) * BLOCK), jnp.float32),
            pltpu.VMEM((blk + 1, BLOCK, width), bf16),
            pltpu.VMEM((chunks, seq, BLOCK, width), bf16),
            pltpu.VMEM((chunks, seq - 1, BLOCK, width), bf16),
            dma((2 * groups_kv + chunks,)),
            dma((chunks, blk - 1)),
            dma((chunks, blk - 1)),
            dma((groups_kv, 2, blk - 1)),
            dma((groups_kv, 2, blk - 1)),
            dma((groups_kv, 2, blk)),
            dma((groups_kv, 2, blk)),
            dma((chunks, seq - 1)),
            dma((chunks, seq - 1)),
            dma((chunks, seq)),
            dma((chunks, slots, blk)),
        ],
        compiler_params=pltpu.CompilerParams(collective_id=0, has_side_effects=True),
    )(doc_lengths, owner_plan.T, queries, rotated_keys, head_value_rows)
    pieces = PIECES
    return pl.pallas_call(
        functools.partial(settle, pieces),
        out_shape=jax.ShapeDtypeStruct(placed.shape, bf16),
        in_specs=[pl.BlockSpec(memory_space=pl.ANY)],
        out_specs=pl.BlockSpec(memory_space=pl.ANY),
        scratch_shapes=[
            pltpu.VMEM((pieces, placed.shape[0] // pieces, placed.shape[1]), bf16),
            dma((pieces,)),
            dma((pieces,)),
        ],
    )(placed)


def solution(mesh):
    in_specs = (
        P(("groups", "seq", "blk"), "tp"),
        P(("groups", "seq", "blk"), "tp"),
        P(("groups", "seq", "blk"), "tp"),
        P("groups"),
        P("groups", None),
    )
    out_specs = P(("groups", "seq", "blk"), "tp")
    return jax.shard_map(
        per_device, mesh=mesh, in_specs=in_specs, out_specs=out_specs, check_vma=False
    )
```

```python
import functools
import math

import jax
import jax.numpy as jnp
from jax import lax
from jax.experimental import pallas as pl
from jax.experimental.pallas import tpu as pltpu
from jax.sharding import PartitionSpec as P

QUERY_HEADS = 64
KEY_HEADS = 8
HEAD_WIDTH = 128
BLOCK = 128
CHUNK_HEADS = 2
HEAD_SPLIT = (2,)
TAIL_SPLIT = (2,)
PIECES = 8

MESH = pl.DeviceIdType.MESH
masked_score = -1e30
JOIN_LAG = 1
LAGS = (3,3)
KV_EARLY = 2
DETOUR = 2
QUERY_SECOND = 2
DIRECT_HEADS = 0
VMEM_MAIN = 58 * 2**20
QUERY_FIRST = 1
QUERY_LEAD = 2
KV_LEAD = 4
VMEM_REST = 4 * 2**20


def kernel(
    dims,
    lengths_ref,
    plan_ref,
    q_ref,
    k_ref,
    v_ref,
    out_ref,
    q_group,
    k_near,
    v_near,
    bias,
    block_out,
    message,
    landed,
    local_sem,
    q_send,
    q_recv,
    kv_send,
    kv_recv,
    near_send,
    near_recv,
    z_send,
    z_recv,
    x_send,
    x_recv,
):
    seq, blk, heads_dev, groups_kv, heads_per_group, chunk_heads, slots = dims
    g = lax.axis_index("seq")
    b = lax.axis_index("blk")
    chunks = heads_dev // chunk_heads
    width = chunk_heads * HEAD_WIDTH
    columns_dev = heads_dev * HEAD_WIDTH
    window = (blk + 1) * BLOCK
    group_len = blk * BLOCK
    scale = 1.0 / math.sqrt(HEAD_WIDTH)

    def kv_columns(owner, h):
        first = owner * heads_dev // heads_per_group + h
        return pl.ds(pl.multiple_of(first * HEAD_WIDTH, HEAD_WIDTH), HEAD_WIDTH)

    def q_columns(owner, c):
        return pl.ds(pl.multiple_of(owner * columns_dev + c * width, HEAD_WIDTH), width)

    barrier = pltpu.get_barrier_semaphore()
    for e in range(1, blk):
        pl.semaphore_signal(
            barrier, inc=1, device_id={"blk": lax.rem(b + e, blk)}, device_id_type=MESH
        )
    for d in range(1, seq):
        pl.semaphore_signal(
            barrier, inc=1, device_id={"seq": lax.rem(g + d, seq)}, device_id_type=MESH
        )

    pairs = ((k_ref, k_near), (v_ref, v_near))
    own_kv = [
        pltpu.make_async_copy(
            src.at[:, kv_columns(b, h)], dst.at[h, blk + b], local_sem.at[2 * h + i]
        )
        for h in range(groups_kv)
        for i, (src, dst) in enumerate(pairs)
    ]
    own_q = [
        pltpu.make_async_copy(
            q_ref.at[:, q_columns(b, c)], q_group.at[c, b], local_sem.at[2 * groups_kv + c]
        )
        for c in range(chunks)
    ]
    for copy in own_kv + own_q:
        copy.start()

    def kv_copy(h, i, e):
        src, dst = pairs[i]
        peer = lax.rem(b + e, blk)
        return pltpu.make_async_remote_copy(
            src_ref=src.at[:, kv_columns(peer, h)],
            dst_ref=dst.at[h, blk + b],
            send_sem=kv_send.at[h, i, e - 1],
            recv_sem=kv_recv.at[h, i, e - 1],
            device_id={"blk": peer},
            device_id_type=MESH,
        )

    def near_copy(h, i, e):
        src, dst = pairs[i]
        origin = lax.rem(b - e + blk, blk)
        if e == 0:
            source = src.at[:, kv_columns(b, h)]
        else:
            source = dst.at[h, blk + origin]
        return pltpu.make_async_remote_copy(
            src_ref=source,
            dst_ref=dst.at[h, origin],
            send_sem=near_send.at[h, i, e],
            recv_sem=near_recv.at[h, i, e],
            device_id={"seq": lax.rem(g + 1, seq)},
            device_id_type=MESH,
        )

    def q_copy(c, e):
        peer = lax.rem(b + e, blk)
        return pltpu.make_async_remote_copy(
            src_ref=q_ref.at[:, q_columns(peer, c)],
            dst_ref=q_group.at[c, b],
            send_sem=q_send.at[c, e - 1],
            recv_sem=q_recv.at[c, e - 1],
            device_id={"blk": peer},
            device_id_type=MESH,
        )

    for j in range(blk):
        first_row = g * group_len + j * BLOCK
        row_pos = first_row + lax.broadcasted_iota(jnp.int32, (BLOCK, 1), 0)
        end = jnp.int32(0)
        start = jnp.zeros((BLOCK, 1), jnp.int32)
        for n in range(lengths_ref.shape[0]):
            end = end + lengths_ref[n]
            start = jnp.where(row_pos >= end, end, start)
        key_pos = first_row - group_len + lax.broadcasted_iota(jnp.int32, (BLOCK, window), 1)
        allowed = (key_pos >= start) & (key_pos <= row_pos)
        bias[j] = jnp.where(allowed, 0.0, masked_score)
    block_out[blk] = jnp.zeros(block_out.shape[1:], block_out.dtype)

    @pl.when(g == 0)
    def _():
        for h in range(groups_kv):
            for j in range(blk):
                k_near[h, j] = jnp.zeros(k_near.shape[2:], k_near.dtype)
                v_near[h, j] = jnp.zeros(v_near.shape[2:], v_near.dtype)

    pl.semaphore_wait(barrier, blk - 1 + seq - 1)

    def send_kv(h):
        for e in range(1, blk):
            for i in range(2):
                kv_copy(h, i, e).start()

    def send_q(c):
        for e in range(1, blk):
            q_copy(c, e).start()

    def forward_kv(h):
        for e in range(1, blk):
            for i in range(2):
                kv_copy(h, i, e).wait_recv()

        @pl.when(g < seq - 1)
        def _():
            for e in range(1, blk):
                for i in range(2):
                    near_copy(h, i, e).start()

    def wait_near(h):
        @pl.when(g > 0)
        def _():
            for e in range(blk):
                for i in range(2):
                    near_copy(h, i, e).wait_recv()

    send_kv(0)

    @pl.when(g < seq - 1)
    def _():
        for h in range(groups_kv):
            for i in range(2):
                near_copy(h, i, 0).start()

    send_q(0)
    for h in range(1, groups_kv):
        send_kv(h)
    for c in range(1, chunks):
        send_q(c)

    forward_kv(0)
    for copy in own_kv:
        copy.wait()

    half = seq // 2
    side, place_in = g // half, lax.rem(g, half)

    def target(k):
        if k < half:
            return side * half + lax.rem(place_in + k, half)
        return (1 - side) * half + lax.rem(place_in + k - half, half)

    def origin_of(k):
        if k < half:
            return side * half + lax.rem(place_in - k + half, half)
        return (1 - side) * half + lax.rem(place_in - (k - half) + half, half)

    picked = []
    for d in range(seq):
        owner = target(d)
        index = jnp.int32(blk)
        for j in range(blk):
            index = jnp.where(plan_ref[j, g] == owner, jnp.int32(j), index)
        picked.append(index)

    def z_copy(c, d):
        return pltpu.make_async_remote_copy(
            src_ref=message.at[c, d],
            dst_ref=landed.at[c, d - 1],
            send_sem=z_send.at[c, d - 1],
            recv_sem=z_recv.at[c, d - 1],
            device_id={"seq": target(d)},
            device_id_type=MESH,
        )

    near, far = list(range(1, half)), list(range(half, seq))
    sends = [[] for _ in range(chunks)]
    for c in range(chunks):
        if c > 0:
            sends[c] += [(c, k) for k in near]
        if c in (0, chunks - 1):
            sends[c] += [(m, k) for m in range(max(c - 1, min(c, 1)), c + 1) for k in far]
        elif c > 1:
            sends[c] += [(c - 1, k) for k in far]
        if c == 0:
            sends[c] += [(c, k) for k in near]
    arrivals = [message for row in sends for message in row]
    for c in range(chunks):
        own_q[c].wait()
        for e in range(1, blk):
            q_copy(c, e).wait_recv()
        kv_head = c * chunk_heads // heads_per_group
        if c * chunk_heads % heads_per_group == 0 or c == 0:
            wait_near(kv_head)
        for j in range(blk):
            query = q_group[c, j]
            rows = jnp.concatenate(
                [query[:, h * HEAD_WIDTH : (h + 1) * HEAD_WIDTH] for h in range(chunk_heads)], axis=0
            )
            keys = k_near[kv_head, j : j + blk + 1].reshape(window, HEAD_WIDTH)
            values = v_near[kv_head, j : j + blk + 1].reshape(window, HEAD_WIDTH)
            scores = lax.dot_general(
                rows, keys, (((1,), (1,)), ((), ())), preferred_element_type=jnp.float32
            )
            scores = scores.reshape(chunk_heads, BLOCK, window) * scale + bias[j][None]
            top = jnp.max(scores, axis=2, keepdims=True)
            weights = jnp.exp(scores - top)
            total = jnp.sum(weights, axis=2, keepdims=True)
            mixed = jnp.dot(
                weights.astype(jnp.bfloat16).reshape(chunk_heads * BLOCK, window),
                values,
                preferred_element_type=jnp.float32,
            ).reshape(chunk_heads, BLOCK, HEAD_WIDTH)
            result = (mixed / total).astype(jnp.bfloat16)
            for h in range(chunk_heads):
                block_out[j, :, h * HEAD_WIDTH : (h + 1) * HEAD_WIDTH] = result[h]
        for d in range(seq):
            message[c, d] = block_out[picked[d]]
        for m, k in sends[c]:
            z_copy(m, k).start()
        if c == 0:
            for h in range(1, groups_kv):
                forward_kv(h)

    def place(c, d, waiting):
        origin = origin_of(d)
        source = message.at[c, 0] if d == 0 else landed.at[c, d - 1]
        holder = origin // slots
        slot = lax.rem(origin, slots)
        target = out_ref.at[
            pl.ds(pl.multiple_of(slot * BLOCK, BLOCK), BLOCK), q_columns(b, c)
        ]
        hop = lax.rem(holder - b + blk, blk)

        @pl.when(holder == b)
        def _():
            copy = pltpu.make_async_copy(source, target, x_send.at[c, d])
            if waiting:
                copy.wait()
            else:
                copy.start()

        @pl.when(holder != b)
        def _():
            copy = pltpu.make_async_remote_copy(
                src_ref=source,
                dst_ref=target,
                send_sem=x_send.at[c, d],
                recv_sem=x_recv.at[c, slot, lax.rem(hop - 1 + blk, blk)],
                device_id={"blk": holder},
                device_id_type=MESH,
            )
            if waiting:
                copy.wait_send()
            else:
                copy.start()

    for c in range(chunks):
        place(c, 0, False)
    for c, d in arrivals:
        z_copy(c, d).wait_recv()
        place(c, d, False)

    for c in range(chunks):
        for s in range(slots):
            for e in range(1, blk):
                sender = lax.rem(b - e + blk, blk)
                pltpu.make_async_remote_copy(
                    src_ref=message.at[c, 0],
                    dst_ref=out_ref.at[s * BLOCK : (s + 1) * BLOCK, q_columns(sender, c)],
                    send_sem=x_send.at[c, 0],
                    recv_sem=x_recv.at[c, s, e - 1],
                    device_id={"blk": sender},
                    device_id_type=MESH,
                ).wait_recv()
        for d in range(seq):
            place(c, d, True)
            if d > 0:
                z_copy(c, d).wait_send()
        for e in range(1, blk):
            q_copy(c, e).wait_send()
    for h in range(groups_kv):
        for i in range(2):
            for e in range(1, blk):
                kv_copy(h, i, e).wait_send()

    @pl.when(g < seq - 1)
    def _():
        for h in range(groups_kv):
            for e in range(blk):
                for i in range(2):
                    near_copy(h, i, e).wait_send()


def settle(pieces, src_ref, dst_ref, held, in_sem, out_sem):
    rows = src_ref.shape[0] // pieces
    taken = [
        pltpu.make_async_copy(src_ref.at[pl.ds(n * rows, rows)], held.at[n], in_sem.at[n])
        for n in range(pieces)
    ]
    put = [
        pltpu.make_async_copy(held.at[n], dst_ref.at[pl.ds(n * rows, rows)], out_sem.at[n])
        for n in range(pieces)
    ]
    for copy in taken:
        copy.start()
    for n in range(pieces):
        taken[n].wait()
        put[n].start()
    for copy in put:
        copy.wait()


def quad_kernel(
    dims,
    lengths_hbm,
    plan_hbm,
    q_ref,
    k_ref,
    v_ref,
    out_ref,
    extra_ref,
    flag_ref,
    q_group,
    k_near,
    v_near,
    bias,
    block_out,
    first,
    second,
    homeward,
    relay,
    spare,
    land_first,
    land_near,
    land_second,
    mine,
    word,
    word_in,
    lengths_ref,
    plan_ref,
    table_sem,
    local_sem,
    q_send,
    q_recv,
    kv_send,
    kv_recv,
    near_send,
    near_recv,
    first_send,
    first_recv,
    second_send,
    near_x_recv,
    second_recv,
    home_send,
    x_send,
    x_recv,
    extra_sem,
    word_send,
    word_recv,
    credit,
):
    seq, blk, heads_dev, groups_kv, heads_per_group, pieces, slots, parts = dims
    g = lax.axis_index("seq")
    b = lax.axis_index("blk")
    part = lax.axis_index("groups")
    tp = lax.axis_index("tp")
    chunks = len(pieces)
    columns_dev = heads_dev * HEAD_WIDTH
    window = (blk + 1) * BLOCK
    group_len = blk * BLOCK
    scale = math.log2(math.e) / math.sqrt(HEAD_WIDTH)

    left = g < 2
    inner = (g == 1) | (g == 2)
    outer = jnp.logical_not(inner)
    far_inner = jnp.where(left, 2, 1)
    far_outer = jnp.where(left, 3, 0)
    near_inner = jnp.where(left, 1, 2)
    near_outer = jnp.where(left, 0, 3)
    peer = 1 - b

    def kv_columns(owner, h):
        start = owner * heads_dev // heads_per_group + h
        return pl.ds(pl.multiple_of(start * HEAD_WIDTH, HEAD_WIDTH), HEAD_WIDTH)

    def q_columns(owner, c):
        start, heads = pieces[c]
        return pl.ds(
            pl.multiple_of(owner * columns_dev + start * HEAD_WIDTH, HEAD_WIDTH),
            heads * HEAD_WIDTH,
        )

    def unit(ref, c, *index):
        return ref.at[(c,) + index + (slice(None), slice(0, pieces[c][1] * HEAD_WIDTH))]

    def chosen(c, index):
        return block_out[index, :, : pieces[c][1] * HEAD_WIDTH]

    def remote(src, dst, send, recv, **where):
        return pltpu.make_async_remote_copy(
            src_ref=src,
            dst_ref=dst,
            send_sem=send,
            recv_sem=recv,
            device_id=where,
            device_id_type=MESH,
        )

    barrier = pltpu.get_barrier_semaphore()
    everyone = [
        {"blk": peer},
        {"groups": lax.rem(part + 1, parts)},
        {"seq": lax.rem(g + 2, seq)},
        {"seq": jnp.where(inner, near_outer, near_inner)},
        {"seq": jnp.where(inner, near_outer, near_inner), "blk": peer},
    ]
    across = [{"seq": far_inner}, {"seq": far_inner, "blk": peer}]

    def greet(devices):
        for device in devices:
            pl.semaphore_signal(barrier, inc=1, device_id=device, device_id_type=MESH)

    greet(everyone)

    @pl.when(inner)
    def _():
        greet(across)

    tables = [
        pltpu.make_async_copy(lengths_hbm, lengths_ref, table_sem.at[0]),
        pltpu.make_async_copy(plan_hbm, plan_ref, table_sem.at[1]),
    ]
    for copy in tables:
        copy.start()
    pairs = ((k_ref, k_near), (v_ref, v_near))
    own_kv = [
        pltpu.make_async_copy(
            src.at[:, kv_columns(b, h)], dst.at[h, blk + b], local_sem.at[2 * h + i]
        )
        for h in range(groups_kv)
        for i, (src, dst) in enumerate(pairs)
    ]
    own_q = [
        pltpu.make_async_copy(
            q_ref.at[:, q_columns(b, c)], unit(q_group, c, b), local_sem.at[2 * groups_kv + c]
        )
        for c in range(chunks)
    ]
    for copy in own_kv + own_q:
        copy.start()

    def kv_copy(h, i):
        src, dst = pairs[i]
        return remote(
            src.at[:, kv_columns(peer, h)],
            dst.at[h, blk + b],
            kv_send.at[h, i],
            kv_recv.at[h, i],
            blk=peer,
        )

    def near_copy(h, i, e):
        src, dst = pairs[i]
        if e == 0:
            source, origin, to = src.at[:, kv_columns(b, h)], b, b
        elif h < DIRECT_HEADS:
            source, origin, to = src.at[:, kv_columns(peer, h)], b, peer
        else:
            source, origin, to = dst.at[h, blk + peer], peer, b
        return remote(
            source,
            dst.at[h, origin],
            near_send.at[h, i, e],
            near_recv.at[h, i, e],
            seq=lax.rem(g + 1, seq),
            blk=to,
        )

    def q_copy(c):
        return remote(
            q_ref.at[:, q_columns(peer, c)],
            unit(q_group, c, b),
            q_send.at[c],
            q_recv.at[c],
            blk=peer,
        )

    @pl.when(g == 0)
    def _():
        for h in range(groups_kv):
            for j in range(blk):
                k_near[h, j] = jnp.zeros(k_near.shape[2:], k_near.dtype)
                v_near[h, j] = jnp.zeros(v_near.shape[2:], v_near.dtype)

    @pl.when(inner)
    def _():
        pl.semaphore_wait(barrier, len(everyone) + len(across))

    @pl.when(outer)
    def _():
        pl.semaphore_wait(barrier, len(everyone))


    def word_copy():
        return remote(word, word_in, word_send, word_recv, groups=lax.rem(part + 1, parts))

    def send_kv(h):
        @pl.when(g < seq - 1)
        def _():
            for e in range(2 if h < DIRECT_HEADS else 1):
                for i in range(2):
                    near_copy(h, i, e).start()

        for i in range(2):
            kv_copy(h, i).start()

    def forward_kv(h):
        for i in range(2):
            kv_copy(h, i).wait_recv()

        if h >= DIRECT_HEADS:

            @pl.when(g < seq - 1)
            def _():
                for i in range(2):
                    near_copy(h, i, 1).start()

    send_kv(0)
    for c in range(QUERY_FIRST):
        q_copy(c).start()

    for copy in tables:
        copy.wait()

    def has(group, owner):
        return (plan_ref[0, group] == owner) | (plan_ref[1, group] == owner)

    def pick(owner):
        return jnp.where(
            plan_ref[0, g] == owner,
            jnp.int32(0),
            jnp.where(plan_ref[1, g] == owner, jnp.int32(1), jnp.int32(blk)),
        )

    full_right = has(0, 2) & has(0, 3) & has(1, 2) & has(1, 3)
    full_left = has(3, 1) & has(3, 0) & has(2, 1) & has(2, 0)
    spilled = jnp.where(full_right | full_left, jnp.int32(1), jnp.int32(0))
    word[...] = jnp.full(word.shape, spilled, jnp.int32)

    for j in range(blk):
        first_row = g * group_len + j * BLOCK
        row_pos = first_row + lax.broadcasted_iota(jnp.int32, (BLOCK, 1), 0)
        end = jnp.int32(0)
        start = jnp.zeros((BLOCK, 1), jnp.int32)
        for n in range(lengths_ref.shape[0]):
            end = end + lengths_ref[n]
            start = jnp.where(row_pos >= end, end, start)
        key_pos = first_row - group_len + lax.broadcasted_iota(jnp.int32, (BLOCK, window), 1)
        allowed = (key_pos >= start) & (key_pos <= row_pos)
        bias[j] = jnp.where(allowed, 0.0, masked_score)
    block_out[blk] = jnp.zeros(block_out.shape[1:], block_out.dtype)

    forward_kv(0)
    for c in range(QUERY_FIRST, QUERY_SECOND):
        q_copy(c).start()
    if KV_EARLY:
        send_kv(1)
    word_copy().start()
    for copy in own_kv:
        copy.wait()

    sender = jnp.where(inner, 1, 0)

    def first_copy(c, which):
        return remote(
            unit(first, c),
            unit(land_first, c, which),
            first_send.at[c],
            first_recv.at[c, which],
            seq=far_inner,
        )

    def to_near(c):
        return remote(
            unit(second, c), unit(land_near, c), second_send.at[c], near_x_recv.at[c], seq=near_inner
        )

    def to_far(c):
        return remote(
            unit(second, c), unit(land_second, c), second_send.at[c], second_recv.at[c], seq=far_inner
        )

    def out_rows(group, half, c):
        slot = lax.rem(group, slots)
        return out_ref.at[
            pl.ds(pl.multiple_of(slot * BLOCK, BLOCK), BLOCK), q_columns(half, c)
        ]

    def home_copy(c, k):
        source = unit(homeward, c) if k == 0 else unit(relay, c, k - 1)
        group = (near_inner, far_inner, far_outer)[k]
        return remote(
            source,
            out_rows(group, b, c),
            home_send.at[c, k],
            x_recv.at[c, lax.rem(group, slots), b],
            seq=near_outer,
            blk=group // slots,
        )

    def extra_copy(c):
        return pltpu.make_async_copy(unit(spare, c), unit(extra_ref, c), extra_sem.at[c])

    def place(c, group, waiting):
        source = unit(mine, c, group)
        holder = group // slots
        target = out_rows(group, b, c)

        @pl.when(holder == b)
        def _():
            copy = pltpu.make_async_copy(source, target, x_send.at[c, group])
            if waiting:
                copy.wait()
            else:
                copy.start()

        @pl.when(holder != b)
        def _():
            copy = remote(
                source,
                target,
                x_send.at[c, group],
                x_recv.at[c, lax.rem(group, slots), b],
                blk=holder,
            )
            if waiting:
                copy.wait_send()
            else:
                copy.start()

    to_inner, to_outer = pick(far_inner), pick(far_outer)
    both = (to_inner < blk) & (to_outer < blk)
    first_index = jnp.where(to_inner < blk, to_inner, to_outer)
    second_index = jnp.where(both, to_outer, jnp.int32(blk))
    near_index = jnp.where(both, to_outer, pick(near_inner))
    home_index, own_index = pick(near_outer), pick(g)

    near_both = has(near_outer, far_inner) & has(near_outer, far_outer)
    near_here = has(near_outer, g)
    a_here, a_on = has(far_outer, g), has(far_outer, near_outer)
    b_here, b_on = has(far_inner, g), has(far_inner, near_outer)

    def attend(c):
        own_q[c].wait()
        q_copy(c).wait_recv()
        for m in range(max(QUERY_SECOND, c and c + QUERY_LEAD), min(c + QUERY_LEAD + 1, chunks)):
            q_copy(m).start()
        begin, chunk_heads = pieces[c]
        kv_head = begin // heads_per_group
        if begin % heads_per_group == 0:

            @pl.when(g > 0)
            def _():
                for e in range(2):
                    for i in range(2):
                        near_copy(kv_head, i, e).wait_recv()

        for j in range(blk):
            query = unit(q_group, c, j)[...]
            rows = jnp.concatenate(
                [query[:, h * HEAD_WIDTH : (h + 1) * HEAD_WIDTH] for h in range(chunk_heads)], axis=0
            )
            keys = k_near[kv_head, j : j + blk + 1].reshape(window, HEAD_WIDTH)
            values = v_near[kv_head, j : j + blk + 1].reshape(window, HEAD_WIDTH)
            scores = lax.dot_general(
                rows, keys, (((1,), (1,)), ((), ())), preferred_element_type=jnp.float32
            )
            scores = scores.reshape(chunk_heads, BLOCK, window) * scale + bias[j][None]
            top = jnp.max(scores, axis=2, keepdims=True)
            weights = jnp.exp2(scores - top)
            total = jnp.sum(weights, axis=2, keepdims=True)
            mixed = jnp.dot(
                weights.astype(jnp.bfloat16).reshape(chunk_heads * BLOCK, window),
                values,
                preferred_element_type=jnp.float32,
            ).reshape(chunk_heads, BLOCK, HEAD_WIDTH)
            result = (mixed / total).astype(jnp.bfloat16)
            for h in range(chunk_heads):
                block_out[j, :, h * HEAD_WIDTH : (h + 1) * HEAD_WIDTH] = result[h]

    def dispatch(c):
        unit(first, c)[...] = chosen(c, first_index)

        @pl.when(outer)
        def _():
            unit(second, c)[...] = chosen(c, near_index)
            to_near(c).start()
            for core, lag in enumerate(LAGS):
                if c >= lag:

                    @pl.when(tp == core)
                    def _():
                        pl.semaphore_wait(credit, 1)


        first_copy(c, sender).start()

        @pl.when(inner)
        def _():
            unit(homeward, c)[...] = chosen(c, home_index)
            home_copy(c, 0).start()
            unit(spare, c)[...] = chosen(c, second_index)
            extra_copy(c).start()

        unit(mine, c, g)[...] = chosen(c, own_index)
        place(c, g, False)

    def join(c):
        to_near(c).wait_recv()
        arrived = unit(land_near, c)[...]
        unit(second, c)[...] = jnp.where(near_both, arrived, unit(spare, c)[...])
        to_far(c).start()
        unit(mine, c, near_outer)[...] = jnp.where(near_here, arrived, jnp.zeros_like(arrived))
        place(c, near_outer, False)

    def spread(c, lag):
        first_copy(c, 1).wait_recv()
        from_inner = unit(land_first, c, 1)[...]
        nothing = jnp.zeros_like(from_inner)
        unit(mine, c, far_inner)[...] = jnp.where(b_here, from_inner, nothing)
        place(c, far_inner, False)
        first_copy(c, 0).wait_recv()
        from_outer = unit(land_first, c, 0)[...]
        unit(mine, c, far_outer)[...] = jnp.where(a_here, from_outer, nothing)
        place(c, far_outer, False)
        to_far(c).wait_recv()
        if c + lag < chunks:
            pl.semaphore_signal(
                credit, inc=1, device_id={"seq": far_outer}, device_id_type=MESH
            )
        last = unit(land_second, c)[...]
        unit(relay, c, 1)[...] = jnp.where(a_on, jnp.where(a_here, last, from_outer), nothing)
        home_copy(c, 2).start()
        rest = jnp.where(a_here & a_on, nothing, last)
        unit(relay, c, 0)[...] = jnp.where(b_on, jnp.where(b_here, rest, from_inner), nothing)
        home_copy(c, 1).start()

    def landed(c, s, half):
        remote(
            unit(mine, c, 0),
            out_rows(b * slots + s, half, c),
            x_send.at[c, 0],
            x_recv.at[c, s, half],
            blk=peer,
        ).wait_recv()

    for t in range(chunks + max(JOIN_LAG, *LAGS)):
        if t < chunks:
            attend(t)
            dispatch(t)
            if KV_EARLY and t == KV_EARLY - 1:
                forward_kv(1)
            for h in range(2 if KV_EARLY else 1, groups_kv):
                start = [begin for begin, _ in pieces].index(h * heads_per_group)
                if t == start - KV_LEAD:
                    send_kv(h)
                if t == start - KV_LEAD + 1:
                    forward_kv(h)

        @pl.when(inner)
        def _():
            if 0 <= t - JOIN_LAG < chunks:
                join(t - JOIN_LAG)

        for core, lag in enumerate(LAGS):
            if 0 <= t - lag < chunks:

                @pl.when(inner & (tp == core))
                def _():
                    spread(t - lag, lag)

    word_copy().wait()
    flag_ref[0, 0] = spilled * (1 + part) + jnp.max(word_in[...]) * (2 - part)

    for h in range(groups_kv):
        for i in range(2):
            kv_copy(h, i).wait_send()

    @pl.when(g < seq - 1)
    def _():
        for h in range(groups_kv):
            for e in range(2):
                for i in range(2):
                    near_copy(h, i, e).wait_send()

    for c in range(chunks):
        q_copy(c).wait_send()
        first_copy(c, sender).wait_send()

        @pl.when(outer)
        def _():
            to_near(c).wait_send()

        @pl.when(inner)
        def _():
            to_far(c).wait_send()
            extra_copy(c).wait()
            for k in range(3):
                home_copy(c, k).wait_send()
            for group in (near_outer, far_inner, far_outer):
                place(c, group, True)

        place(c, g, True)
        for s in range(slots):
            landed(c, s, peer)

            @pl.when(outer & (b * slots + s != g))
            def _():
                landed(c, s, b)


def spill_kernel(dims, active, extra_ref, got_ref, via, send, recv, via_recv):
    seq, blk, columns_dev, pieces, slots, parts = dims
    chunks = len(pieces)
    part = lax.axis_index("groups")
    g = lax.axis_index("seq")
    b = lax.axis_index("blk")
    inner = (g == 1) | (g == 2)
    mate = lax.rem(g + 2, seq)
    other = lax.rem(part + 1, parts)
    direct = chunks if active is None else chunks - DETOUR
    barrier = pltpu.get_barrier_semaphore()
    greeted = [{"seq": mate, "blk": e} for e in range(blk)]
    greeted += [{"groups": other, "seq": mate, "blk": e} for e in range(blk)]
    greeted += [{"groups": other}]
    for device in greeted:
        pl.semaphore_signal(barrier, inc=1, device_id=device, device_id_type=MESH)
    pl.semaphore_wait(barrier, len(greeted))

    def spill(c, half, holder, source, owner_part):
        start, width = pieces[c][0] * HEAD_WIDTH, pieces[c][1] * HEAD_WIDTH
        return pltpu.make_async_remote_copy(
            src_ref=source.at[c, :, :width],
            dst_ref=got_ref.at[
                :, pl.ds(pl.multiple_of(half * columns_dev + start, HEAD_WIDTH), width)
            ],
            send_sem=send.at[c],
            recv_sem=recv.at[c, half],
            device_id={"groups": owner_part, "seq": mate, "blk": holder},
            device_id_type=MESH,
        )

    def to_side(c):
        return pltpu.make_async_remote_copy(
            src_ref=extra_ref.at[c],
            dst_ref=via.at[c],
            send_sem=send.at[c],
            recv_sem=via_recv.at[c],
            device_id={"groups": other},
            device_id_type=MESH,
        )

    mine = part < parts if active is None else part == active

    @pl.when(mine & inner)
    def _():
        for c in range(direct, chunks):
            to_side(c).start()
        for c in range(direct):
            spill(c, b, g // slots, extra_ref, part).start()
        for c in range(direct, chunks):
            to_side(c).wait_send()
        for c in range(direct):
            spill(c, b, g // slots, extra_ref, part).wait_send()

    @pl.when(jnp.logical_not(mine) & inner)
    def _():
        for c in range(direct, chunks):
            to_side(c).wait_recv()
            spill(c, b, g // slots, via, other).start()
        for c in range(direct, chunks):
            spill(c, b, g // slots, via, other).wait_send()

    @pl.when(mine & jnp.logical_not(inner) & (b == mate // slots))
    def _():
        for c in range(chunks):
            for half in range(blk):
                spill(c, half, b, extra_ref, part).wait_recv()


def finish_spilled(slots, plan_ref, placed_ref, got_ref, dst_ref, sem):
    owner = lax.axis_index("seq")
    b = lax.axis_index("blk")

    def has(group, wanted):
        return (plan_ref[0, group] == wanted) | (plan_ref[1, group] == wanted)

    full_right = has(0, 2) & has(0, 3) & has(1, 2) & has(1, 3)
    full_left = has(3, 1) & has(3, 0) & has(2, 1) & has(2, 0)
    for s in range(slots):
        group = b * slots + s
        rows = pl.ds(s * BLOCK, BLOCK)
        spilled = ((group == 1) & (owner == 3) & full_right) | (
            (group == 2) & (owner == 0) & full_left
        )

        @pl.when(spilled)
        def _():
            copy = pltpu.make_async_copy(got_ref, dst_ref.at[rows], sem.at[s])
            copy.start()
            copy.wait()


def quad(queries, rotated_keys, head_value_rows, doc_lengths, owner_plan):
    blk = lax.axis_size("blk")
    seq = lax.axis_size("seq")
    parts = lax.axis_size("groups")
    heads_dev = queries.shape[1] // HEAD_WIDTH // blk
    heads_per_group = QUERY_HEADS // KEY_HEADS
    groups_kv = heads_dev // heads_per_group
    sizes = []
    for h in range(groups_kv):
        row = [CHUNK_HEADS] * (heads_per_group // CHUNK_HEADS)
        if h == 0:
            row = list(HEAD_SPLIT) + row[1:]
        if h == groups_kv - 1:
            row = row[:-1] + list(TAIL_SPLIT)
        sizes += row
    pieces = [(sum(sizes[:c]), sizes[c]) for c in range(len(sizes))]
    chunks = len(pieces)
    slots = seq // blk
    width = max(sizes) * HEAD_WIDTH
    dims = (seq, blk, heads_dev, groups_kv, heads_per_group, pieces, slots, parts)
    bf16 = jnp.bfloat16
    dma = pltpu.SemaphoreType.DMA
    hbm = pl.BlockSpec(memory_space=pltpu.HBM)
    plan = owner_plan.T
    out_shape = jax.ShapeDtypeStruct((slots * BLOCK, queries.shape[1]), bf16)

    def unit(*lead):
        return pltpu.VMEM(lead + (BLOCK, width), bf16)

    placed, extra, flag = pl.pallas_call(
        functools.partial(quad_kernel, dims),
        out_shape=(
            out_shape,
            jax.ShapeDtypeStruct((chunks, BLOCK, width), bf16),
            jax.ShapeDtypeStruct((1, 1), jnp.int32),
        ),
        in_specs=[hbm] * 5,
        out_specs=(
            pl.BlockSpec(memory_space=pl.ANY),
            pl.BlockSpec(memory_space=pl.ANY),
            pl.BlockSpec(memory_space=pltpu.SMEM),
        ),
        scratch_shapes=[
            unit(chunks, blk),
            pltpu.VMEM((groups_kv, 2 * blk, BLOCK, HEAD_WIDTH), bf16),
            pltpu.VMEM((groups_kv, 2 * blk, BLOCK, HEAD_WIDTH), bf16),
            pltpu.VMEM((blk, BLOCK, (blk + 1) * BLOCK), jnp.float32),
            unit(blk + 1),
            unit(chunks),
            unit(chunks),
            unit(chunks),
            unit(chunks, 2),
            unit(chunks),
            unit(chunks, 2),
            unit(chunks),
            unit(chunks),
            unit(chunks, seq),
            pltpu.VMEM((8, 128), jnp.int32),
            pltpu.VMEM((8, 128), jnp.int32),
            pltpu.SMEM(doc_lengths.shape, jnp.int32),
            pltpu.SMEM(plan.shape, jnp.int32),
            dma((2,)),
            dma((2 * groups_kv + chunks,)),
            dma((chunks,)),
            dma((chunks,)),
            dma((groups_kv, 2)),
            dma((groups_kv, 2)),
            dma((groups_kv, 2, 2)),
            dma((groups_kv, 2, 2)),
            dma((chunks,)),
            dma((chunks, 2)),
            dma((chunks,)),
            dma((chunks,)),
            dma((chunks,)),
            dma((chunks, 3)),
            dma((chunks, seq)),
            dma((chunks, slots, blk)),
            dma((chunks,)),
            dma,
            dma,
            pltpu.SemaphoreType.REGULAR,
        ],
        compiler_params=pltpu.CompilerParams(
            collective_id=0, has_side_effects=True, vmem_limit_bytes=VMEM_MAIN
        ),
    )(doc_lengths, plan, queries, rotated_keys, head_value_rows)

    def plain(placed, extra):
        return placed

    def spilled(active, collective_id, placed, extra):
        got = pl.pallas_call(
            functools.partial(
                spill_kernel, (seq, blk, heads_dev * HEAD_WIDTH, pieces, slots, parts), active
            ),
            out_shape=jax.ShapeDtypeStruct((BLOCK, queries.shape[1]), bf16),
            in_specs=[pl.BlockSpec(memory_space=pl.ANY)],
            out_specs=pl.BlockSpec(memory_space=pl.ANY),
            scratch_shapes=[unit(chunks), dma((chunks,)), dma((chunks, blk)), dma((chunks,))],
            compiler_params=pltpu.CompilerParams(
                collective_id=collective_id, has_side_effects=True, vmem_limit_bytes=VMEM_REST
            ),
        )(extra)
        return pl.pallas_call(
            functools.partial(finish_spilled, slots),
            out_shape=out_shape,
            in_specs=[pl.BlockSpec(memory_space=pltpu.SMEM)]
            + [pl.BlockSpec(memory_space=pl.ANY)] * 2,
            out_specs=pl.BlockSpec(memory_space=pl.ANY),
            scratch_shapes=[dma((slots,))],
            input_output_aliases={1: 0},
            compiler_params=pltpu.CompilerParams(vmem_limit_bytes=VMEM_REST),
        )(plan, placed, got)

    branches = [plain] + [
        functools.partial(spilled, active, 1 + n) for n, active in enumerate((0, 1, None))
    ]
    return lax.switch(flag[0, 0], branches, placed, extra)


def per_device(queries, rotated_keys, head_value_rows, doc_lengths, owner_plan):
    blk = lax.axis_size("blk")
    seq = lax.axis_size("seq")
    heads_dev = queries.shape[1] // HEAD_WIDTH // blk
    heads_per_group = QUERY_HEADS // KEY_HEADS
    groups_kv = max(1, heads_dev // heads_per_group)
    chunk_heads = min(CHUNK_HEADS, heads_dev, heads_per_group)
    chunks = heads_dev // chunk_heads
    slots = seq // blk
    if (seq, blk, lax.axis_size("groups")) == (4, 2, 2) and heads_dev % heads_per_group == 0:
        return quad(queries, rotated_keys, head_value_rows, doc_lengths, owner_plan)
    width = chunk_heads * HEAD_WIDTH
    dims = (seq, blk, heads_dev, groups_kv, heads_per_group, chunk_heads, slots)
    bf16 = jnp.bfloat16
    dma = pltpu.SemaphoreType.DMA
    placed = pl.pallas_call(
        functools.partial(kernel, dims),
        out_shape=jax.ShapeDtypeStruct((slots * BLOCK, queries.shape[1]), bf16),
        in_specs=[pl.BlockSpec(memory_space=pltpu.SMEM)] * 2
        + [pl.BlockSpec(memory_space=pl.ANY)] * 3,
        out_specs=pl.BlockSpec(memory_space=pl.ANY),
        scratch_shapes=[
            pltpu.VMEM((chunks, blk, BLOCK, width), bf16),
            pltpu.VMEM((groups_kv, 2 * blk, BLOCK, HEAD_WIDTH), bf16),
            pltpu.VMEM((groups_kv, 2 * blk, BLOCK, HEAD_WIDTH), bf16),
            pltpu.VMEM((blk, BLOCK, (blk + 1) * BLOCK), jnp.float32),
            pltpu.VMEM((blk + 1, BLOCK, width), bf16),
            pltpu.VMEM((chunks, seq, BLOCK, width), bf16),
            pltpu.VMEM((chunks, seq - 1, BLOCK, width), bf16),
            dma((2 * groups_kv + chunks,)),
            dma((chunks, blk - 1)),
            dma((chunks, blk - 1)),
            dma((groups_kv, 2, blk - 1)),
            dma((groups_kv, 2, blk - 1)),
            dma((groups_kv, 2, blk)),
            dma((groups_kv, 2, blk)),
            dma((chunks, seq - 1)),
            dma((chunks, seq - 1)),
            dma((chunks, seq)),
            dma((chunks, slots, blk)),
        ],
        compiler_params=pltpu.CompilerParams(collective_id=0, has_side_effects=True),
    )(doc_lengths, owner_plan.T, queries, rotated_keys, head_value_rows)
    pieces = PIECES
    return pl.pallas_call(
        functools.partial(settle, pieces),
        out_shape=jax.ShapeDtypeStruct(placed.shape, bf16),
        in_specs=[pl.BlockSpec(memory_space=pl.ANY)],
        out_specs=pl.BlockSpec(memory_space=pl.ANY),
        scratch_shapes=[
            pltpu.VMEM((pieces, placed.shape[0] // pieces, placed.shape[1]), bf16),
            dma((pieces,)),
            dma((pieces,)),
        ],
    )(placed)


def solution(mesh):
    in_specs = (
        P(("groups", "seq", "blk"), "tp"),
        P(("groups", "seq", "blk"), "tp"),
        P(("groups", "seq", "blk"), "tp"),
        P("groups"),
        P("groups", None),
    )
    out_specs = P(("groups", "seq", "blk"), "tp")
    return jax.shard_map(
        per_device, mesh=mesh, in_specs=in_specs, out_specs=out_specs, check_vma=False
    )
```

```python
import functools
import math

import jax
import jax.numpy as jnp
from jax import lax
from jax.experimental import pallas as pl
from jax.experimental.pallas import tpu as pltpu
from jax.sharding import PartitionSpec as P

QUERY_HEADS = 64
KEY_HEADS = 8
HEAD_WIDTH = 128
BLOCK = 128
CHUNK_HEADS = 2
HEAD_SPLIT = (2,)
TAIL_SPLIT = (2,)
PIECES = 8

MESH = pl.DeviceIdType.MESH
masked_score = -1e30
JOIN_LAG = 1
LAGS = (3,3)
KV_EARLY = 3
DETOUR = 2
QUERY_SECOND = 2
DIRECT_HEADS = 0
VMEM_MAIN = 58 * 2**20
QUERY_FIRST = 1
QUERY_LEAD = 2
KV_LEAD = 4
VMEM_REST = 4 * 2**20


def kernel(
    dims,
    lengths_ref,
    plan_ref,
    q_ref,
    k_ref,
    v_ref,
    out_ref,
    q_group,
    k_near,
    v_near,
    bias,
    block_out,
    message,
    landed,
    local_sem,
    q_send,
    q_recv,
    kv_send,
    kv_recv,
    near_send,
    near_recv,
    z_send,
    z_recv,
    x_send,
    x_recv,
):
    seq, blk, heads_dev, groups_kv, heads_per_group, chunk_heads, slots = dims
    g = lax.axis_index("seq")
    b = lax.axis_index("blk")
    chunks = heads_dev // chunk_heads
    width = chunk_heads * HEAD_WIDTH
    columns_dev = heads_dev * HEAD_WIDTH
    window = (blk + 1) * BLOCK
    group_len = blk * BLOCK
    scale = 1.0 / math.sqrt(HEAD_WIDTH)

    def kv_columns(owner, h):
        first = owner * heads_dev // heads_per_group + h
        return pl.ds(pl.multiple_of(first * HEAD_WIDTH, HEAD_WIDTH), HEAD_WIDTH)

    def q_columns(owner, c):
        return pl.ds(pl.multiple_of(owner * columns_dev + c * width, HEAD_WIDTH), width)

    barrier = pltpu.get_barrier_semaphore()
    for e in range(1, blk):
        pl.semaphore_signal(
            barrier, inc=1, device_id={"blk": lax.rem(b + e, blk)}, device_id_type=MESH
        )
    for d in range(1, seq):
        pl.semaphore_signal(
            barrier, inc=1, device_id={"seq": lax.rem(g + d, seq)}, device_id_type=MESH
        )

    pairs = ((k_ref, k_near), (v_ref, v_near))
    own_kv = [
        pltpu.make_async_copy(
            src.at[:, kv_columns(b, h)], dst.at[h, blk + b], local_sem.at[2 * h + i]
        )
        for h in range(groups_kv)
        for i, (src, dst) in enumerate(pairs)
    ]
    own_q = [
        pltpu.make_async_copy(
            q_ref.at[:, q_columns(b, c)], q_group.at[c, b], local_sem.at[2 * groups_kv + c]
        )
        for c in range(chunks)
    ]
    for copy in own_kv + own_q:
        copy.start()

    def kv_copy(h, i, e):
        src, dst = pairs[i]
        peer = lax.rem(b + e, blk)
        return pltpu.make_async_remote_copy(
            src_ref=src.at[:, kv_columns(peer, h)],
            dst_ref=dst.at[h, blk + b],
            send_sem=kv_send.at[h, i, e - 1],
            recv_sem=kv_recv.at[h, i, e - 1],
            device_id={"blk": peer},
            device_id_type=MESH,
        )

    def near_copy(h, i, e):
        src, dst = pairs[i]
        origin = lax.rem(b - e + blk, blk)
        if e == 0:
            source = src.at[:, kv_columns(b, h)]
        else:
            source = dst.at[h, blk + origin]
        return pltpu.make_async_remote_copy(
            src_ref=source,
            dst_ref=dst.at[h, origin],
            send_sem=near_send.at[h, i, e],
            recv_sem=near_recv.at[h, i, e],
            device_id={"seq": lax.rem(g + 1, seq)},
            device_id_type=MESH,
        )

    def q_copy(c, e):
        peer = lax.rem(b + e, blk)
        return pltpu.make_async_remote_copy(
            src_ref=q_ref.at[:, q_columns(peer, c)],
            dst_ref=q_group.at[c, b],
            send_sem=q_send.at[c, e - 1],
            recv_sem=q_recv.at[c, e - 1],
            device_id={"blk": peer},
            device_id_type=MESH,
        )

    for j in range(blk):
        first_row = g * group_len + j * BLOCK
        row_pos = first_row + lax.broadcasted_iota(jnp.int32, (BLOCK, 1), 0)
        end = jnp.int32(0)
        start = jnp.zeros((BLOCK, 1), jnp.int32)
        for n in range(lengths_ref.shape[0]):
            end = end + lengths_ref[n]
            start = jnp.where(row_pos >= end, end, start)
        key_pos = first_row - group_len + lax.broadcasted_iota(jnp.int32, (BLOCK, window), 1)
        allowed = (key_pos >= start) & (key_pos <= row_pos)
        bias[j] = jnp.where(allowed, 0.0, masked_score)
    block_out[blk] = jnp.zeros(block_out.shape[1:], block_out.dtype)

    @pl.when(g == 0)
    def _():
        for h in range(groups_kv):
            for j in range(blk):
                k_near[h, j] = jnp.zeros(k_near.shape[2:], k_near.dtype)
                v_near[h, j] = jnp.zeros(v_near.shape[2:], v_near.dtype)

    pl.semaphore_wait(barrier, blk - 1 + seq - 1)

    def send_kv(h):
        for e in range(1, blk):
            for i in range(2):
                kv_copy(h, i, e).start()

    def send_q(c):
        for e in range(1, blk):
            q_copy(c, e).start()

    def forward_kv(h):
        for e in range(1, blk):
            for i in range(2):
                kv_copy(h, i, e).wait_recv()

        @pl.when(g < seq - 1)
        def _():
            for e in range(1, blk):
                for i in range(2):
                    near_copy(h, i, e).start()

    def wait_near(h):
        @pl.when(g > 0)
        def _():
            for e in range(blk):
                for i in range(2):
                    near_copy(h, i, e).wait_recv()

    send_kv(0)

    @pl.when(g < seq - 1)
    def _():
        for h in range(groups_kv):
            for i in range(2):
                near_copy(h, i, 0).start()

    send_q(0)
    for h in range(1, groups_kv):
        send_kv(h)
    for c in range(1, chunks):
        send_q(c)

    forward_kv(0)
    for copy in own_kv:
        copy.wait()

    half = seq // 2
    side, place_in = g // half, lax.rem(g, half)

    def target(k):
        if k < half:
            return side * half + lax.rem(place_in + k, half)
        return (1 - side) * half + lax.rem(place_in + k - half, half)

    def origin_of(k):
        if k < half:
            return side * half + lax.rem(place_in - k + half, half)
        return (1 - side) * half + lax.rem(place_in - (k - half) + half, half)

    picked = []
    for d in range(seq):
        owner = target(d)
        index = jnp.int32(blk)
        for j in range(blk):
            index = jnp.where(plan_ref[j, g] == owner, jnp.int32(j), index)
        picked.append(index)

    def z_copy(c, d):
        return pltpu.make_async_remote_copy(
            src_ref=message.at[c, d],
            dst_ref=landed.at[c, d - 1],
            send_sem=z_send.at[c, d - 1],
            recv_sem=z_recv.at[c, d - 1],
            device_id={"seq": target(d)},
            device_id_type=MESH,
        )

    near, far = list(range(1, half)), list(range(half, seq))
    sends = [[] for _ in range(chunks)]
    for c in range(chunks):
        if c > 0:
            sends[c] += [(c, k) for k in near]
        if c in (0, chunks - 1):
            sends[c] += [(m, k) for m in range(max(c - 1, min(c, 1)), c + 1) for k in far]
        elif c > 1:
            sends[c] += [(c - 1, k) for k in far]
        if c == 0:
            sends[c] += [(c, k) for k in near]
    arrivals = [message for row in sends for message in row]
    for c in range(chunks):
        own_q[c].wait()
        for e in range(1, blk):
            q_copy(c, e).wait_recv()
        kv_head = c * chunk_heads // heads_per_group
        if c * chunk_heads % heads_per_group == 0 or c == 0:
            wait_near(kv_head)
        for j in range(blk):
            query = q_group[c, j]
            rows = jnp.concatenate(
                [query[:, h * HEAD_WIDTH : (h + 1) * HEAD_WIDTH] for h in range(chunk_heads)], axis=0
            )
            keys = k_near[kv_head, j : j + blk + 1].reshape(window, HEAD_WIDTH)
            values = v_near[kv_head, j : j + blk + 1].reshape(window, HEAD_WIDTH)
            scores = lax.dot_general(
                rows, keys, (((1,), (1,)), ((), ())), preferred_element_type=jnp.float32
            )
            scores = scores.reshape(chunk_heads, BLOCK, window) * scale + bias[j][None]
            top = jnp.max(scores, axis=2, keepdims=True)
            weights = jnp.exp(scores - top)
            total = jnp.sum(weights, axis=2, keepdims=True)
            mixed = jnp.dot(
                weights.astype(jnp.bfloat16).reshape(chunk_heads * BLOCK, window),
                values,
                preferred_element_type=jnp.float32,
            ).reshape(chunk_heads, BLOCK, HEAD_WIDTH)
            result = (mixed / total).astype(jnp.bfloat16)
            for h in range(chunk_heads):
                block_out[j, :, h * HEAD_WIDTH : (h + 1) * HEAD_WIDTH] = result[h]
        for d in range(seq):
            message[c, d] = block_out[picked[d]]
        for m, k in sends[c]:
            z_copy(m, k).start()
        if c == 0:
            for h in range(1, groups_kv):
                forward_kv(h)

    def place(c, d, waiting):
        origin = origin_of(d)
        source = message.at[c, 0] if d == 0 else landed.at[c, d - 1]
        holder = origin // slots
        slot = lax.rem(origin, slots)
        target = out_ref.at[
            pl.ds(pl.multiple_of(slot * BLOCK, BLOCK), BLOCK), q_columns(b, c)
        ]
        hop = lax.rem(holder - b + blk, blk)

        @pl.when(holder == b)
        def _():
            copy = pltpu.make_async_copy(source, target, x_send.at[c, d])
            if waiting:
                copy.wait()
            else:
                copy.start()

        @pl.when(holder != b)
        def _():
            copy = pltpu.make_async_remote_copy(
                src_ref=source,
                dst_ref=target,
                send_sem=x_send.at[c, d],
                recv_sem=x_recv.at[c, slot, lax.rem(hop - 1 + blk, blk)],
                device_id={"blk": holder},
                device_id_type=MESH,
            )
            if waiting:
                copy.wait_send()
            else:
                copy.start()

    for c in range(chunks):
        place(c, 0, False)
    for c, d in arrivals:
        z_copy(c, d).wait_recv()
        place(c, d, False)

    for c in range(chunks):
        for s in range(slots):
            for e in range(1, blk):
                sender = lax.rem(b - e + blk, blk)
                pltpu.make_async_remote_copy(
                    src_ref=message.at[c, 0],
                    dst_ref=out_ref.at[s * BLOCK : (s + 1) * BLOCK, q_columns(sender, c)],
                    send_sem=x_send.at[c, 0],
                    recv_sem=x_recv.at[c, s, e - 1],
                    device_id={"blk": sender},
                    device_id_type=MESH,
                ).wait_recv()
        for d in range(seq):
            place(c, d, True)
            if d > 0:
                z_copy(c, d).wait_send()
        for e in range(1, blk):
            q_copy(c, e).wait_send()
    for h in range(groups_kv):
        for i in range(2):
            for e in range(1, blk):
                kv_copy(h, i, e).wait_send()

    @pl.when(g < seq - 1)
    def _():
        for h in range(groups_kv):
            for e in range(blk):
                for i in range(2):
                    near_copy(h, i, e).wait_send()


def settle(pieces, src_ref, dst_ref, held, in_sem, out_sem):
    rows = src_ref.shape[0] // pieces
    taken = [
        pltpu.make_async_copy(src_ref.at[pl.ds(n * rows, rows)], held.at[n], in_sem.at[n])
        for n in range(pieces)
    ]
    put = [
        pltpu.make_async_copy(held.at[n], dst_ref.at[pl.ds(n * rows, rows)], out_sem.at[n])
        for n in range(pieces)
    ]
    for copy in taken:
        copy.start()
    for n in range(pieces):
        taken[n].wait()
        put[n].start()
    for copy in put:
        copy.wait()


def quad_kernel(
    dims,
    lengths_hbm,
    plan_hbm,
    q_ref,
    k_ref,
    v_ref,
    out_ref,
    extra_ref,
    flag_ref,
    q_group,
    k_near,
    v_near,
    bias,
    block_out,
    first,
    second,
    homeward,
    relay,
    spare,
    land_first,
    land_near,
    land_second,
    mine,
    word,
    word_in,
    lengths_ref,
    plan_ref,
    table_sem,
    local_sem,
    q_send,
    q_recv,
    kv_send,
    kv_recv,
    near_send,
    near_recv,
    first_send,
    first_recv,
    second_send,
    near_x_recv,
    second_recv,
    home_send,
    x_send,
    x_recv,
    extra_sem,
    word_send,
    word_recv,
    credit,
):
    seq, blk, heads_dev, groups_kv, heads_per_group, pieces, slots, parts = dims
    g = lax.axis_index("seq")
    b = lax.axis_index("blk")
    part = lax.axis_index("groups")
    tp = lax.axis_index("tp")
    chunks = len(pieces)
    columns_dev = heads_dev * HEAD_WIDTH
    window = (blk + 1) * BLOCK
    group_len = blk * BLOCK
    scale = math.log2(math.e) / math.sqrt(HEAD_WIDTH)

    left = g < 2
    inner = (g == 1) | (g == 2)
    outer = jnp.logical_not(inner)
    far_inner = jnp.where(left, 2, 1)
    far_outer = jnp.where(left, 3, 0)
    near_inner = jnp.where(left, 1, 2)
    near_outer = jnp.where(left, 0, 3)
    peer = 1 - b

    def kv_columns(owner, h):
        start = owner * heads_dev // heads_per_group + h
        return pl.ds(pl.multiple_of(start * HEAD_WIDTH, HEAD_WIDTH), HEAD_WIDTH)

    def q_columns(owner, c):
        start, heads = pieces[c]
        return pl.ds(
            pl.multiple_of(owner * columns_dev + start * HEAD_WIDTH, HEAD_WIDTH),
            heads * HEAD_WIDTH,
        )

    def unit(ref, c, *index):
        return ref.at[(c,) + index + (slice(None), slice(0, pieces[c][1] * HEAD_WIDTH))]

    def chosen(c, index):
        return block_out[index, :, : pieces[c][1] * HEAD_WIDTH]

    def remote(src, dst, send, recv, **where):
        return pltpu.make_async_remote_copy(
            src_ref=src,
            dst_ref=dst,
            send_sem=send,
            recv_sem=recv,
            device_id=where,
            device_id_type=MESH,
        )

    barrier = pltpu.get_barrier_semaphore()
    everyone = [
        {"blk": peer},
        {"groups": lax.rem(part + 1, parts)},
        {"seq": lax.rem(g + 2, seq)},
        {"seq": jnp.where(inner, near_outer, near_inner)},
        {"seq": jnp.where(inner, near_outer, near_inner), "blk": peer},
    ]
    across = [{"seq": far_inner}, {"seq": far_inner, "blk": peer}]

    def greet(devices):
        for device in devices:
            pl.semaphore_signal(barrier, inc=1, device_id=device, device_id_type=MESH)

    greet(everyone)

    @pl.when(inner)
    def _():
        greet(across)

    tables = [
        pltpu.make_async_copy(lengths_hbm, lengths_ref, table_sem.at[0]),
        pltpu.make_async_copy(plan_hbm, plan_ref, table_sem.at[1]),
    ]
    for copy in tables:
        copy.start()
    pairs = ((k_ref, k_near), (v_ref, v_near))
    own_kv = [
        pltpu.make_async_copy(
            src.at[:, kv_columns(b, h)], dst.at[h, blk + b], local_sem.at[2 * h + i]
        )
        for h in range(groups_kv)
        for i, (src, dst) in enumerate(pairs)
    ]
    own_q = [
        pltpu.make_async_copy(
            q_ref.at[:, q_columns(b, c)], unit(q_group, c, b), local_sem.at[2 * groups_kv + c]
        )
        for c in range(chunks)
    ]
    for copy in own_kv + own_q:
        copy.start()

    def kv_copy(h, i):
        src, dst = pairs[i]
        return remote(
            src.at[:, kv_columns(peer, h)],
            dst.at[h, blk + b],
            kv_send.at[h, i],
            kv_recv.at[h, i],
            blk=peer,
        )

    def near_copy(h, i, e):
        src, dst = pairs[i]
        if e == 0:
            source, origin, to = src.at[:, kv_columns(b, h)], b, b
        elif h < DIRECT_HEADS:
            source, origin, to = src.at[:, kv_columns(peer, h)], b, peer
        else:
            source, origin, to = dst.at[h, blk + peer], peer, b
        return remote(
            source,
            dst.at[h, origin],
            near_send.at[h, i, e],
            near_recv.at[h, i, e],
            seq=lax.rem(g + 1, seq),
            blk=to,
        )

    def q_copy(c):
        return remote(
            q_ref.at[:, q_columns(peer, c)],
            unit(q_group, c, b),
            q_send.at[c],
            q_recv.at[c],
            blk=peer,
        )

    @pl.when(g == 0)
    def _():
        for h in range(groups_kv):
            for j in range(blk):
                k_near[h, j] = jnp.zeros(k_near.shape[2:], k_near.dtype)
                v_near[h, j] = jnp.zeros(v_near.shape[2:], v_near.dtype)

    @pl.when(inner)
    def _():
        pl.semaphore_wait(barrier, len(everyone) + len(across))

    @pl.when(outer)
    def _():
        pl.semaphore_wait(barrier, len(everyone))


    def word_copy():
        return remote(word, word_in, word_send, word_recv, groups=lax.rem(part + 1, parts))

    def send_kv(h):
        @pl.when(g < seq - 1)
        def _():
            for e in range(2 if h < DIRECT_HEADS else 1):
                for i in range(2):
                    near_copy(h, i, e).start()

        for i in range(2):
            kv_copy(h, i).start()

    def forward_kv(h):
        for i in range(2):
            kv_copy(h, i).wait_recv()

        if h >= DIRECT_HEADS:

            @pl.when(g < seq - 1)
            def _():
                for i in range(2):
                    near_copy(h, i, 1).start()

    send_kv(0)
    for c in range(QUERY_FIRST):
        q_copy(c).start()

    for copy in tables:
        copy.wait()

    def has(group, owner):
        return (plan_ref[0, group] == owner) | (plan_ref[1, group] == owner)

    def pick(owner):
        return jnp.where(
            plan_ref[0, g] == owner,
            jnp.int32(0),
            jnp.where(plan_ref[1, g] == owner, jnp.int32(1), jnp.int32(blk)),
        )

    full_right = has(0, 2) & has(0, 3) & has(1, 2) & has(1, 3)
    full_left = has(3, 1) & has(3, 0) & has(2, 1) & has(2, 0)
    spilled = jnp.where(full_right | full_left, jnp.int32(1), jnp.int32(0))
    word[...] = jnp.full(word.shape, spilled, jnp.int32)

    for j in range(blk):
        first_row = g * group_len + j * BLOCK
        row_pos = first_row + lax.broadcasted_iota(jnp.int32, (BLOCK, 1), 0)
        end = jnp.int32(0)
        start = jnp.zeros((BLOCK, 1), jnp.int32)
        for n in range(lengths_ref.shape[0]):
            end = end + lengths_ref[n]
            start = jnp.where(row_pos >= end, end, start)
        key_pos = first_row - group_len + lax.broadcasted_iota(jnp.int32, (BLOCK, window), 1)
        allowed = (key_pos >= start) & (key_pos <= row_pos)
        bias[j] = jnp.where(allowed, 0.0, masked_score)
    block_out[blk] = jnp.zeros(block_out.shape[1:], block_out.dtype)

    forward_kv(0)
    for c in range(QUERY_FIRST, QUERY_SECOND):
        q_copy(c).start()
    if KV_EARLY:
        send_kv(1)
    word_copy().start()
    for copy in own_kv:
        copy.wait()

    sender = jnp.where(inner, 1, 0)

    def first_copy(c, which):
        return remote(
            unit(first, c),
            unit(land_first, c, which),
            first_send.at[c],
            first_recv.at[c, which],
            seq=far_inner,
        )

    def to_near(c):
        return remote(
            unit(second, c), unit(land_near, c), second_send.at[c], near_x_recv.at[c], seq=near_inner
        )

    def to_far(c):
        return remote(
            unit(second, c), unit(land_second, c), second_send.at[c], second_recv.at[c], seq=far_inner
        )

    def out_rows(group, half, c):
        slot = lax.rem(group, slots)
        return out_ref.at[
            pl.ds(pl.multiple_of(slot * BLOCK, BLOCK), BLOCK), q_columns(half, c)
        ]

    def home_copy(c, k):
        source = unit(homeward, c) if k == 0 else unit(relay, c, k - 1)
        group = (near_inner, far_inner, far_outer)[k]
        return remote(
            source,
            out_rows(group, b, c),
            home_send.at[c, k],
            x_recv.at[c, lax.rem(group, slots), b],
            seq=near_outer,
            blk=group // slots,
        )

    def extra_copy(c):
        return pltpu.make_async_copy(unit(spare, c), unit(extra_ref, c), extra_sem.at[c])

    def place(c, group, waiting):
        source = unit(mine, c, group)
        holder = group // slots
        target = out_rows(group, b, c)

        @pl.when(holder == b)
        def _():
            copy = pltpu.make_async_copy(source, target, x_send.at[c, group])
            if waiting:
                copy.wait()
            else:
                copy.start()

        @pl.when(holder != b)
        def _():
            copy = remote(
                source,
                target,
                x_send.at[c, group],
                x_recv.at[c, lax.rem(group, slots), b],
                blk=holder,
            )
            if waiting:
                copy.wait_send()
            else:
                copy.start()

    to_inner, to_outer = pick(far_inner), pick(far_outer)
    both = (to_inner < blk) & (to_outer < blk)
    first_index = jnp.where(to_inner < blk, to_inner, to_outer)
    second_index = jnp.where(both, to_outer, jnp.int32(blk))
    near_index = jnp.where(both, to_outer, pick(near_inner))
    home_index, own_index = pick(near_outer), pick(g)

    near_both = has(near_outer, far_inner) & has(near_outer, far_outer)
    near_here = has(near_outer, g)
    a_here, a_on = has(far_outer, g), has(far_outer, near_outer)
    b_here, b_on = has(far_inner, g), has(far_inner, near_outer)

    def attend(c):
        own_q[c].wait()
        q_copy(c).wait_recv()
        for m in range(max(QUERY_SECOND, c and c + QUERY_LEAD), min(c + QUERY_LEAD + 1, chunks)):
            q_copy(m).start()
        begin, chunk_heads = pieces[c]
        kv_head = begin // heads_per_group
        if begin % heads_per_group == 0:

            @pl.when(g > 0)
            def _():
                for e in range(2):
                    for i in range(2):
                        near_copy(kv_head, i, e).wait_recv()

        for j in range(blk):
            query = unit(q_group, c, j)[...]
            rows = jnp.concatenate(
                [query[:, h * HEAD_WIDTH : (h + 1) * HEAD_WIDTH] for h in range(chunk_heads)], axis=0
            )
            keys = k_near[kv_head, j : j + blk + 1].reshape(window, HEAD_WIDTH)
            values = v_near[kv_head, j : j + blk + 1].reshape(window, HEAD_WIDTH)
            scores = lax.dot_general(
                rows, keys, (((1,), (1,)), ((), ())), preferred_element_type=jnp.float32
            )
            scores = scores.reshape(chunk_heads, BLOCK, window) * scale + bias[j][None]
            top = jnp.max(scores, axis=2, keepdims=True)
            weights = jnp.exp2(scores - top)
            total = jnp.sum(weights, axis=2, keepdims=True)
            mixed = jnp.dot(
                weights.astype(jnp.bfloat16).reshape(chunk_heads * BLOCK, window),
                values,
                preferred_element_type=jnp.float32,
            ).reshape(chunk_heads, BLOCK, HEAD_WIDTH)
            result = (mixed / total).astype(jnp.bfloat16)
            for h in range(chunk_heads):
                block_out[j, :, h * HEAD_WIDTH : (h + 1) * HEAD_WIDTH] = result[h]

    def dispatch(c):
        unit(first, c)[...] = chosen(c, first_index)

        @pl.when(outer)
        def _():
            unit(second, c)[...] = chosen(c, near_index)
            to_near(c).start()
            for core, lag in enumerate(LAGS):
                if c >= lag:

                    @pl.when(tp == core)
                    def _():
                        pl.semaphore_wait(credit, 1)


        first_copy(c, sender).start()

        @pl.when(inner)
        def _():
            unit(homeward, c)[...] = chosen(c, home_index)
            home_copy(c, 0).start()
            unit(spare, c)[...] = chosen(c, second_index)
            extra_copy(c).start()

        unit(mine, c, g)[...] = chosen(c, own_index)
        place(c, g, False)

    def join(c):
        to_near(c).wait_recv()
        arrived = unit(land_near, c)[...]
        unit(second, c)[...] = jnp.where(near_both, arrived, unit(spare, c)[...])
        to_far(c).start()
        unit(mine, c, near_outer)[...] = jnp.where(near_here, arrived, jnp.zeros_like(arrived))
        place(c, near_outer, False)

    def spread(c, lag):
        first_copy(c, 0).wait_recv()
        first_copy(c, 1).wait_recv()
        to_far(c).wait_recv()
        if c + lag < chunks:
            pl.semaphore_signal(
                credit, inc=1, device_id={"seq": far_outer}, device_id_type=MESH
            )
        from_outer = unit(land_first, c, 0)[...]
        from_inner = unit(land_first, c, 1)[...]
        last = unit(land_second, c)[...]
        nothing = jnp.zeros_like(last)
        unit(relay, c, 1)[...] = jnp.where(a_on, jnp.where(a_here, last, from_outer), nothing)
        home_copy(c, 2).start()
        rest = jnp.where(a_here & a_on, nothing, last)
        unit(relay, c, 0)[...] = jnp.where(b_on, jnp.where(b_here, rest, from_inner), nothing)
        home_copy(c, 1).start()
        unit(mine, c, far_outer)[...] = jnp.where(a_here, from_outer, nothing)
        place(c, far_outer, False)
        unit(mine, c, far_inner)[...] = jnp.where(b_here, from_inner, nothing)
        place(c, far_inner, False)

    def landed(c, s, half):
        remote(
            unit(mine, c, 0),
            out_rows(b * slots + s, half, c),
            x_send.at[c, 0],
            x_recv.at[c, s, half],
            blk=peer,
        ).wait_recv()

    for t in range(chunks + max(JOIN_LAG, *LAGS)):
        if t < chunks:
            attend(t)
            dispatch(t)
            if KV_EARLY and t == KV_EARLY - 1:
                forward_kv(1)
            for h in range(2 if KV_EARLY else 1, groups_kv):
                start = [begin for begin, _ in pieces].index(h * heads_per_group)
                if t == start - KV_LEAD:
                    send_kv(h)
                if t == start - KV_LEAD + 1:
                    forward_kv(h)

        @pl.when(inner)
        def _():
            if 0 <= t - JOIN_LAG < chunks:
                join(t - JOIN_LAG)

        for core, lag in enumerate(LAGS):
            if 0 <= t - lag < chunks:

                @pl.when(inner & (tp == core))
                def _():
                    spread(t - lag, lag)

    word_copy().wait()
    flag_ref[0, 0] = spilled * (1 + part) + jnp.max(word_in[...]) * (2 - part)

    for h in range(groups_kv):
        for i in range(2):
            kv_copy(h, i).wait_send()

    @pl.when(g < seq - 1)
    def _():
        for h in range(groups_kv):
            for e in range(2):
                for i in range(2):
                    near_copy(h, i, e).wait_send()

    for c in range(chunks):
        q_copy(c).wait_send()
        first_copy(c, sender).wait_send()

        @pl.when(outer)
        def _():
            to_near(c).wait_send()

        @pl.when(inner)
        def _():
            to_far(c).wait_send()
            extra_copy(c).wait()
            for k in range(3):
                home_copy(c, k).wait_send()
            for group in (near_outer, far_inner, far_outer):
                place(c, group, True)

        place(c, g, True)
        for s in range(slots):
            landed(c, s, peer)

            @pl.when(outer & (b * slots + s != g))
            def _():
                landed(c, s, b)


def spill_kernel(dims, active, extra_ref, got_ref, via, send, recv, via_recv):
    seq, blk, columns_dev, pieces, slots, parts = dims
    chunks = len(pieces)
    part = lax.axis_index("groups")
    g = lax.axis_index("seq")
    b = lax.axis_index("blk")
    inner = (g == 1) | (g == 2)
    mate = lax.rem(g + 2, seq)
    other = lax.rem(part + 1, parts)
    direct = chunks if active is None else chunks - DETOUR
    barrier = pltpu.get_barrier_semaphore()
    greeted = [{"seq": mate, "blk": e} for e in range(blk)]
    greeted += [{"groups": other, "seq": mate, "blk": e} for e in range(blk)]
    greeted += [{"groups": other}]
    for device in greeted:
        pl.semaphore_signal(barrier, inc=1, device_id=device, device_id_type=MESH)
    pl.semaphore_wait(barrier, len(greeted))

    def spill(c, half, holder, source, owner_part):
        start, width = pieces[c][0] * HEAD_WIDTH, pieces[c][1] * HEAD_WIDTH
        return pltpu.make_async_remote_copy(
            src_ref=source.at[c, :, :width],
            dst_ref=got_ref.at[
                :, pl.ds(pl.multiple_of(half * columns_dev + start, HEAD_WIDTH), width)
            ],
            send_sem=send.at[c],
            recv_sem=recv.at[c, half],
            device_id={"groups": owner_part, "seq": mate, "blk": holder},
            device_id_type=MESH,
        )

    def to_side(c):
        return pltpu.make_async_remote_copy(
            src_ref=extra_ref.at[c],
            dst_ref=via.at[c],
            send_sem=send.at[c],
            recv_sem=via_recv.at[c],
            device_id={"groups": other},
            device_id_type=MESH,
        )

    mine = part < parts if active is None else part == active

    @pl.when(mine & inner)
    def _():
        for c in range(direct, chunks):
            to_side(c).start()
        for c in range(direct):
            spill(c, b, g // slots, extra_ref, part).start()
        for c in range(direct, chunks):
            to_side(c).wait_send()
        for c in range(direct):
            spill(c, b, g // slots, extra_ref, part).wait_send()

    @pl.when(jnp.logical_not(mine) & inner)
    def _():
        for c in range(direct, chunks):
            to_side(c).wait_recv()
            spill(c, b, g // slots, via, other).start()
        for c in range(direct, chunks):
            spill(c, b, g // slots, via, other).wait_send()

    @pl.when(mine & jnp.logical_not(inner) & (b == mate // slots))
    def _():
        for c in range(chunks):
            for half in range(blk):
                spill(c, half, b, extra_ref, part).wait_recv()


def finish_spilled(slots, plan_ref, src_ref, got_ref, dst_ref, sem):
    owner = lax.axis_index("seq")
    b = lax.axis_index("blk")

    def has(group, wanted):
        return (plan_ref[0, group] == wanted) | (plan_ref[1, group] == wanted)

    full_right = has(0, 2) & has(0, 3) & has(1, 2) & has(1, 3)
    full_left = has(3, 1) & has(3, 0) & has(2, 1) & has(2, 0)
    for s in range(slots):
        group = b * slots + s
        rows = pl.ds(s * BLOCK, BLOCK)
        spilled = ((group == 1) & (owner == 3) & full_right) | (
            (group == 2) & (owner == 0) & full_left
        )

        @pl.when(spilled)
        def _():
            copy = pltpu.make_async_copy(got_ref, dst_ref.at[rows], sem.at[s])
            copy.start()
            copy.wait()

        @pl.when(jnp.logical_not(spilled))
        def _():
            copy = pltpu.make_async_copy(src_ref.at[rows], dst_ref.at[rows], sem.at[s])
            copy.start()
            copy.wait()


def quad(queries, rotated_keys, head_value_rows, doc_lengths, owner_plan):
    blk = lax.axis_size("blk")
    seq = lax.axis_size("seq")
    parts = lax.axis_size("groups")
    heads_dev = queries.shape[1] // HEAD_WIDTH // blk
    heads_per_group = QUERY_HEADS // KEY_HEADS
    groups_kv = heads_dev // heads_per_group
    sizes = []
    for h in range(groups_kv):
        row = [CHUNK_HEADS] * (heads_per_group // CHUNK_HEADS)
        if h == 0:
            row = list(HEAD_SPLIT) + row[1:]
        if h == groups_kv - 1:
            row = row[:-1] + list(TAIL_SPLIT)
        sizes += row
    pieces = [(sum(sizes[:c]), sizes[c]) for c in range(len(sizes))]
    chunks = len(pieces)
    slots = seq // blk
    width = max(sizes) * HEAD_WIDTH
    dims = (seq, blk, heads_dev, groups_kv, heads_per_group, pieces, slots, parts)
    bf16 = jnp.bfloat16
    dma = pltpu.SemaphoreType.DMA
    hbm = pl.BlockSpec(memory_space=pltpu.HBM)
    plan = owner_plan.T
    out_shape = jax.ShapeDtypeStruct((slots * BLOCK, queries.shape[1]), bf16)

    def unit(*lead):
        return pltpu.VMEM(lead + (BLOCK, width), bf16)

    placed, extra, flag = pl.pallas_call(
        functools.partial(quad_kernel, dims),
        out_shape=(
            out_shape,
            jax.ShapeDtypeStruct((chunks, BLOCK, width), bf16),
            jax.ShapeDtypeStruct((1, 1), jnp.int32),
        ),
        in_specs=[hbm] * 5,
        out_specs=(
            pl.BlockSpec(memory_space=pl.ANY),
            pl.BlockSpec(memory_space=pl.ANY),
            pl.BlockSpec(memory_space=pltpu.SMEM),
        ),
        scratch_shapes=[
            unit(chunks, blk),
            pltpu.VMEM((groups_kv, 2 * blk, BLOCK, HEAD_WIDTH), bf16),
            pltpu.VMEM((groups_kv, 2 * blk, BLOCK, HEAD_WIDTH), bf16),
            pltpu.VMEM((blk, BLOCK, (blk + 1) * BLOCK), jnp.float32),
            unit(blk + 1),
            unit(chunks),
            unit(chunks),
            unit(chunks),
            unit(chunks, 2),
            unit(chunks),
            unit(chunks, 2),
            unit(chunks),
            unit(chunks),
            unit(chunks, seq),
            pltpu.VMEM((8, 128), jnp.int32),
            pltpu.VMEM((8, 128), jnp.int32),
            pltpu.SMEM(doc_lengths.shape, jnp.int32),
            pltpu.SMEM(plan.shape, jnp.int32),
            dma((2,)),
            dma((2 * groups_kv + chunks,)),
            dma((chunks,)),
            dma((chunks,)),
            dma((groups_kv, 2)),
            dma((groups_kv, 2)),
            dma((groups_kv, 2, 2)),
            dma((groups_kv, 2, 2)),
            dma((chunks,)),
            dma((chunks, 2)),
            dma((chunks,)),
            dma((chunks,)),
            dma((chunks,)),
            dma((chunks, 3)),
            dma((chunks, seq)),
            dma((chunks, slots, blk)),
            dma((chunks,)),
            dma,
            dma,
            pltpu.SemaphoreType.REGULAR,
        ],
        compiler_params=pltpu.CompilerParams(
            collective_id=0, has_side_effects=True, vmem_limit_bytes=VMEM_MAIN
        ),
    )(doc_lengths, plan, queries, rotated_keys, head_value_rows)

    def plain(placed, extra):
        return placed

    def spilled(active, collective_id, placed, extra):
        got = pl.pallas_call(
            functools.partial(
                spill_kernel, (seq, blk, heads_dev * HEAD_WIDTH, pieces, slots, parts), active
            ),
            out_shape=jax.ShapeDtypeStruct((BLOCK, queries.shape[1]), bf16),
            in_specs=[pl.BlockSpec(memory_space=pl.ANY)],
            out_specs=pl.BlockSpec(memory_space=pl.ANY),
            scratch_shapes=[unit(chunks), dma((chunks,)), dma((chunks, blk)), dma((chunks,))],
            compiler_params=pltpu.CompilerParams(
                collective_id=collective_id, has_side_effects=True, vmem_limit_bytes=VMEM_REST
            ),
        )(extra)
        return pl.pallas_call(
            functools.partial(finish_spilled, slots),
            out_shape=out_shape,
            in_specs=[pl.BlockSpec(memory_space=pltpu.SMEM)]
            + [pl.BlockSpec(memory_space=pl.ANY)] * 2,
            out_specs=hbm,
            scratch_shapes=[dma((slots,))],
            compiler_params=pltpu.CompilerParams(vmem_limit_bytes=VMEM_REST),
        )(plan, placed, got)

    branches = [plain] + [
        functools.partial(spilled, active, 1 + n) for n, active in enumerate((0, 1, None))
    ]
    return lax.switch(flag[0, 0], branches, placed, extra)


def per_device(queries, rotated_keys, head_value_rows, doc_lengths, owner_plan):
    blk = lax.axis_size("blk")
    seq = lax.axis_size("seq")
    heads_dev = queries.shape[1] // HEAD_WIDTH // blk
    heads_per_group = QUERY_HEADS // KEY_HEADS
    groups_kv = max(1, heads_dev // heads_per_group)
    chunk_heads = min(CHUNK_HEADS, heads_dev, heads_per_group)
    chunks = heads_dev // chunk_heads
    slots = seq // blk
    if (seq, blk, lax.axis_size("groups")) == (4, 2, 2) and heads_dev % heads_per_group == 0:
        return quad(queries, rotated_keys, head_value_rows, doc_lengths, owner_plan)
    width = chunk_heads * HEAD_WIDTH
    dims = (seq, blk, heads_dev, groups_kv, heads_per_group, chunk_heads, slots)
    bf16 = jnp.bfloat16
    dma = pltpu.SemaphoreType.DMA
    placed = pl.pallas_call(
        functools.partial(kernel, dims),
        out_shape=jax.ShapeDtypeStruct((slots * BLOCK, queries.shape[1]), bf16),
        in_specs=[pl.BlockSpec(memory_space=pltpu.SMEM)] * 2
        + [pl.BlockSpec(memory_space=pl.ANY)] * 3,
        out_specs=pl.BlockSpec(memory_space=pl.ANY),
        scratch_shapes=[
            pltpu.VMEM((chunks, blk, BLOCK, width), bf16),
            pltpu.VMEM((groups_kv, 2 * blk, BLOCK, HEAD_WIDTH), bf16),
            pltpu.VMEM((groups_kv, 2 * blk, BLOCK, HEAD_WIDTH), bf16),
            pltpu.VMEM((blk, BLOCK, (blk + 1) * BLOCK), jnp.float32),
            pltpu.VMEM((blk + 1, BLOCK, width), bf16),
            pltpu.VMEM((chunks, seq, BLOCK, width), bf16),
            pltpu.VMEM((chunks, seq - 1, BLOCK, width), bf16),
            dma((2 * groups_kv + chunks,)),
            dma((chunks, blk - 1)),
            dma((chunks, blk - 1)),
            dma((groups_kv, 2, blk - 1)),
            dma((groups_kv, 2, blk - 1)),
            dma((groups_kv, 2, blk)),
            dma((groups_kv, 2, blk)),
            dma((chunks, seq - 1)),
            dma((chunks, seq - 1)),
            dma((chunks, seq)),
            dma((chunks, slots, blk)),
        ],
        compiler_params=pltpu.CompilerParams(collective_id=0, has_side_effects=True),
    )(doc_lengths, owner_plan.T, queries, rotated_keys, head_value_rows)
    pieces = PIECES
    return pl.pallas_call(
        functools.partial(settle, pieces),
        out_shape=jax.ShapeDtypeStruct(placed.shape, bf16),
        in_specs=[pl.BlockSpec(memory_space=pl.ANY)],
        out_specs=pl.BlockSpec(memory_space=pl.ANY),
        scratch_shapes=[
            pltpu.VMEM((pieces, placed.shape[0] // pieces, placed.shape[1]), bf16),
            dma((pieces,)),
            dma((pieces,)),
        ],
    )(placed)


def solution(mesh):
    in_specs = (
        P(("groups", "seq", "blk"), "tp"),
        P(("groups", "seq", "blk"), "tp"),
        P(("groups", "seq", "blk"), "tp"),
        P("groups"),
        P("groups", None),
    )
    out_specs = P(("groups", "seq", "blk"), "tp")
    return jax.shard_map(
        per_device, mesh=mesh, in_specs=in_specs, out_specs=out_specs, check_vma=False
    )
```
